256 devices in a mesh: src: 2 (over y_lo), tx: 8 (over y_hi, x), ty: 16 (over z, core).
Axes of the slice: x: 4, y: 4 (y_hi: 2, y_lo: 2; y = y_hi * 2 + y_lo), z: 8, core: 2. Of those that a mesh axis runs over, the one named last changes fastest.
Arguments:
- orders: float32 [8, 2, 512, 512], P('src', None, 'tx', 'ty'), may hold values from -0.00390625 to 0.00390625
- offsets: int32 [8, 2], P('src'), may hold values from -8 to 7
- material: int32 [6, 2048, 2048], P(None, 'tx', 'ty'), may hold values from 0 to 3
- e_field: float32 [3, 6, 2048, 2048], P(None, None, 'tx', 'ty'), may hold values from -6 to 6
- h_field: float32 [3, 6, 2048, 2048], P(None, None, 'tx', 'ty'), may hold values from -6 to 6
Outputs:
- e_out: float32 [3, 6, 2048, 2048], P(None, None, 'tx', 'ty')
- h_out: float32 [3, 6, 2048, 2048], P(None, None, 'tx', 'ty')
The draws below stay inside these ranges and needn't reach their ends.
All inputs are finite; a program needn't handle non-finite values.
Results may differ from the reference program's by a relative error of at most 0.0003.
Values sent between devices are 32-bit elements; how exact they have to be, the bound alone decides.
A program may use at most 128 MiB of HBM per device.

```python
import math
import jax
import jax.numpy as jnp
from jax import lax

NZ = 6
MX = 512
MY = 512
STEPS = 4
ZINJ = 1
NX = 2048
NY = 2048
P_ALL = 8


def place_ends(entries, own_key, least, high):
    shape = entries.shape
    place = [jax.random.randint(jax.random.fold_in(own_key, axis), (), 0, shape[axis]) for axis in range(len(shape))]
    entries = entries.at[tuple(place)].set(least)
    longest = shape.index(max(shape))
    place[longest] = (place[longest] + 1) % shape[longest]
    return entries.at[tuple(place)].set(high)


def block_levels(own_key, shape, split, least, top_value):
    def one(position, shards_of):
        heights = jax.random.uniform(jax.random.fold_in(jax.random.fold_in(own_key, 6), position), (shards_of,), jnp.float32, least / len(split), top_value / len(split))
        return jnp.repeat(jnp.exp(heights), shape[position] // shards_of).reshape((-1,) + (1,) * (len(shape) - position - 1))

    factor_of = one(*split[0])
    for cut in split[1:]:
        factor_of = factor_of * one(*cut)
    return factor_of


def centred(stream_key, extent, scale, bound, cuts=(), kind=jnp.bfloat16):
    factor_of = block_levels(stream_key, extent, cuts, -0.22, 0.18) if cuts else 1.0
    result = jax.random.normal(stream_key, extent, jnp.float32) * scale * factor_of
    return jnp.minimum(jnp.maximum(result, -bound), bound).astype(kind)


def setup_inputs(seed: int = 0) -> dict:
    arg_keys = jax.random.split(jax.random.key(seed), 6)
    orders = centred(arg_keys[0], (P_ALL, 2, MX, MY), (MX * MY * P_ALL) ** -0.5, 0.00390625, ((0, 2), (2, 8), (3, 16)), jnp.float32)
    offsets = place_ends(jax.random.randint(arg_keys[1], (P_ALL, 2), -8, 8), jax.random.fold_in(arg_keys[1], 1), -8, 7).astype(jnp.int32)
    material = place_ends(jax.random.randint(arg_keys[2], (NZ, NX, NY), 0, 4), jax.random.fold_in(arg_keys[2], 1), 0, 3).astype(jnp.int32)
    e_field = centred(arg_keys[3], (3, NZ, NX, NY), 1.0, 6.0, ((2, 8), (3, 16)), jnp.float32)
    h_field = centred(arg_keys[4], (3, NZ, NX, NY), 1.0, 6.0, ((2, 8), (3, 16)), jnp.float32)
    return dict(orders=orders, offsets=offsets, material=material, e_field=e_field, h_field=h_field)


COURANT = 0.5
OMEGA = 0.7
PERMITTIVITY = (1.0, 2.6, 11.9, 2.1)
HIGH = lax.Precision.HIGHEST


def phase_tables(freqs, positions, length):
    product = jnp.mod(freqs[:, :, None] * positions[None, None, :], length)
    angle = product.astype(jnp.float32) * (2.0 * math.pi / length)
    return jnp.cos(angle), jnp.sin(angle)


def cell_coefficient(material):
    total = jnp.zeros(material.shape, jnp.float32)
    for number in range(len(PERMITTIVITY)):
        total = total + jnp.where(material == number, COURANT / PERMITTIVITY[number], 0.0)
    return total


def ahead(field, axis):
    if axis == 0:
        zero = jnp.zeros((1,) + field.shape[1:], jnp.float32)
        return jnp.concatenate([field[1:], zero], 0) - field
    return jnp.roll(field, -1, axis) - field


def behind(field, axis):
    if axis == 0:
        zero = jnp.zeros((1,) + field.shape[1:], jnp.float32)
        return field - jnp.concatenate([zero, field[:-1]], 0)
    return field - jnp.roll(field, 1, axis)


def reference(orders, offsets, material, e_field, h_field):
    x_pos = jnp.arange(NX, dtype=jnp.int32)
    y_pos = jnp.arange(NY, dtype=jnp.int32)
    kx_base = jnp.arange(MX, dtype=jnp.int32) - MX // 2
    ky_base = jnp.arange(MY, dtype=jnp.int32) - MY // 2

    def one_point(total, item):
        amp, shift = item
        cos_y, sin_y = phase_tables((ky_base + shift[1])[None, :], y_pos, NY)
        cos_x, sin_x = phase_tables((kx_base + shift[0])[None, :], x_pos, NX)
        cos_y, sin_y = cos_y[0], sin_y[0]
        cos_x, sin_x = cos_x[0].T, sin_x[0].T
        inner_re = jnp.dot(amp[0], cos_y, precision=HIGH) - jnp.dot(amp[1], sin_y, precision=HIGH)
        inner_im = jnp.dot(amp[0], sin_y, precision=HIGH) + jnp.dot(amp[1], cos_y, precision=HIGH)
        plane_re = jnp.dot(cos_x, inner_re, precision=HIGH) - jnp.dot(sin_x, inner_im, precision=HIGH)
        plane_im = jnp.dot(cos_x, inner_im, precision=HIGH) + jnp.dot(sin_x, inner_re, precision=HIGH)
        return total + jnp.stack([plane_re, plane_im]), None

    plane, _ = lax.scan(one_point, jnp.zeros((2, NX, NY), jnp.float32), (orders, offsets))
    coefficient = cell_coefficient(material)
    e_x, e_y, e_z = e_field[0], e_field[1], e_field[2]
    h_x, h_y, h_z = h_field[0], h_field[1], h_field[2]
    for step in range(STEPS):
        h_x = h_x - COURANT * (ahead(e_z, 2) - ahead(e_y, 0))
        h_y = h_y - COURANT * (ahead(e_x, 0) - ahead(e_z, 1))
        h_z = h_z - COURANT * (ahead(e_y, 1) - ahead(e_x, 2))
        e_x = e_x + coefficient * (behind(h_z, 2) - behind(h_y, 0))
        e_y = e_y + coefficient * (behind(h_x, 0) - behind(h_z, 1))
        e_z = e_z + coefficient * (behind(h_y, 1) - behind(h_x, 2))
        cosine = math.cos(OMEGA * (step + 1))
        sine = math.sin(OMEGA * (step + 1))
        e_x = e_x.at[ZINJ].add(COURANT * (cosine * plane[0] - sine * plane[1]))
        e_y = e_y.at[ZINJ].add(COURANT * (sine * plane[0] + cosine * plane[1]))
    return jnp.stack([e_x, e_y, e_z]), jnp.stack([h_x, h_y, h_z])
```

```python
import math

import jax
import jax.numpy as jnp
from jax import lax
from jax.sharding import PartitionSpec as P

STEPS = 4
ZINJ = 1


COURANT = 0.5
OMEGA = 0.7
PERMITTIVITY = (1.0, 2.6, 11.9, 2.1)
PREC = lax.Precision.HIGH
SPLIT = 32


def passed_along(block, axis, distance):
    devices = range(lax.axis_size(axis))
    route = [((i - distance) % len(devices), i) for i in devices]
    return lax.ppermute(block, axis, route)


def phase_tables(freqs, positions, length):
    product = jnp.mod(freqs[:, None] * positions[None, :], length)
    angle = product.astype(jnp.float32) * (2.0 * math.pi / length)
    return (jnp.cos(angle), jnp.sin(angle))


def base_tables(orders_n, positions, length):
    hi = jnp.arange(orders_n // SPLIT, dtype=jnp.int32) * SPLIT
    lo = jnp.arange(SPLIT, dtype=jnp.int32) - orders_n // 2
    c1, s1 = phase_tables(hi, positions, length)
    c2, s2 = phase_tables(lo, positions, length)
    cos_t = c1[:, None, :] * c2[None, :, :] - s1[:, None, :] * s2[None, :, :]
    sin_t = s1[:, None, :] * c2[None, :, :] + c1[:, None, :] * s2[None, :, :]
    return cos_t.reshape(orders_n, -1), sin_t.reshape(orders_n, -1)


def cell_coefficient(material):
    total = jnp.zeros(material.shape, jnp.float32)
    for number in range(len(PERMITTIVITY)):
        total = total + jnp.where(material == number, COURANT / PERMITTIVITY[number], 0.0)
    return total


def fwd(field, axis):
    if axis == 0:
        zero = jnp.zeros((1,) + field.shape[1:], jnp.float32)
        return jnp.concatenate([field[1:], zero], 0) - field
    return jnp.roll(field, -1, axis) - field


def bwd(field, axis):
    if axis == 0:
        zero = jnp.zeros((1,) + field.shape[1:], jnp.float32)
        return field - jnp.concatenate([zero, field[:-1]], 0)
    return field - jnp.roll(field, 1, axis)


def injection_plane(orders, offsets, cells_x, cells_y):
    points, _, rows_kx, cols_ky = orders.shape
    n_tx = lax.axis_size("tx")
    n_ty = lax.axis_size("ty")
    full_x = cells_x * n_tx
    full_y = cells_y * n_ty
    mx = rows_kx * n_tx
    my = cols_ky * n_ty
    amp = lax.all_gather(orders, "ty", axis=3, tiled=True)
    a_re = amp[:, 0]
    a_im = amp[:, 1]
    y_pos = lax.axis_index("ty") * cells_y + jnp.arange(cells_y, dtype=jnp.int32)
    by_c, by_s = base_tables(my, y_pos, full_y)
    sy_c, sy_s = phase_tables(offsets[:, 1], y_pos, full_y)
    m_re = jnp.einsum("pkj,jy->pky", a_re, by_c, precision=PREC) - jnp.einsum(
        "pkj,jy->pky", a_im, by_s, precision=PREC
    )
    m_im = jnp.einsum("pkj,jy->pky", a_re, by_s, precision=PREC) + jnp.einsum(
        "pkj,jy->pky", a_im, by_c, precision=PREC
    )
    sy_c = sy_c[:, None, :]
    sy_s = sy_s[:, None, :]
    inner = jnp.stack([m_re * sy_c - m_im * sy_s, m_re * sy_s + m_im * sy_c], 1)
    inner = lax.all_gather(inner, "tx", axis=2, tiled=True)
    i_re = inner[:, 0]
    i_im = inner[:, 1]
    x_pos = lax.axis_index("tx") * cells_x + jnp.arange(cells_x, dtype=jnp.int32)
    bx_c, bx_s = base_tables(mx, x_pos, full_x)
    sx_c, sx_s = phase_tables(offsets[:, 0], x_pos, full_x)
    q_re = jnp.einsum("kx,pky->pxy", bx_c, i_re, precision=PREC) - jnp.einsum(
        "kx,pky->pxy", bx_s, i_im, precision=PREC
    )
    q_im = jnp.einsum("kx,pky->pxy", bx_c, i_im, precision=PREC) + jnp.einsum(
        "kx,pky->pxy", bx_s, i_re, precision=PREC
    )
    sx_c = sx_c[:, :, None]
    sx_s = sx_s[:, :, None]
    plane = jnp.stack(
        [jnp.sum(q_re * sx_c - q_im * sx_s, 0), jnp.sum(q_re * sx_s + q_im * sx_c, 0)]
    )
    return lax.psum(plane, "src")


def with_halo(stack, depth):
    ahead = passed_along(stack[:, :depth], "tx", -1)
    behind = passed_along(stack[:, -depth:], "tx", 1)
    stack = jnp.concatenate([stack, ahead, behind], 1)
    ahead = passed_along(jnp.swapaxes(stack[:, :, :depth], 1, 2), "ty", -1)
    behind = passed_along(jnp.swapaxes(stack[:, :, -depth:], 1, 2), "ty", 1)
    return jnp.concatenate([stack, jnp.swapaxes(ahead, 1, 2), jnp.swapaxes(behind, 1, 2)], 2)


def per_device(orders, offsets, material, e_field, h_field):
    layers, cells_x, cells_y = material.shape
    plane = injection_plane(orders, offsets, cells_x, cells_y)
    coefficient = cell_coefficient(material)
    stack = jnp.concatenate(
        [
            e_field.reshape(3 * layers, cells_x, cells_y),
            h_field.reshape(3 * layers, cells_x, cells_y),
            coefficient,
            plane,
        ],
        0,
    )
    ext = with_halo(stack, STEPS)
    n = 3 * layers
    e_x, e_y, e_z = (ext[i * layers:(i + 1) * layers] for i in range(3))
    h_x, h_y, h_z = (ext[n + i * layers:n + (i + 1) * layers] for i in range(3))
    coefficient = ext[2 * n:2 * n + layers]
    plane_re = ext[2 * n + layers]
    plane_im = ext[2 * n + layers + 1]
    for step in range(STEPS):
        h_x = h_x - COURANT * (fwd(e_z, 2) - fwd(e_y, 0))
        h_y = h_y - COURANT * (fwd(e_x, 0) - fwd(e_z, 1))
        h_z = h_z - COURANT * (fwd(e_y, 1) - fwd(e_x, 2))
        e_x = e_x + coefficient * (bwd(h_z, 2) - bwd(h_y, 0))
        e_y = e_y + coefficient * (bwd(h_x, 0) - bwd(h_z, 1))
        e_z = e_z + coefficient * (bwd(h_y, 1) - bwd(h_x, 2))
        cosine = math.cos(OMEGA * (step + 1))
        sine = math.sin(OMEGA * (step + 1))
        e_x = e_x.at[ZINJ].add(COURANT * (cosine * plane_re - sine * plane_im))
        e_y = e_y.at[ZINJ].add(COURANT * (sine * plane_re + cosine * plane_im))
    crop = lambda f: f[:, :cells_x, :cells_y]
    return (
        jnp.stack([crop(e_x), crop(e_y), crop(e_z)]),
        jnp.stack([crop(h_x), crop(h_y), crop(h_z)]),
    )


def solution(mesh):
    in_specs = (
        P("src", None, "tx", "ty"),
        P("src", None),
        P(None, "tx", "ty"),
        P(None, None, "tx", "ty"),
        P(None, None, "tx", "ty"),
    )
    out_specs = (P(None, None, "tx", "ty"), P(None, None, "tx", "ty"))
    return jax.shard_map(
        per_device, mesh=mesh, in_specs=in_specs, out_specs=out_specs, check_vma=False
    )
```

```python
import math

import jax
import jax.numpy as jnp
from jax import lax
from jax.sharding import PartitionSpec as P

STEPS = 4
ZINJ = 1


COURANT = 0.5
OMEGA = 0.7
PERMITTIVITY = (1.0, 2.6, 11.9, 2.1)
PREC = lax.Precision.HIGH


def passed_along(block, axis, distance):
    devices = range(lax.axis_size(axis))
    route = [((i - distance) % len(devices), i) for i in devices]
    return lax.ppermute(block, axis, route)


def phase_tables(freqs, positions, length):
    product = jnp.mod(freqs[:, None] * positions[None, :], length)
    angle = product.astype(jnp.float32) * (2.0 * math.pi / length)
    return (jnp.cos(angle), jnp.sin(angle))


def cell_coefficient(material):
    total = jnp.zeros(material.shape, jnp.float32)
    for number in range(len(PERMITTIVITY)):
        total = total + jnp.where(material == number, COURANT / PERMITTIVITY[number], 0.0)
    return total


def ahead(field, rim, axis):
    following = lax.slice_in_dim(field, 1, field.shape[axis], axis=axis)
    return jnp.concatenate([following, rim], axis) - field


def behind(field, rim, axis):
    earlier = lax.slice_in_dim(field, 0, field.shape[axis] - 1, axis=axis)
    return field - jnp.concatenate([rim, earlier], axis)


def neighbour_rims(row_x, col_y, offset):
    got_x = passed_along(row_x, "tx", offset)
    got_y = passed_along(col_y, "ty", offset)
    return (got_x, got_y)


def butterfly_gather(block, axis, order):
    me = lax.axis_index(axis)
    n = lax.axis_size(axis)
    held = block[None]
    for d in order:
        other = lax.ppermute(held, axis, [(i, i ^ d) for i in range(n)])
        low = (me // d) % 2 == 0
        held = jnp.where(low, jnp.concatenate([held, other], 0), jnp.concatenate([other, held], 0))
    return held


def gather_order(n):
    order = []
    d = n // 2
    while d >= 1:
        order.append(d)
        d //= 2
    return order


def chunk_starts(order, size):
    starts = []
    for q in range(2 ** len(order)):
        c = sum(order[t] for t in range(len(order)) if (q >> t) & 1)
        starts.append(c * size)
    return jnp.array(starts, dtype=jnp.int32)


def chunk_tables(order, size, total, positions, length):
    c1, s1 = phase_tables(chunk_starts(order, size), positions, length)
    c2, s2 = phase_tables(jnp.arange(size, dtype=jnp.int32) - total // 2, positions, length)
    cos_t = c1[:, None, :] * c2[None, :, :] - s1[:, None, :] * s2[None, :, :]
    sin_t = s1[:, None, :] * c2[None, :, :] + c1[:, None, :] * s2[None, :, :]
    return cos_t, sin_t


def injection_plane(orders, offsets, cells_x, cells_y):
    points, _, rows_kx, cols_ky = orders.shape
    n_tx = lax.axis_size("tx")
    n_ty = lax.axis_size("ty")
    full_x = cells_x * n_tx
    full_y = cells_y * n_ty
    order_y = gather_order(n_ty)
    amp = butterfly_gather(orders, "ty", order_y)
    a_re = amp[:, :, 0]
    a_im = amp[:, :, 1]
    y_pos = lax.axis_index("ty") * cells_y + jnp.arange(cells_y, dtype=jnp.int32)
    by_c, by_s = chunk_tables(order_y, cols_ky, cols_ky * n_ty, y_pos, full_y)
    sy_c, sy_s = phase_tables(offsets[:, 1], y_pos, full_y)
    m_re = jnp.einsum("cpkj,cjy->pky", a_re, by_c, precision=PREC) - jnp.einsum(
        "cpkj,cjy->pky", a_im, by_s, precision=PREC
    )
    m_im = jnp.einsum("cpkj,cjy->pky", a_re, by_s, precision=PREC) + jnp.einsum(
        "cpkj,cjy->pky", a_im, by_c, precision=PREC
    )
    sy_c = sy_c[:, None, :]
    sy_s = sy_s[:, None, :]
    inner = jnp.stack([m_re * sy_c - m_im * sy_s, m_re * sy_s + m_im * sy_c], 1)
    order_x = gather_order(n_tx)
    inner = butterfly_gather(inner, "tx", order_x)
    i_re = inner[:, :, 0]
    i_im = inner[:, :, 1]
    x_pos = lax.axis_index("tx") * cells_x + jnp.arange(cells_x, dtype=jnp.int32)
    bx_c, bx_s = chunk_tables(order_x, rows_kx, rows_kx * n_tx, x_pos, full_x)
    sx_c, sx_s = phase_tables(offsets[:, 0], x_pos, full_x)
    q_re = jnp.einsum("ckx,cpky->pxy", bx_c, i_re, precision=PREC) - jnp.einsum(
        "ckx,cpky->pxy", bx_s, i_im, precision=PREC
    )
    q_im = jnp.einsum("ckx,cpky->pxy", bx_c, i_im, precision=PREC) + jnp.einsum(
        "ckx,cpky->pxy", bx_s, i_re, precision=PREC
    )
    sx_c = sx_c[:, :, None]
    sx_s = sx_s[:, :, None]
    plane = jnp.stack(
        [jnp.sum(q_re * sx_c - q_im * sx_s, 0), jnp.sum(q_re * sx_s + q_im * sx_c, 0)]
    )
    n_src = lax.axis_size("src")
    other = lax.ppermute(plane, "src", [(i, (i + 1) % n_src) for i in range(n_src)])
    return plane + other


def per_device(orders, offsets, material, e_field, h_field):
    layers, cells_x, cells_y = material.shape
    plane = injection_plane(orders, offsets, cells_x, cells_y)
    plane_re = plane[0]
    plane_im = plane[1]
    coefficient = cell_coefficient(material)
    zero_z = jnp.zeros((1, cells_x, cells_y), jnp.float32)
    e_x, e_y, e_z = (e_field[0], e_field[1], e_field[2])
    h_x, h_y, h_z = (h_field[0], h_field[1], h_field[2])
    for step in range(STEPS):
        rim_x, rim_y = neighbour_rims(
            jnp.stack([e_y[:, 0, :], e_z[:, 0, :]]), jnp.stack([e_x[:, :, 0], e_z[:, :, 0]]), -1
        )
        h_x = h_x - COURANT * (ahead(e_z, rim_y[1][:, :, None], 2) - ahead(e_y, zero_z, 0))
        h_y = h_y - COURANT * (ahead(e_x, zero_z, 0) - ahead(e_z, rim_x[1][:, None, :], 1))
        h_z = h_z - COURANT * (
            ahead(e_y, rim_x[0][:, None, :], 1) - ahead(e_x, rim_y[0][:, :, None], 2)
        )
        rim_x, rim_y = neighbour_rims(
            jnp.stack([h_y[:, -1, :], h_z[:, -1, :]]), jnp.stack([h_x[:, :, -1], h_z[:, :, -1]]), 1
        )
        e_x = e_x + coefficient * (behind(h_z, rim_y[1][:, :, None], 2) - behind(h_y, zero_z, 0))
        e_y = e_y + coefficient * (behind(h_x, zero_z, 0) - behind(h_z, rim_x[1][:, None, :], 1))
        e_z = e_z + coefficient * (
            behind(h_y, rim_x[0][:, None, :], 1) - behind(h_x, rim_y[0][:, :, None], 2)
        )
        cosine = math.cos(OMEGA * (step + 1))
        sine = math.sin(OMEGA * (step + 1))
        e_x = e_x.at[ZINJ].add(COURANT * (cosine * plane_re - sine * plane_im))
        e_y = e_y.at[ZINJ].add(COURANT * (sine * plane_re + cosine * plane_im))
    return (jnp.stack([e_x, e_y, e_z]), jnp.stack([h_x, h_y, h_z]))


def solution(mesh):
    in_specs = (
        P("src", None, "tx", "ty"),
        P("src", None),
        P(None, "tx", "ty"),
        P(None, None, "tx", "ty"),
        P(None, None, "tx", "ty"),
    )
    out_specs = (P(None, None, "tx", "ty"), P(None, None, "tx", "ty"))
    return jax.shard_map(
        per_device, mesh=mesh, in_specs=in_specs, out_specs=out_specs, check_vma=False
    )
```

```python
import math

import jax
import jax.numpy as jnp
from jax import lax
from jax.sharding import PartitionSpec as P
from jax.experimental import pallas as pl
from jax.experimental.pallas import tpu as pltpu

STEPS = 4
ZINJ = 1


COURANT = 0.5
OMEGA = 0.7
PERMITTIVITY = (1.0, 2.6, 11.9, 2.1)
PREC = lax.Precision.HIGH


def passed_along(block, axis, distance):
    devices = range(lax.axis_size(axis))
    route = [((i - distance) % len(devices), i) for i in devices]
    return lax.ppermute(block, axis, route)


def phase_tables(freqs, positions, length):
    product = jnp.mod(freqs[:, None] * positions[None, :], length)
    angle = product.astype(jnp.float32) * (2.0 * math.pi / length)
    return (jnp.cos(angle), jnp.sin(angle))


def cell_coefficient(material):
    total = jnp.zeros(material.shape, jnp.float32)
    for number in range(len(PERMITTIVITY)):
        total = total + jnp.where(material == number, COURANT / PERMITTIVITY[number], 0.0)
    return total


def ahead(field, rim, axis):
    following = lax.slice_in_dim(field, 1, field.shape[axis], axis=axis)
    return jnp.concatenate([following, rim], axis) - field


def behind(field, rim, axis):
    earlier = lax.slice_in_dim(field, 0, field.shape[axis] - 1, axis=axis)
    return field - jnp.concatenate([rim, earlier], axis)


def neighbour_rims(row_x, col_y, offset):
    got_x = passed_along(row_x, "tx", offset)
    got_y = passed_along(col_y, "ty", offset)
    return (got_x, got_y)


def butterfly_gather(block, axis, order):
    me = lax.axis_index(axis)
    n = lax.axis_size(axis)
    held = block[None]
    for d in order:
        other = lax.ppermute(held, axis, [(i, i ^ d) for i in range(n)])
        low = (me // d) % 2 == 0
        held = jnp.where(low, jnp.concatenate([held, other], 0), jnp.concatenate([other, held], 0))
    return held


def gather_order(n):
    order = []
    d = n // 2
    while d >= 1:
        order.append(d)
        d //= 2
    return order


def chunk_starts(order, size):
    starts = []
    for q in range(2 ** len(order)):
        c = sum(order[t] for t in range(len(order)) if (q >> t) & 1)
        starts.append(c * size)
    return jnp.array(starts, dtype=jnp.int32)


def chunk_tables(order, size, total, positions, length):
    c1, s1 = phase_tables(chunk_starts(order, size), positions, length)
    c2, s2 = phase_tables(jnp.arange(size, dtype=jnp.int32) - total // 2, positions, length)
    cos_t = c1[:, None, :] * c2[None, :, :] - s1[:, None, :] * s2[None, :, :]
    sin_t = s1[:, None, :] * c2[None, :, :] + c1[:, None, :] * s2[None, :, :]
    return cos_t, sin_t


def injection_plane(orders, offsets, cells_x, cells_y):
    points, _, rows_kx, cols_ky = orders.shape
    n_tx = lax.axis_size("tx")
    n_ty = lax.axis_size("ty")
    full_x = cells_x * n_tx
    full_y = cells_y * n_ty
    order_y = gather_order(n_ty)
    amp = butterfly_gather(orders, "ty", order_y)
    a_re = amp[:, :, 0]
    a_im = amp[:, :, 1]
    y_pos = lax.axis_index("ty") * cells_y + jnp.arange(cells_y, dtype=jnp.int32)
    by_c, by_s = chunk_tables(order_y, cols_ky, cols_ky * n_ty, y_pos, full_y)
    sy_c, sy_s = phase_tables(offsets[:, 1], y_pos, full_y)
    m_re = jnp.einsum("cpkj,cjy->pky", a_re, by_c, precision=PREC) - jnp.einsum(
        "cpkj,cjy->pky", a_im, by_s, precision=PREC
    )
    m_im = jnp.einsum("cpkj,cjy->pky", a_re, by_s, precision=PREC) + jnp.einsum(
        "cpkj,cjy->pky", a_im, by_c, precision=PREC
    )
    sy_c = sy_c[:, None, :]
    sy_s = sy_s[:, None, :]
    inner = jnp.stack([m_re * sy_c - m_im * sy_s, m_re * sy_s + m_im * sy_c], 1)
    order_x = gather_order(n_tx)
    inner = butterfly_gather(inner, "tx", order_x)
    i_re = inner[:, :, 0]
    i_im = inner[:, :, 1]
    x_pos = lax.axis_index("tx") * cells_x + jnp.arange(cells_x, dtype=jnp.int32)
    bx_c, bx_s = chunk_tables(order_x, rows_kx, rows_kx * n_tx, x_pos, full_x)
    sx_c, sx_s = phase_tables(offsets[:, 0], x_pos, full_x)
    q_re = jnp.einsum("ckx,cpky->pxy", bx_c, i_re, precision=PREC) - jnp.einsum(
        "ckx,cpky->pxy", bx_s, i_im, precision=PREC
    )
    q_im = jnp.einsum("ckx,cpky->pxy", bx_c, i_im, precision=PREC) + jnp.einsum(
        "ckx,cpky->pxy", bx_s, i_re, precision=PREC
    )
    sx_c = sx_c[:, :, None]
    sx_s = sx_s[:, :, None]
    plane = jnp.stack(
        [jnp.sum(q_re * sx_c - q_im * sx_s, 0), jnp.sum(q_re * sx_s + q_im * sx_c, 0)]
    )
    n_src = lax.axis_size("src")
    other = lax.ppermute(plane, "src", [(i, (i + 1) % n_src) for i in range(n_src)])
    return plane + other


def yee_kernel(e_ref, h_ref, coef_ref, plane_ref, xa_ref, xb_ref, yh_ref, eo_ref, ho_ref, ext, cp, tmp):
    layers, cells_x, cells_y = coef_ref.shape
    depth = xa_ref.shape[1]
    rows = cells_x + 2 * depth
    lanes = ext.shape[2]
    slab = layers + 2
    n_field = 6 * layers
    zero = jnp.zeros((rows, lanes), jnp.float32)
    for comp in range(3):
        ext[comp * slab + slab - 1] = zero
        ext[(3 + comp) * slab] = zero
    tmp[...] = jnp.zeros_like(tmp)
    lane = lax.broadcasted_iota(jnp.int32, (rows, cells_y), 1)

    def place(h, slot, own):
        dst = ext if slot is not None else cp
        idx = slot if slot is not None else h - n_field
        dst[idx, 0:cells_x, 0:cells_y] = own
        dst[idx, cells_x:cells_x + depth, 0:cells_y] = xa_ref[h]
        dst[idx, cells_x + depth:rows, 0:cells_y] = xb_ref[h]
        tmp[:, 0:2 * depth] = yh_ref[h].T
        v = tmp[...]
        front = jnp.where(lane < depth, v, 0.0)
        back = jnp.where(lane >= depth, v, 0.0)
        dst[idx, :, cells_y:lanes] = front + pltpu.roll(back, cells_y - 2 * depth, 1)

    def fields(h, carry):
        comp = h // layers
        z = h % layers
        slot = comp * slab + z + 1
        own = jnp.where(comp < 3, e_ref[comp % 3, z], h_ref[comp % 3, z])
        place(h, slot, own)
        return carry

    lax.fori_loop(0, n_field, fields, 0)
    for z in range(layers):
        place(n_field + z, None, coef_ref[z])
    for k in range(2):
        place(n_field + layers + k, None, plane_ref[k])

    ahead_x = lambda f: pltpu.roll(f, rows - 1, 0)
    ahead_y = lambda f: pltpu.roll(f, lanes - 1, 1)
    behind_x = lambda f: pltpu.roll(f, 1, 0)
    behind_y = lambda f: pltpu.roll(f, 1, 1)
    ex_, ey_, ez_, hx_, hy_, hz_ = (c * slab for c in range(6))

    for step in range(STEPS):
        def h_update(z, carry):
            s = z + 1
            e_x = ext[ex_ + s]
            e_y = ext[ey_ + s]
            e_z = ext[ez_ + s]
            ext[hx_ + s] = ext[hx_ + s] - COURANT * ((ahead_y(e_z) - e_z) - (ext[ey_ + s + 1] - e_y))
            ext[hy_ + s] = ext[hy_ + s] - COURANT * ((ext[ex_ + s + 1] - e_x) - (ahead_x(e_z) - e_z))
            ext[hz_ + s] = ext[hz_ + s] - COURANT * ((ahead_x(e_y) - e_y) - (ahead_y(e_x) - e_x))
            return carry

        def e_update(z, carry):
            s = z + 1
            h_x = ext[hx_ + s]
            h_y = ext[hy_ + s]
            h_z = ext[hz_ + s]
            c = cp[z]
            ext[ex_ + s] = ext[ex_ + s] + c * ((h_z - behind_y(h_z)) - (h_y - ext[hy_ + s - 1]))
            ext[ey_ + s] = ext[ey_ + s] + c * ((h_x - ext[hx_ + s - 1]) - (h_z - behind_x(h_z)))
            ext[ez_ + s] = ext[ez_ + s] + c * ((h_y - behind_x(h_y)) - (h_x - behind_y(h_x)))
            return carry

        lax.fori_loop(0, layers, h_update, 0)
        lax.fori_loop(0, layers, e_update, 0)
        cosine = math.cos(OMEGA * (step + 1))
        sine = math.sin(OMEGA * (step + 1))
        p_re = cp[layers]
        p_im = cp[layers + 1]
        s = ZINJ + 1
        ext[ex_ + s] = ext[ex_ + s] + COURANT * (cosine * p_re - sine * p_im)
        ext[ey_ + s] = ext[ey_ + s] + COURANT * (sine * p_re + cosine * p_im)

    for comp in range(3):
        for z in range(layers):
            eo_ref[comp, z] = ext[comp * slab + z + 1, 0:cells_x, 0:cells_y]
            ho_ref[comp, z] = ext[(3 + comp) * slab + z + 1, 0:cells_x, 0:cells_y]


def exchange_halos(parts, depth):
    n_tx = lax.axis_size("tx")
    n_ty = lax.axis_size("ty")

    def from_offset(block, dx, dy):
        pairs = []
        for i in range(n_tx):
            for j in range(n_ty):
                src_dev = ((i + dx) % n_tx) * n_ty + (j + dy) % n_ty
                pairs.append((src_dev, i * n_ty + j))
        return lax.ppermute(block, ("tx", "ty"), pairs)

    head = slice(0, depth)
    tail = slice(-depth, None)
    xa = from_offset(parts[:, head, :], 1, 0)
    xb = from_offset(parts[:, tail, :], -1, 0)
    t = lambda b: jnp.swapaxes(b, 1, 2)
    ya = from_offset(t(parts[:, :, head]), 0, 1)
    yb = from_offset(t(parts[:, :, tail]), 0, -1)
    aa = from_offset(t(parts[:, head, head]), 1, 1)
    ab = from_offset(t(parts[:, head, tail]), 1, -1)
    ba = from_offset(t(parts[:, tail, head]), -1, 1)
    bb = from_offset(t(parts[:, tail, tail]), -1, -1)
    y_ahead = jnp.concatenate([ya, aa, ba], 2)
    y_behind = jnp.concatenate([yb, ab, bb], 2)
    return xa, xb, jnp.concatenate([y_ahead, y_behind], 1)


def per_device(orders, offsets, material, e_field, h_field):
    layers, cells_x, cells_y = material.shape
    plane = injection_plane(orders, offsets, cells_x, cells_y)
    coefficient = cell_coefficient(material)
    parts = jnp.concatenate(
        [
            e_field.reshape(3 * layers, cells_x, cells_y),
            h_field.reshape(3 * layers, cells_x, cells_y),
            coefficient,
            plane,
        ],
        0,
    )
    depth = STEPS
    xa, xb, yh = exchange_halos(parts, depth)
    rows = cells_x + 2 * depth
    lanes = 2 * cells_y
    vmem = pltpu.MemorySpace.VMEM
    spec = pl.BlockSpec(memory_space=vmem)
    out = jax.ShapeDtypeStruct(e_field.shape, jnp.float32)
    return pl.pallas_call(
        yee_kernel,
        out_shape=(out, out),
        in_specs=[spec] * 7,
        out_specs=(spec, spec),
        scratch_shapes=[
            pltpu.VMEM((6 * (layers + 2), rows, lanes), jnp.float32),
            pltpu.VMEM((layers + 2, rows, lanes), jnp.float32),
            pltpu.VMEM((rows, cells_y), jnp.float32),
        ],
        compiler_params=pltpu.CompilerParams(vmem_limit_bytes=64 * 1024 * 1024),
    )(e_field, h_field, coefficient, plane, xa, xb, yh)


def solution(mesh):
    in_specs = (
        P("src", None, "tx", "ty"),
        P("src", None),
        P(None, "tx", "ty"),
        P(None, None, "tx", "ty"),
        P(None, None, "tx", "ty"),
    )
    out_specs = (P(None, None, "tx", "ty"), P(None, None, "tx", "ty"))
    return jax.shard_map(
        per_device, mesh=mesh, in_specs=in_specs, out_specs=out_specs, check_vma=False
    )
```

```python
import math

import jax
import jax.numpy as jnp
from jax import lax
from jax.sharding import PartitionSpec as P
from jax.experimental import pallas as pl
from jax.experimental.pallas import tpu as pltpu

STEPS = 4
ZINJ = 1


COURANT = 0.5
OMEGA = 0.7
PERMITTIVITY = (1.0, 2.6, 11.9, 2.1)
PREC = lax.Precision.HIGH


def phase_tables(freqs, positions, length):
    product = jnp.mod(freqs[:, None] * positions[None, :], length)
    angle = product.astype(jnp.float32) * (2.0 * math.pi / length)
    return (jnp.cos(angle), jnp.sin(angle))


def cell_coefficient(material):
    total = jnp.zeros(material.shape, jnp.float32)
    for number in range(len(PERMITTIVITY)):
        total = total + jnp.where(material == number, COURANT / PERMITTIVITY[number], 0.0)
    return total


MESH = pl.DeviceIdType.MESH
VMEM_SPEC = pl.BlockSpec(memory_space=pltpu.MemorySpace.VMEM)


def gather_along(block, axis, collective):
    n = lax.axis_size(axis)

    def kernel(x_ref, o_ref, send, recv, local):
        me = lax.axis_index(axis)
        barrier = pltpu.get_barrier_semaphore()
        for k in range(1, n):
            pl.semaphore_signal(barrier, 1, device_id={axis: lax.rem(me + k, n)}, device_id_type=MESH)
        pl.semaphore_wait(barrier, n - 1)
        own = pltpu.make_async_copy(x_ref, o_ref.at[me], local.at[0])
        own.start()
        copies = []
        for k in range(1, n):
            copy = pltpu.make_async_remote_copy(
                src_ref=x_ref,
                dst_ref=o_ref.at[me],
                send_sem=send.at[k - 1],
                recv_sem=recv.at[k - 1],
                device_id={axis: lax.rem(me + k, n)},
                device_id_type=MESH,
            )
            copy.start()
            copies.append(copy)
        own.wait()
        for copy in copies:
            copy.wait()

    return pl.pallas_call(
        kernel,
        out_shape=jax.ShapeDtypeStruct((n,) + block.shape, block.dtype),
        in_specs=[VMEM_SPEC],
        out_specs=VMEM_SPEC,
        scratch_shapes=[
            pltpu.SemaphoreType.DMA((n - 1,)),
            pltpu.SemaphoreType.DMA((n - 1,)),
            pltpu.SemaphoreType.DMA((1,)),
        ],
        compiler_params=pltpu.CompilerParams(collective_id=collective, has_side_effects=True),
    )(block)


def summed_over_pair(block, axis, collective):
    def kernel(x_ref, o_ref, got, send, recv):
        other = 1 - lax.axis_index(axis)
        barrier = pltpu.get_barrier_semaphore()
        pl.semaphore_signal(barrier, 1, device_id={axis: other}, device_id_type=MESH)
        pl.semaphore_wait(barrier, 1)
        copy = pltpu.make_async_remote_copy(
            src_ref=x_ref, dst_ref=got, send_sem=send.at[0], recv_sem=recv.at[0],
            device_id={axis: other}, device_id_type=MESH,
        )
        copy.start()
        copy.wait()
        o_ref[...] = x_ref[...] + got[...]

    return pl.pallas_call(
        kernel,
        out_shape=jax.ShapeDtypeStruct(block.shape, block.dtype),
        in_specs=[VMEM_SPEC],
        out_specs=VMEM_SPEC,
        scratch_shapes=[
            pltpu.VMEM(block.shape, block.dtype),
            pltpu.SemaphoreType.DMA((1,)),
            pltpu.SemaphoreType.DMA((1,)),
        ],
        compiler_params=pltpu.CompilerParams(collective_id=collective, has_side_effects=True),
    )(block)


def chunk_tables(size, count, positions, length):
    c1, s1 = phase_tables(jnp.arange(count, dtype=jnp.int32) * size, positions, length)
    c2, s2 = phase_tables(jnp.arange(size, dtype=jnp.int32) - size * count // 2, positions, length)
    cos_t = c1[:, None, :] * c2[None, :, :] - s1[:, None, :] * s2[None, :, :]
    sin_t = s1[:, None, :] * c2[None, :, :] + c1[:, None, :] * s2[None, :, :]
    return cos_t, sin_t


def injection_plane(orders, offsets, cells_x, cells_y):
    points, _, rows_kx, cols_ky = orders.shape
    n_tx = lax.axis_size("tx")
    n_ty = lax.axis_size("ty")
    full_x = cells_x * n_tx
    full_y = cells_y * n_ty
    amp = gather_along(orders, "ty", 0)
    a_re = amp[:, :, 0]
    a_im = amp[:, :, 1]
    y_pos = lax.axis_index("ty") * cells_y + jnp.arange(cells_y, dtype=jnp.int32)
    by_c, by_s = chunk_tables(cols_ky, n_ty, y_pos, full_y)
    sy_c, sy_s = phase_tables(offsets[:, 1], y_pos, full_y)
    m_re = jnp.einsum("cpkj,cjy->pky", a_re, by_c, precision=PREC) - jnp.einsum(
        "cpkj,cjy->pky", a_im, by_s, precision=PREC
    )
    m_im = jnp.einsum("cpkj,cjy->pky", a_re, by_s, precision=PREC) + jnp.einsum(
        "cpkj,cjy->pky", a_im, by_c, precision=PREC
    )
    sy_c = sy_c[:, None, :]
    sy_s = sy_s[:, None, :]
    inner = jnp.stack([m_re * sy_c - m_im * sy_s, m_re * sy_s + m_im * sy_c], 1)
    inner = gather_along(inner, "tx", 1)
    i_re = inner[:, :, 0]
    i_im = inner[:, :, 1]
    x_pos = lax.axis_index("tx") * cells_x + jnp.arange(cells_x, dtype=jnp.int32)
    bx_c, bx_s = chunk_tables(rows_kx, n_tx, x_pos, full_x)
    sx_c, sx_s = phase_tables(offsets[:, 0], x_pos, full_x)
    q_re = jnp.einsum("ckx,cpky->pxy", bx_c, i_re, precision=PREC) - jnp.einsum(
        "ckx,cpky->pxy", bx_s, i_im, precision=PREC
    )
    q_im = jnp.einsum("ckx,cpky->pxy", bx_c, i_im, precision=PREC) + jnp.einsum(
        "ckx,cpky->pxy", bx_s, i_re, precision=PREC
    )
    sx_c = sx_c[:, :, None]
    sx_s = sx_s[:, :, None]
    plane = jnp.stack(
        [jnp.sum(q_re * sx_c - q_im * sx_s, 0), jnp.sum(q_re * sx_s + q_im * sx_c, 0)]
    )
    return summed_over_pair(plane, "src", 2)


def yee_kernel(e_ref, h_ref, coef_ref, plane_ref, xa_ref, xb_ref, yh_ref, eo_ref, ho_ref, ext, cp, tmp):
    layers, cells_x, cells_y = coef_ref.shape
    depth = xa_ref.shape[1]
    rows = cells_x + 2 * depth
    lanes = ext.shape[2]
    slab = layers + 2
    n_field = 6 * layers
    zero = jnp.zeros((rows, lanes), jnp.float32)
    for comp in range(3):
        ext[comp * slab + slab - 1] = zero
        ext[(3 + comp) * slab] = zero
    tmp[...] = jnp.zeros_like(tmp)
    lane = lax.broadcasted_iota(jnp.int32, (rows, cells_y), 1)

    def place(h, slot, own):
        dst = ext if slot is not None else cp
        idx = slot if slot is not None else h - n_field
        dst[idx, 0:cells_x, 0:cells_y] = own
        dst[idx, cells_x:cells_x + depth, 0:cells_y] = xa_ref[h]
        dst[idx, cells_x + depth:rows, 0:cells_y] = xb_ref[h]
        tmp[:, 0:2 * depth] = yh_ref[h].T
        v = tmp[...]
        front = jnp.where(lane < depth, v, 0.0)
        back = jnp.where(lane >= depth, v, 0.0)
        dst[idx, :, cells_y:lanes] = front + pltpu.roll(back, cells_y - 2 * depth, 1)

    def fields(h, carry):
        comp = h // layers
        z = h % layers
        slot = comp * slab + z + 1
        own = jnp.where(comp < 3, e_ref[comp % 3, z], h_ref[comp % 3, z])
        place(h, slot, own)
        return carry

    lax.fori_loop(0, n_field, fields, 0)
    for z in range(layers):
        place(n_field + z, None, coef_ref[z])
    for k in range(2):
        place(n_field + layers + k, None, plane_ref[k])

    ahead_x = lambda f: pltpu.roll(f, rows - 1, 0)
    ahead_y = lambda f: pltpu.roll(f, lanes - 1, 1)
    behind_x = lambda f: pltpu.roll(f, 1, 0)
    behind_y = lambda f: pltpu.roll(f, 1, 1)
    ex_, ey_, ez_, hx_, hy_, hz_ = (c * slab for c in range(6))

    for step in range(STEPS):
        def h_update(z, carry):
            s = z + 1
            e_x = ext[ex_ + s]
            e_y = ext[ey_ + s]
            e_z = ext[ez_ + s]
            ext[hx_ + s] = ext[hx_ + s] - COURANT * ((ahead_y(e_z) - e_z) - (ext[ey_ + s + 1] - e_y))
            ext[hy_ + s] = ext[hy_ + s] - COURANT * ((ext[ex_ + s + 1] - e_x) - (ahead_x(e_z) - e_z))
            ext[hz_ + s] = ext[hz_ + s] - COURANT * ((ahead_x(e_y) - e_y) - (ahead_y(e_x) - e_x))
            return carry

        def e_update(z, carry):
            s = z + 1
            h_x = ext[hx_ + s]
            h_y = ext[hy_ + s]
            h_z = ext[hz_ + s]
            c = cp[z]
            ext[ex_ + s] = ext[ex_ + s] + c * ((h_z - behind_y(h_z)) - (h_y - ext[hy_ + s - 1]))
            ext[ey_ + s] = ext[ey_ + s] + c * ((h_x - ext[hx_ + s - 1]) - (h_z - behind_x(h_z)))
            ext[ez_ + s] = ext[ez_ + s] + c * ((h_y - behind_x(h_y)) - (h_x - behind_y(h_x)))
            return carry

        lax.fori_loop(0, layers, h_update, 0)
        lax.fori_loop(0, layers, e_update, 0)
        cosine = math.cos(OMEGA * (step + 1))
        sine = math.sin(OMEGA * (step + 1))
        p_re = cp[layers]
        p_im = cp[layers + 1]
        s = ZINJ + 1
        ext[ex_ + s] = ext[ex_ + s] + COURANT * (cosine * p_re - sine * p_im)
        ext[ey_ + s] = ext[ey_ + s] + COURANT * (sine * p_re + cosine * p_im)

    for comp in range(3):
        for z in range(layers):
            eo_ref[comp, z] = ext[comp * slab + z + 1, 0:cells_x, 0:cells_y]
            ho_ref[comp, z] = ext[(3 + comp) * slab + z + 1, 0:cells_x, 0:cells_y]


OFFSETS = ((1, 0), (-1, 0), (0, 1), (0, -1), (1, 1), (1, -1), (-1, 1), (-1, -1))


def exchange_halos(parts, depth):
    head = slice(0, depth)
    tail = slice(-depth, None)
    t = lambda b: jnp.swapaxes(b, 1, 2)
    outgoing = [
        parts[:, head, :],
        parts[:, tail, :],
        t(parts[:, :, head]),
        t(parts[:, :, tail]),
        t(parts[:, head, head]),
        t(parts[:, head, tail]),
        t(parts[:, tail, head]),
        t(parts[:, tail, tail]),
    ]
    count = len(OFFSETS)

    def kernel(*refs):
        ins = refs[:count]
        outs = refs[count:2 * count]
        send, recv = refs[2 * count:]
        n_tx = lax.axis_size("tx")
        n_ty = lax.axis_size("ty")
        me_x = lax.axis_index("tx")
        me_y = lax.axis_index("ty")
        targets = [
            {"tx": lax.rem(me_x - dx + n_tx, n_tx), "ty": lax.rem(me_y - dy + n_ty, n_ty)}
            for dx, dy in OFFSETS
        ]
        barrier = pltpu.get_barrier_semaphore()
        for target in targets:
            pl.semaphore_signal(barrier, 1, device_id=target, device_id_type=MESH)
        pl.semaphore_wait(barrier, count)
        copies = []
        for k in range(count):
            copy = pltpu.make_async_remote_copy(
                src_ref=ins[k], dst_ref=outs[k], send_sem=send.at[k], recv_sem=recv.at[k],
                device_id=targets[k], device_id_type=MESH,
            )
            copy.start()
            copies.append(copy)
        for copy in copies:
            copy.wait()

    got = pl.pallas_call(
        kernel,
        out_shape=tuple(jax.ShapeDtypeStruct(p.shape, p.dtype) for p in outgoing),
        in_specs=[VMEM_SPEC] * count,
        out_specs=tuple([VMEM_SPEC] * count),
        scratch_shapes=[pltpu.SemaphoreType.DMA((count,)), pltpu.SemaphoreType.DMA((count,))],
        compiler_params=pltpu.CompilerParams(collective_id=3, has_side_effects=True),
    )(*outgoing)
    xa, xb, ya, yb, aa, ab, ba, bb = got
    y_ahead = jnp.concatenate([ya, aa, ba], 2)
    y_behind = jnp.concatenate([yb, ab, bb], 2)
    return xa, xb, jnp.concatenate([y_ahead, y_behind], 1)


def per_device(orders, offsets, material, e_field, h_field):
    layers, cells_x, cells_y = material.shape
    plane = injection_plane(orders, offsets, cells_x, cells_y)
    coefficient = cell_coefficient(material)
    parts = jnp.concatenate(
        [
            e_field.reshape(3 * layers, cells_x, cells_y),
            h_field.reshape(3 * layers, cells_x, cells_y),
            coefficient,
            plane,
        ],
        0,
    )
    depth = STEPS
    xa, xb, yh = exchange_halos(parts, depth)
    rows = cells_x + 2 * depth
    lanes = 2 * cells_y
    vmem = pltpu.MemorySpace.VMEM
    spec = pl.BlockSpec(memory_space=vmem)
    out = jax.ShapeDtypeStruct(e_field.shape, jnp.float32)
    return pl.pallas_call(
        yee_kernel,
        out_shape=(out, out),
        in_specs=[spec] * 7,
        out_specs=(spec, spec),
        scratch_shapes=[
            pltpu.VMEM((6 * (layers + 2), rows, lanes), jnp.float32),
            pltpu.VMEM((layers + 2, rows, lanes), jnp.float32),
            pltpu.VMEM((rows, cells_y), jnp.float32),
        ],
        compiler_params=pltpu.CompilerParams(vmem_limit_bytes=64 * 1024 * 1024),
    )(e_field, h_field, coefficient, plane, xa, xb, yh)


def solution(mesh):
    in_specs = (
        P("src", None, "tx", "ty"),
        P("src", None),
        P(None, "tx", "ty"),
        P(None, None, "tx", "ty"),
        P(None, None, "tx", "ty"),
    )
    out_specs = (P(None, None, "tx", "ty"), P(None, None, "tx", "ty"))
    return jax.shard_map(
        per_device, mesh=mesh, in_specs=in_specs, out_specs=out_specs, check_vma=False
    )
```

```python
import math

import jax
import jax.numpy as jnp
from jax import lax
from jax.sharding import PartitionSpec as P
from jax.experimental import pallas as pl
from jax.experimental.pallas import tpu as pltpu

STEPS = 4
ZINJ = 1


COURANT = 0.5
OMEGA = 0.7
PERMITTIVITY = (1.0, 2.6, 11.9, 2.1)
PREC = lax.Precision.HIGH
SHIFT = 8


def phase_tables(freqs, positions, length):
    product = jnp.mod(freqs[:, None] * positions[None, :], length)
    angle = product.astype(jnp.float32) * (2.0 * math.pi / length)
    return (jnp.cos(angle), jnp.sin(angle))


def cell_coefficient(material):
    total = jnp.zeros(material.shape, jnp.float32)
    for number in range(len(PERMITTIVITY)):
        total = total + jnp.where(material == number, COURANT / PERMITTIVITY[number], 0.0)
    return total


MESH = pl.DeviceIdType.MESH
VMEM_SPEC = pl.BlockSpec(memory_space=pltpu.MemorySpace.VMEM)


def gather_along(block, axes, collective):
    sizes = [lax.axis_size(a) for a in axes]
    n = 1
    for s in sizes:
        n *= s

    def coords(linear):
        out = {}
        for a, s in reversed(list(zip(axes, sizes))):
            out[a] = lax.rem(linear, s)
            linear = linear // s
        return out

    def kernel(x_ref, o_ref, send, recv, local):
        me = 0
        for a, s in zip(axes, sizes):
            me = me * s + lax.axis_index(a)
        barrier = pltpu.get_barrier_semaphore()
        for k in range(1, n):
            pl.semaphore_signal(barrier, 1, device_id=coords(lax.rem(me + k, n)), device_id_type=MESH)
        pl.semaphore_wait(barrier, n - 1)
        own = pltpu.make_async_copy(x_ref, o_ref.at[me], local.at[0])
        own.start()
        copies = []
        for k in range(1, n):
            copy = pltpu.make_async_remote_copy(
                src_ref=x_ref,
                dst_ref=o_ref.at[me],
                send_sem=send.at[k - 1],
                recv_sem=recv.at[k - 1],
                device_id=coords(lax.rem(me + k, n)),
                device_id_type=MESH,
            )
            copy.start()
            copies.append(copy)
        own.wait()
        for copy in copies:
            copy.wait()

    return pl.pallas_call(
        kernel,
        out_shape=jax.ShapeDtypeStruct((n,) + block.shape, block.dtype),
        in_specs=[VMEM_SPEC],
        out_specs=VMEM_SPEC,
        scratch_shapes=[
            pltpu.SemaphoreType.DMA((n - 1,)),
            pltpu.SemaphoreType.DMA((n - 1,)),
            pltpu.SemaphoreType.DMA((1,)),
        ],
        compiler_params=pltpu.CompilerParams(collective_id=collective, has_side_effects=True),
    )(block)


def chunk_tables(step, span, count, base, positions, length):
    c1, s1 = phase_tables(jnp.arange(count, dtype=jnp.int32) * step, positions, length)
    c2, s2 = phase_tables(jnp.arange(span, dtype=jnp.int32) - base, positions, length)
    cos_t = c1[:, None, :] * c2[None, :, :] - s1[:, None, :] * s2[None, :, :]
    sin_t = s1[:, None, :] * c2[None, :, :] + c1[:, None, :] * s2[None, :, :]
    return cos_t, sin_t


def lane_dense(block):
    flat = block.reshape(-1)
    pad = (-flat.shape[0]) % 1024
    return jnp.pad(flat, (0, pad)).reshape(-1, 128)


def injection_plane(orders, offsets, cells_x, cells_y):
    points, _, rows_kx, cols_ky = orders.shape
    n_src = lax.axis_size("src")
    n_tx = lax.axis_size("tx")
    n_ty = lax.axis_size("ty")
    full_x = cells_x * n_tx
    full_y = cells_y * n_ty
    mx = rows_kx * n_tx
    my = cols_ky * n_ty
    span_x = rows_kx + 2 * SHIFT
    span_y = cols_ky + 2 * SHIFT
    merged = jnp.zeros((2, span_x, span_y), jnp.float32)
    for p in range(points):
        placed = lax.dynamic_update_slice(
            jnp.zeros((2, span_x, span_y), jnp.float32),
            orders[p],
            (0, offsets[p, 0] + SHIFT, offsets[p, 1] + SHIFT),
        )
        merged = merged + placed
    size = merged.size
    got = gather_along(lane_dense(merged), ("src", "ty"), 0)
    got = got.reshape(n_src * n_ty, -1)[:, :size].reshape(n_src, n_ty, 2, span_x, span_y)
    got = jnp.sum(got, 0)
    g_re = got[:, 0]
    g_im = got[:, 1]
    y_pos = lax.axis_index("ty") * cells_y + jnp.arange(cells_y, dtype=jnp.int32)
    by_c, by_s = chunk_tables(cols_ky, span_y, n_ty, my // 2 + SHIFT, y_pos, full_y)
    i_re = jnp.einsum("cuv,cvy->uy", g_re, by_c, precision=PREC) - jnp.einsum(
        "cuv,cvy->uy", g_im, by_s, precision=PREC
    )
    i_im = jnp.einsum("cuv,cvy->uy", g_re, by_s, precision=PREC) + jnp.einsum(
        "cuv,cvy->uy", g_im, by_c, precision=PREC
    )
    inner = gather_along(jnp.stack([i_re, i_im]), ("tx",), 1)
    i_re = inner[:, 0]
    i_im = inner[:, 1]
    x_pos = lax.axis_index("tx") * cells_x + jnp.arange(cells_x, dtype=jnp.int32)
    bx_c, bx_s = chunk_tables(rows_kx, span_x, n_tx, mx // 2 + SHIFT, x_pos, full_x)
    p_re = jnp.einsum("cux,cuy->xy", bx_c, i_re, precision=PREC) - jnp.einsum(
        "cux,cuy->xy", bx_s, i_im, precision=PREC
    )
    p_im = jnp.einsum("cux,cuy->xy", bx_c, i_im, precision=PREC) + jnp.einsum(
        "cux,cuy->xy", bx_s, i_re, precision=PREC
    )
    return jnp.stack([p_re, p_im])


def yee_kernel(e_ref, h_ref, coef_ref, plane_ref, xa_ref, xb_ref, yh_ref, eo_ref, ho_ref, ext, cp, tmp):
    layers, cells_x, cells_y = coef_ref.shape
    depth = xa_ref.shape[1]
    rows = cells_x + 2 * depth
    lanes = ext.shape[2]
    slab = layers + 2
    n_field = 6 * layers
    zero = jnp.zeros((rows, lanes), jnp.float32)
    for comp in range(3):
        ext[comp * slab + slab - 1] = zero
        ext[(3 + comp) * slab] = zero
    tmp[...] = jnp.zeros_like(tmp)
    lane = lax.broadcasted_iota(jnp.int32, (rows, cells_y), 1)

    def place(h, slot, own):
        dst = ext if slot is not None else cp
        idx = slot if slot is not None else h - n_field
        dst[idx, 0:cells_x, 0:cells_y] = own
        dst[idx, cells_x:cells_x + depth, 0:cells_y] = xa_ref[h]
        dst[idx, cells_x + depth:rows, 0:cells_y] = xb_ref[h]
        tmp[:, 0:2 * depth] = yh_ref[h].T
        v = tmp[...]
        front = jnp.where(lane < depth, v, 0.0)
        back = jnp.where(lane >= depth, v, 0.0)
        dst[idx, :, cells_y:lanes] = front + pltpu.roll(back, cells_y - 2 * depth, 1)

    def fields(h, carry):
        comp = h // layers
        z = h % layers
        slot = comp * slab + z + 1
        own = jnp.where(comp < 3, e_ref[comp % 3, z], h_ref[comp % 3, z])
        place(h, slot, own)
        return carry

    lax.fori_loop(0, n_field, fields, 0)
    for z in range(layers):
        place(n_field + z, None, coef_ref[z])
    for k in range(2):
        place(n_field + layers + k, None, plane_ref[k])

    ahead_x = lambda f: pltpu.roll(f, rows - 1, 0)
    ahead_y = lambda f: pltpu.roll(f, lanes - 1, 1)
    behind_x = lambda f: pltpu.roll(f, 1, 0)
    behind_y = lambda f: pltpu.roll(f, 1, 1)
    ex_, ey_, ez_, hx_, hy_, hz_ = (c * slab for c in range(6))

    for step in range(STEPS):
        def h_update(z, carry):
            s = z + 1
            e_x = ext[ex_ + s]
            e_y = ext[ey_ + s]
            e_z = ext[ez_ + s]
            ext[hx_ + s] = ext[hx_ + s] - COURANT * ((ahead_y(e_z) - e_z) - (ext[ey_ + s + 1] - e_y))
            ext[hy_ + s] = ext[hy_ + s] - COURANT * ((ext[ex_ + s + 1] - e_x) - (ahead_x(e_z) - e_z))
            ext[hz_ + s] = ext[hz_ + s] - COURANT * ((ahead_x(e_y) - e_y) - (ahead_y(e_x) - e_x))
            return carry

        def e_update(z, carry):
            s = z + 1
            h_x = ext[hx_ + s]
            h_y = ext[hy_ + s]
            h_z = ext[hz_ + s]
            c = cp[z]
            ext[ex_ + s] = ext[ex_ + s] + c * ((h_z - behind_y(h_z)) - (h_y - ext[hy_ + s - 1]))
            ext[ey_ + s] = ext[ey_ + s] + c * ((h_x - ext[hx_ + s - 1]) - (h_z - behind_x(h_z)))
            ext[ez_ + s] = ext[ez_ + s] + c * ((h_y - behind_x(h_y)) - (h_x - behind_y(h_x)))
            return carry

        lax.fori_loop(0, layers, h_update, 0)
        lax.fori_loop(0, layers, e_update, 0)
        cosine = math.cos(OMEGA * (step + 1))
        sine = math.sin(OMEGA * (step + 1))
        p_re = cp[layers]
        p_im = cp[layers + 1]
        s = ZINJ + 1
        ext[ex_ + s] = ext[ex_ + s] + COURANT * (cosine * p_re - sine * p_im)
        ext[ey_ + s] = ext[ey_ + s] + COURANT * (sine * p_re + cosine * p_im)

    for comp in range(3):
        for z in range(layers):
            eo_ref[comp, z] = ext[comp * slab + z + 1, 0:cells_x, 0:cells_y]
            ho_ref[comp, z] = ext[(3 + comp) * slab + z + 1, 0:cells_x, 0:cells_y]


OFFSETS = ((1, 0), (-1, 0), (0, 1), (0, -1), (1, 1), (1, -1), (-1, 1), (-1, -1))


def exchange_halos(parts, depth):
    head = slice(0, depth)
    tail = slice(-depth, None)
    t = lambda b: jnp.swapaxes(b, 1, 2)
    outgoing = [
        parts[:, head, :],
        parts[:, tail, :],
        t(parts[:, :, head]),
        t(parts[:, :, tail]),
        t(parts[:, head, head]),
        t(parts[:, head, tail]),
        t(parts[:, tail, head]),
        t(parts[:, tail, tail]),
    ]
    count = len(OFFSETS)

    def kernel(*refs):
        ins = refs[:count]
        outs = refs[count:2 * count]
        send, recv = refs[2 * count:]
        n_tx = lax.axis_size("tx")
        n_ty = lax.axis_size("ty")
        me_x = lax.axis_index("tx")
        me_y = lax.axis_index("ty")
        targets = [
            {"tx": lax.rem(me_x - dx + n_tx, n_tx), "ty": lax.rem(me_y - dy + n_ty, n_ty)}
            for dx, dy in OFFSETS
        ]
        barrier = pltpu.get_barrier_semaphore()
        for target in targets:
            pl.semaphore_signal(barrier, 1, device_id=target, device_id_type=MESH)
        pl.semaphore_wait(barrier, count)
        copies = []
        for k in range(count):
            copy = pltpu.make_async_remote_copy(
                src_ref=ins[k], dst_ref=outs[k], send_sem=send.at[k], recv_sem=recv.at[k],
                device_id=targets[k], device_id_type=MESH,
            )
            copy.start()
            copies.append(copy)
        for copy in copies:
            copy.wait()

    shapes = [p.shape for p in outgoing]
    outgoing = [lane_dense(p) for p in outgoing]
    got = pl.pallas_call(
        kernel,
        out_shape=tuple(jax.ShapeDtypeStruct(p.shape, p.dtype) for p in outgoing),
        in_specs=[VMEM_SPEC] * count,
        out_specs=tuple([VMEM_SPEC] * count),
        scratch_shapes=[pltpu.SemaphoreType.DMA((count,)), pltpu.SemaphoreType.DMA((count,))],
        compiler_params=pltpu.CompilerParams(collective_id=3, has_side_effects=True),
    )(*outgoing)
    got = [g.reshape(-1)[:math.prod(s)].reshape(s) for g, s in zip(got, shapes)]
    xa, xb, ya, yb, aa, ab, ba, bb = got
    y_ahead = jnp.concatenate([ya, aa, ba], 2)
    y_behind = jnp.concatenate([yb, ab, bb], 2)
    return xa, xb, jnp.concatenate([y_ahead, y_behind], 1)


def per_device(orders, offsets, material, e_field, h_field):
    layers, cells_x, cells_y = material.shape
    plane = injection_plane(orders, offsets, cells_x, cells_y)
    coefficient = cell_coefficient(material)
    parts = jnp.concatenate(
        [
            e_field.reshape(3 * layers, cells_x, cells_y),
            h_field.reshape(3 * layers, cells_x, cells_y),
            coefficient,
            plane,
        ],
        0,
    )
    depth = STEPS
    xa, xb, yh = exchange_halos(parts, depth)
    rows = cells_x + 2 * depth
    lanes = 2 * cells_y
    vmem = pltpu.MemorySpace.VMEM
    spec = pl.BlockSpec(memory_space=vmem)
    out = jax.ShapeDtypeStruct(e_field.shape, jnp.float32)
    return pl.pallas_call(
        yee_kernel,
        out_shape=(out, out),
        in_specs=[spec] * 7,
        out_specs=(spec, spec),
        scratch_shapes=[
            pltpu.VMEM((6 * (layers + 2), rows, lanes), jnp.float32),
            pltpu.VMEM((layers + 2, rows, lanes), jnp.float32),
            pltpu.VMEM((rows, cells_y), jnp.float32),
        ],
        compiler_params=pltpu.CompilerParams(vmem_limit_bytes=64 * 1024 * 1024),
    )(e_field, h_field, coefficient, plane, xa, xb, yh)


def solution(mesh):
    in_specs = (
        P("src", None, "tx", "ty"),
        P("src", None),
        P(None, "tx", "ty"),
        P(None, None, "tx", "ty"),
        P(None, None, "tx", "ty"),
    )
    out_specs = (P(None, None, "tx", "ty"), P(None, None, "tx", "ty"))
    return jax.shard_map(
        per_device, mesh=mesh, in_specs=in_specs, out_specs=out_specs, check_vma=False
    )
```

```python
import math

import jax
import jax.numpy as jnp
from jax import lax
from jax.sharding import PartitionSpec as P
from jax.experimental import pallas as pl
from jax.experimental.pallas import tpu as pltpu

STEPS = 4
ZINJ = 1


COURANT = 0.5
OMEGA = 0.7
PERMITTIVITY = (1.0, 2.6, 11.9, 2.1)
PREC = lax.Precision.HIGH
SHIFT = 8
HALO = 8


def phase_tables(freqs, positions, length):
    product = jnp.mod(freqs[:, None] * positions[None, :], length)
    angle = product.astype(jnp.float32) * (2.0 * math.pi / length)
    return (jnp.cos(angle), jnp.sin(angle))


def cell_coefficient(material):
    total = jnp.zeros(material.shape, jnp.float32)
    for number in range(len(PERMITTIVITY)):
        total = total + jnp.where(material == number, COURANT / PERMITTIVITY[number], 0.0)
    return total


MESH = pl.DeviceIdType.MESH
VMEM_SPEC = pl.BlockSpec(memory_space=pltpu.MemorySpace.VMEM)


def gather_along(block, axes, collective):
    sizes = [lax.axis_size(a) for a in axes]
    n = 1
    for s in sizes:
        n *= s

    def coords(linear):
        out = {}
        for a, s in reversed(list(zip(axes, sizes))):
            out[a] = lax.rem(linear, s)
            linear = linear // s
        return out

    def kernel(x_ref, o_ref, send, recv, local):
        me = 0
        for a, s in zip(axes, sizes):
            me = me * s + lax.axis_index(a)
        barrier = pltpu.get_barrier_semaphore()
        for k in range(1, n):
            pl.semaphore_signal(barrier, 1, device_id=coords(lax.rem(me + k, n)), device_id_type=MESH)
        pl.semaphore_wait(barrier, n - 1)
        own = pltpu.make_async_copy(x_ref, o_ref.at[me], local.at[0])
        own.start()
        copies = []
        for k in range(1, n):
            copy = pltpu.make_async_remote_copy(
                src_ref=x_ref,
                dst_ref=o_ref.at[me],
                send_sem=send.at[k - 1],
                recv_sem=recv.at[k - 1],
                device_id=coords(lax.rem(me + k, n)),
                device_id_type=MESH,
            )
            copy.start()
            copies.append(copy)
        own.wait()
        for copy in copies:
            copy.wait()

    return pl.pallas_call(
        kernel,
        out_shape=jax.ShapeDtypeStruct((n,) + block.shape, block.dtype),
        in_specs=[VMEM_SPEC],
        out_specs=VMEM_SPEC,
        scratch_shapes=[
            pltpu.SemaphoreType.DMA((n - 1,)),
            pltpu.SemaphoreType.DMA((n - 1,)),
            pltpu.SemaphoreType.DMA((1,)),
        ],
        compiler_params=pltpu.CompilerParams(collective_id=collective, has_side_effects=True),
    )(block)


def chunk_tables(step, span, count, base, positions, length):
    c1, s1 = phase_tables(jnp.arange(count, dtype=jnp.int32) * step, positions, length)
    c2, s2 = phase_tables(jnp.arange(span, dtype=jnp.int32) - base, positions, length)
    cos_t = c1[:, None, :] * c2[None, :, :] - s1[:, None, :] * s2[None, :, :]
    sin_t = s1[:, None, :] * c2[None, :, :] + c1[:, None, :] * s2[None, :, :]
    return cos_t, sin_t


def lane_dense(block):
    flat = block.reshape(-1)
    pad = (-flat.shape[0]) % 1024
    return jnp.pad(flat, (0, pad)).reshape(-1, 128)


def injection_plane(orders, offsets, cells_x, cells_y):
    points, _, rows_kx, cols_ky = orders.shape
    n_src = lax.axis_size("src")
    n_tx = lax.axis_size("tx")
    n_ty = lax.axis_size("ty")
    full_x = cells_x * n_tx
    full_y = cells_y * n_ty
    mx = rows_kx * n_tx
    my = cols_ky * n_ty
    span_x = rows_kx + 2 * SHIFT
    span_y = cols_ky + 2 * SHIFT
    lift_x = (
        lax.broadcasted_iota(jnp.int32, (points, span_x, rows_kx), 1)
        == lax.broadcasted_iota(jnp.int32, (points, span_x, rows_kx), 2) + offsets[:, 0:1, None] + SHIFT
    ).astype(jnp.float32)
    lift_y = (
        lax.broadcasted_iota(jnp.int32, (points, span_y, cols_ky), 1)
        == lax.broadcasted_iota(jnp.int32, (points, span_y, cols_ky), 2) + offsets[:, 1:2, None] + SHIFT
    ).astype(jnp.float32)
    exact = lax.Precision.HIGHEST
    placed = jnp.einsum("puk,prkj->pruj", lift_x, orders, precision=exact)
    merged = jnp.einsum("pruj,pvj->ruv", placed, lift_y, precision=exact)
    size = merged.size
    got = gather_along(lane_dense(merged), ("src", "ty"), 0)
    got = got.reshape(n_src * n_ty, -1)[:, :size].reshape(n_src, n_ty, 2, span_x, span_y)
    got = jnp.sum(got, 0)
    g_re = got[:, 0]
    g_im = got[:, 1]
    y_pos = lax.axis_index("ty") * cells_y + jnp.arange(cells_y, dtype=jnp.int32)
    by_c, by_s = chunk_tables(cols_ky, span_y, n_ty, my // 2 + SHIFT, y_pos, full_y)
    i_re = jnp.einsum("cuv,cvy->uy", g_re, by_c, precision=PREC) - jnp.einsum(
        "cuv,cvy->uy", g_im, by_s, precision=PREC
    )
    i_im = jnp.einsum("cuv,cvy->uy", g_re, by_s, precision=PREC) + jnp.einsum(
        "cuv,cvy->uy", g_im, by_c, precision=PREC
    )
    inner = gather_along(jnp.stack([i_re, i_im]), ("tx",), 1)
    i_re = inner[:, 0]
    i_im = inner[:, 1]
    x_pos = lax.axis_index("tx") * cells_x + jnp.arange(cells_x, dtype=jnp.int32)
    bx_c, bx_s = chunk_tables(rows_kx, span_x, n_tx, mx // 2 + SHIFT, x_pos, full_x)
    p_re = jnp.einsum("cux,cuy->xy", bx_c, i_re, precision=PREC) - jnp.einsum(
        "cux,cuy->xy", bx_s, i_im, precision=PREC
    )
    p_im = jnp.einsum("cux,cuy->xy", bx_c, i_im, precision=PREC) + jnp.einsum(
        "cux,cuy->xy", bx_s, i_re, precision=PREC
    )
    return jnp.stack([p_re, p_im])


def yee_kernel(e_ref, h_ref, coef_ref, plane_ref, eo_ref, ho_ref,
               ext, cp, tmp, srow, rrow, scol, rcol, send, recv):
    layers, cells_x, cells_y = coef_ref.shape
    depth = srow.shape[2]
    rows = cells_x + 2 * depth
    lanes = ext.shape[2]
    slab = layers + 2
    n_field = 6 * layers
    n_parts = n_field + layers + 2
    n_tx = lax.axis_size("tx")
    n_ty = lax.axis_size("ty")
    me_x = lax.axis_index("tx")
    me_y = lax.axis_index("ty")
    x_lo = {"tx": lax.rem(me_x + n_tx - 1, n_tx)}
    x_hi = {"tx": lax.rem(me_x + 1, n_tx)}
    y_lo = {"ty": lax.rem(me_y + n_ty - 1, n_ty)}
    y_hi = {"ty": lax.rem(me_y + 1, n_ty)}

    barrier = pltpu.get_barrier_semaphore()
    for peer in (x_lo, x_hi, y_lo, y_hi):
        pl.semaphore_signal(barrier, 1, device_id=peer, device_id_type=MESH)
    pl.semaphore_wait(barrier, 4)

    def own_part(h):
        comp = h // layers
        z = h % layers
        return jnp.where(comp < 3, e_ref[comp % 3, z], h_ref[comp % 3, z])

    def field_slot(h):
        return (h // layers) * slab + h % layers + 1

    def fill_rows(h, carry):
        part = own_part(h)
        srow[0, h] = part[0:depth]
        srow[1, h] = part[cells_x - depth:cells_x]
        ext[field_slot(h), 0:cells_x, 0:cells_y] = part
        return carry

    lax.fori_loop(0, n_field, fill_rows, 0)
    for k in range(layers + 2):
        part = coef_ref[k] if k < layers else plane_ref[k - layers]
        srow[0, n_field + k] = part[0:depth]
        srow[1, n_field + k] = part[cells_x - depth:cells_x]
        cp[k, 0:cells_x, 0:cells_y] = part
    row_copies = [
        pltpu.make_async_remote_copy(
            src_ref=srow.at[0], dst_ref=rrow.at[0], send_sem=send.at[0], recv_sem=recv.at[0],
            device_id=x_lo, device_id_type=MESH,
        ),
        pltpu.make_async_remote_copy(
            src_ref=srow.at[1], dst_ref=rrow.at[1], send_sem=send.at[1], recv_sem=recv.at[1],
            device_id=x_hi, device_id_type=MESH,
        ),
    ]
    for copy in row_copies:
        copy.start()
    zero = jnp.zeros((rows, lanes), jnp.float32)
    for comp in range(3):
        ext[comp * slab + slab - 1] = zero
        ext[(3 + comp) * slab] = zero
    tmp[...] = jnp.zeros_like(tmp)
    for copy in row_copies:
        copy.wait()

    def fill_cols(dst, idx, h):
        dst[idx, cells_x:cells_x + depth, 0:cells_y] = rrow[0, h]
        dst[idx, cells_x + depth:rows, 0:cells_y] = rrow[1, h]
        t = dst[idx, :, 0:cells_y].T
        scol[0, h] = t[0:depth]
        scol[1, h] = t[cells_y - depth:cells_y]

    def cols_fields(h, carry):
        fill_cols(ext, field_slot(h), h)
        return carry

    lax.fori_loop(0, n_field, cols_fields, 0)
    for k in range(layers + 2):
        fill_cols(cp, k, n_field + k)
    col_copies = [
        pltpu.make_async_remote_copy(
            src_ref=scol.at[0], dst_ref=rcol.at[0], send_sem=send.at[2], recv_sem=recv.at[2],
            device_id=y_lo, device_id_type=MESH,
        ),
        pltpu.make_async_remote_copy(
            src_ref=scol.at[1], dst_ref=rcol.at[1], send_sem=send.at[3], recv_sem=recv.at[3],
            device_id=y_hi, device_id_type=MESH,
        ),
    ]
    for copy in col_copies:
        copy.start()
    for copy in col_copies:
        copy.wait()
    lane = lax.broadcasted_iota(jnp.int32, (rows, cells_y), 1)

    def place_cols(dst, idx, h):
        v = jnp.concatenate([rcol[0, h], rcol[1, h]], 0)
        tmp[:, 0:2 * depth] = v.T
        w = tmp[...]
        front = jnp.where(lane < depth, w, 0.0)
        back = jnp.where(lane >= depth, w, 0.0)
        dst[idx, :, cells_y:lanes] = front + pltpu.roll(back, cells_y - 2 * depth, 1)

    def place_fields(h, carry):
        place_cols(ext, field_slot(h), h)
        return carry

    lax.fori_loop(0, n_field, place_fields, 0)
    for k in range(layers + 2):
        place_cols(cp, k, n_field + k)

    ahead_x = lambda f: pltpu.roll(f, rows - 1, 0)
    ahead_y = lambda f: pltpu.roll(f, lanes - 1, 1)
    behind_x = lambda f: pltpu.roll(f, 1, 0)
    behind_y = lambda f: pltpu.roll(f, 1, 1)
    ex_, ey_, ez_, hx_, hy_, hz_ = (c * slab for c in range(6))

    for step in range(STEPS):
        def h_update(z, carry):
            s = z + 1
            e_x = ext[ex_ + s]
            e_y = ext[ey_ + s]
            e_z = ext[ez_ + s]
            ext[hx_ + s] = ext[hx_ + s] - COURANT * ((ahead_y(e_z) - e_z) - (ext[ey_ + s + 1] - e_y))
            ext[hy_ + s] = ext[hy_ + s] - COURANT * ((ext[ex_ + s + 1] - e_x) - (ahead_x(e_z) - e_z))
            ext[hz_ + s] = ext[hz_ + s] - COURANT * ((ahead_x(e_y) - e_y) - (ahead_y(e_x) - e_x))
            return carry

        def e_update(z, carry):
            s = z + 1
            h_x = ext[hx_ + s]
            h_y = ext[hy_ + s]
            h_z = ext[hz_ + s]
            c = cp[z]
            ext[ex_ + s] = ext[ex_ + s] + c * ((h_z - behind_y(h_z)) - (h_y - ext[hy_ + s - 1]))
            ext[ey_ + s] = ext[ey_ + s] + c * ((h_x - ext[hx_ + s - 1]) - (h_z - behind_x(h_z)))
            ext[ez_ + s] = ext[ez_ + s] + c * ((h_y - behind_x(h_y)) - (h_x - behind_y(h_x)))
            return carry

        lax.fori_loop(0, layers, h_update, 0)
        lax.fori_loop(0, layers, e_update, 0)
        cosine = math.cos(OMEGA * (step + 1))
        sine = math.sin(OMEGA * (step + 1))
        p_re = cp[layers]
        p_im = cp[layers + 1]
        s = ZINJ + 1
        ext[ex_ + s] = ext[ex_ + s] + COURANT * (cosine * p_re - sine * p_im)
        ext[ey_ + s] = ext[ey_ + s] + COURANT * (sine * p_re + cosine * p_im)

    for comp in range(3):
        for z in range(layers):
            eo_ref[comp, z] = ext[comp * slab + z + 1, 0:cells_x, 0:cells_y]
            ho_ref[comp, z] = ext[(3 + comp) * slab + z + 1, 0:cells_x, 0:cells_y]


def per_device(orders, offsets, material, e_field, h_field):
    layers, cells_x, cells_y = material.shape
    plane = injection_plane(orders, offsets, cells_x, cells_y)
    coefficient = cell_coefficient(material)
    depth = HALO
    rows = cells_x + 2 * depth
    lanes = 2 * cells_y
    n_parts = 6 * layers + layers + 2
    out = jax.ShapeDtypeStruct(e_field.shape, jnp.float32)
    return pl.pallas_call(
        yee_kernel,
        out_shape=(out, out),
        in_specs=[VMEM_SPEC] * 4,
        out_specs=(VMEM_SPEC, VMEM_SPEC),
        scratch_shapes=[
            pltpu.VMEM((6 * (layers + 2), rows, lanes), jnp.float32),
            pltpu.VMEM((layers + 2, rows, lanes), jnp.float32),
            pltpu.VMEM((rows, cells_y), jnp.float32),
            pltpu.VMEM((2, n_parts, depth, cells_y), jnp.float32),
            pltpu.VMEM((2, n_parts, depth, cells_y), jnp.float32),
            pltpu.VMEM((2, n_parts, depth, rows), jnp.float32),
            pltpu.VMEM((2, n_parts, depth, rows), jnp.float32),
            pltpu.SemaphoreType.DMA((4,)),
            pltpu.SemaphoreType.DMA((4,)),
        ],
        compiler_params=pltpu.CompilerParams(
            collective_id=3, has_side_effects=True, vmem_limit_bytes=64 * 1024 * 1024
        ),
    )(e_field, h_field, coefficient, plane)


def solution(mesh):
    in_specs = (
        P("src", None, "tx", "ty"),
        P("src", None),
        P(None, "tx", "ty"),
        P(None, None, "tx", "ty"),
        P(None, None, "tx", "ty"),
    )
    out_specs = (P(None, None, "tx", "ty"), P(None, None, "tx", "ty"))
    return jax.shard_map(
        per_device, mesh=mesh, in_specs=in_specs, out_specs=out_specs, check_vma=False
    )
```

```python
import math

import jax
import jax.numpy as jnp
from jax import lax
from jax.sharding import PartitionSpec as P
from jax.experimental import pallas as pl
from jax.experimental.pallas import tpu as pltpu

STEPS = 4
ZINJ = 1


COURANT = 0.5
OMEGA = 0.7
PERMITTIVITY = (1.0, 2.6, 11.9, 2.1)
PREC = lax.Precision.HIGH
SHIFT = 8
HALO = 8


def phase_tables(freqs, positions, length):
    product = jnp.mod(freqs[:, None] * positions[None, :], length)
    angle = product.astype(jnp.float32) * (2.0 * math.pi / length)
    return (jnp.cos(angle), jnp.sin(angle))


def cell_coefficient(material):
    total = jnp.zeros(material.shape, jnp.float32)
    for number in range(len(PERMITTIVITY)):
        total = total + jnp.where(material == number, COURANT / PERMITTIVITY[number], 0.0)
    return total


MESH = pl.DeviceIdType.MESH
VMEM_SPEC = pl.BlockSpec(memory_space=pltpu.MemorySpace.VMEM)


def gather_along(block, axes, collective):
    sizes = [lax.axis_size(a) for a in axes]
    n = 1
    for s in sizes:
        n *= s

    def coords(linear):
        out = {}
        for a, s in reversed(list(zip(axes, sizes))):
            out[a] = lax.rem(linear, s)
            linear = linear // s
        return out

    def kernel(x_ref, o_ref, send, recv, local):
        me = 0
        for a, s in zip(axes, sizes):
            me = me * s + lax.axis_index(a)
        barrier = pltpu.get_barrier_semaphore()
        for k in range(1, n):
            pl.semaphore_signal(barrier, 1, device_id=coords(lax.rem(me + k, n)), device_id_type=MESH)
        pl.semaphore_wait(barrier, n - 1)
        own = pltpu.make_async_copy(x_ref, o_ref.at[me], local.at[0])
        own.start()
        copies = []
        for k in range(1, n):
            copy = pltpu.make_async_remote_copy(
                src_ref=x_ref,
                dst_ref=o_ref.at[me],
                send_sem=send.at[k - 1],
                recv_sem=recv.at[k - 1],
                device_id=coords(lax.rem(me + k, n)),
                device_id_type=MESH,
            )
            copy.start()
            copies.append(copy)
        own.wait()
        for copy in copies:
            copy.wait()

    return pl.pallas_call(
        kernel,
        out_shape=jax.ShapeDtypeStruct((n,) + block.shape, block.dtype),
        in_specs=[VMEM_SPEC],
        out_specs=VMEM_SPEC,
        scratch_shapes=[
            pltpu.SemaphoreType.DMA((n - 1,)),
            pltpu.SemaphoreType.DMA((n - 1,)),
            pltpu.SemaphoreType.DMA((1,)),
        ],
        compiler_params=pltpu.CompilerParams(collective_id=collective, has_side_effects=True),
    )(block)


def summed_over_pair(block, axis, collective):
    def kernel(x_ref, o_ref, got, send, recv):
        other = {axis: 1 - lax.axis_index(axis)}
        barrier = pltpu.get_barrier_semaphore()
        pl.semaphore_signal(barrier, 1, device_id=other, device_id_type=MESH)
        pl.semaphore_wait(barrier, 1)
        copy = pltpu.make_async_remote_copy(
            src_ref=x_ref, dst_ref=got, send_sem=send.at[0], recv_sem=recv.at[0],
            device_id=other, device_id_type=MESH,
        )
        copy.start()
        copy.wait()
        o_ref[...] = x_ref[...] + got[...]

    return pl.pallas_call(
        kernel,
        out_shape=jax.ShapeDtypeStruct(block.shape, block.dtype),
        in_specs=[VMEM_SPEC],
        out_specs=VMEM_SPEC,
        scratch_shapes=[
            pltpu.VMEM(block.shape, block.dtype),
            pltpu.SemaphoreType.DMA((1,)),
            pltpu.SemaphoreType.DMA((1,)),
        ],
        compiler_params=pltpu.CompilerParams(collective_id=collective, has_side_effects=True),
    )(block)


def chunk_tables(step, span, count, base, positions, length):
    c1, s1 = phase_tables(jnp.arange(count, dtype=jnp.int32) * step, positions, length)
    c2, s2 = phase_tables(jnp.arange(span, dtype=jnp.int32) - base, positions, length)
    cos_t = c1[:, None, :] * c2[None, :, :] - s1[:, None, :] * s2[None, :, :]
    sin_t = s1[:, None, :] * c2[None, :, :] + c1[:, None, :] * s2[None, :, :]
    return cos_t, sin_t


def lane_dense(block):
    flat = block.reshape(-1)
    pad = (-flat.shape[0]) % 1024
    return jnp.pad(flat, (0, pad)).reshape(-1, 128)


def injection_plane(orders, offsets, cells_x, cells_y):
    points, _, rows_kx, cols_ky = orders.shape
    n_src = lax.axis_size("src")
    n_tx = lax.axis_size("tx")
    n_ty = lax.axis_size("ty")
    full_x = cells_x * n_tx
    full_y = cells_y * n_ty
    mx = rows_kx * n_tx
    my = cols_ky * n_ty
    span_x = rows_kx + 2 * SHIFT
    span_y = cols_ky + 2 * SHIFT
    lift_x = (
        lax.broadcasted_iota(jnp.int32, (points, span_x, rows_kx), 1)
        == lax.broadcasted_iota(jnp.int32, (points, span_x, rows_kx), 2) + offsets[:, 0:1, None] + SHIFT
    ).astype(jnp.float32)
    lift_y = (
        lax.broadcasted_iota(jnp.int32, (points, span_y, cols_ky), 1)
        == lax.broadcasted_iota(jnp.int32, (points, span_y, cols_ky), 2) + offsets[:, 1:2, None] + SHIFT
    ).astype(jnp.float32)
    exact = lax.Precision.HIGHEST
    placed = jnp.einsum("puk,prkj->pruj", lift_x, orders, precision=exact)
    merged = jnp.einsum("pruj,pvj->ruv", placed, lift_y, precision=exact)
    size = merged.size
    merged = summed_over_pair(lane_dense(merged), "src", 2)
    got = gather_along(merged, ("ty",), 0)
    got = got.reshape(n_ty, -1)[:, :size].reshape(n_ty, 2, span_x, span_y)
    g_re = got[:, 0]
    g_im = got[:, 1]
    y_pos = lax.axis_index("ty") * cells_y + jnp.arange(cells_y, dtype=jnp.int32)
    by_c, by_s = chunk_tables(cols_ky, span_y, n_ty, my // 2 + SHIFT, y_pos, full_y)
    i_re = jnp.einsum("cuv,cvy->uy", g_re, by_c, precision=PREC) - jnp.einsum(
        "cuv,cvy->uy", g_im, by_s, precision=PREC
    )
    i_im = jnp.einsum("cuv,cvy->uy", g_re, by_s, precision=PREC) + jnp.einsum(
        "cuv,cvy->uy", g_im, by_c, precision=PREC
    )
    inner = gather_along(jnp.stack([i_re, i_im]), ("tx",), 1)
    i_re = inner[:, 0]
    i_im = inner[:, 1]
    x_pos = lax.axis_index("tx") * cells_x + jnp.arange(cells_x, dtype=jnp.int32)
    bx_c, bx_s = chunk_tables(rows_kx, span_x, n_tx, mx // 2 + SHIFT, x_pos, full_x)
    p_re = jnp.einsum("cux,cuy->xy", bx_c, i_re, precision=PREC) - jnp.einsum(
        "cux,cuy->xy", bx_s, i_im, precision=PREC
    )
    p_im = jnp.einsum("cux,cuy->xy", bx_c, i_im, precision=PREC) + jnp.einsum(
        "cux,cuy->xy", bx_s, i_re, precision=PREC
    )
    return jnp.stack([p_re, p_im])


def yee_kernel(e_ref, h_ref, coef_ref, plane_ref, eo_ref, ho_ref,
               ext, cp, tmp, srow, rrow, scol, rcol, send, recv):
    layers, cells_x, cells_y = coef_ref.shape
    depth = srow.shape[2]
    rows = cells_x + 2 * depth
    lanes = ext.shape[2]
    slab = layers + 2
    n_field = 6 * layers
    n_parts = n_field + layers + 2
    n_tx = lax.axis_size("tx")
    n_ty = lax.axis_size("ty")
    me_x = lax.axis_index("tx")
    me_y = lax.axis_index("ty")
    x_lo = {"tx": lax.rem(me_x + n_tx - 1, n_tx)}
    x_hi = {"tx": lax.rem(me_x + 1, n_tx)}
    y_lo = {"ty": lax.rem(me_y + n_ty - 1, n_ty)}
    y_hi = {"ty": lax.rem(me_y + 1, n_ty)}

    barrier = pltpu.get_barrier_semaphore()
    for peer in (x_lo, x_hi, y_lo, y_hi):
        pl.semaphore_signal(barrier, 1, device_id=peer, device_id_type=MESH)
    pl.semaphore_wait(barrier, 4)

    def own_part(h):
        comp = h // layers
        z = h % layers
        return jnp.where(comp < 3, e_ref[comp % 3, z], h_ref[comp % 3, z])

    def field_slot(h):
        return (h // layers) * slab + h % layers + 1

    def fill_rows(h, carry):
        part = own_part(h)
        srow[0, h] = part[0:depth]
        srow[1, h] = part[cells_x - depth:cells_x]
        ext[field_slot(h), 0:cells_x, 0:cells_y] = part
        return carry

    lax.fori_loop(0, n_field, fill_rows, 0)
    for k in range(layers + 2):
        part = coef_ref[k] if k < layers else plane_ref[k - layers]
        srow[0, n_field + k] = part[0:depth]
        srow[1, n_field + k] = part[cells_x - depth:cells_x]
        cp[k, 0:cells_x, 0:cells_y] = part
    row_copies = [
        pltpu.make_async_remote_copy(
            src_ref=srow.at[0], dst_ref=rrow.at[0], send_sem=send.at[0], recv_sem=recv.at[0],
            device_id=x_lo, device_id_type=MESH,
        ),
        pltpu.make_async_remote_copy(
            src_ref=srow.at[1], dst_ref=rrow.at[1], send_sem=send.at[1], recv_sem=recv.at[1],
            device_id=x_hi, device_id_type=MESH,
        ),
    ]
    for copy in row_copies:
        copy.start()
    zero = jnp.zeros((rows, lanes), jnp.float32)
    for comp in range(3):
        ext[comp * slab + slab - 1] = zero
        ext[(3 + comp) * slab] = zero
    tmp[...] = jnp.zeros_like(tmp)
    for copy in row_copies:
        copy.wait()

    def fill_cols(dst, idx, h):
        dst[idx, cells_x:cells_x + depth, 0:cells_y] = rrow[0, h]
        dst[idx, cells_x + depth:rows, 0:cells_y] = rrow[1, h]
        t = dst[idx, :, 0:cells_y].T
        scol[0, h] = t[0:depth]
        scol[1, h] = t[cells_y - depth:cells_y]

    def cols_fields(h, carry):
        fill_cols(ext, field_slot(h), h)
        return carry

    lax.fori_loop(0, n_field, cols_fields, 0)
    for k in range(layers + 2):
        fill_cols(cp, k, n_field + k)
    col_copies = [
        pltpu.make_async_remote_copy(
            src_ref=scol.at[0], dst_ref=rcol.at[0], send_sem=send.at[2], recv_sem=recv.at[2],
            device_id=y_lo, device_id_type=MESH,
        ),
        pltpu.make_async_remote_copy(
            src_ref=scol.at[1], dst_ref=rcol.at[1], send_sem=send.at[3], recv_sem=recv.at[3],
            device_id=y_hi, device_id_type=MESH,
        ),
    ]
    for copy in col_copies:
        copy.start()
    for copy in col_copies:
        copy.wait()
    lane = lax.broadcasted_iota(jnp.int32, (rows, cells_y), 1)

    def place_cols(dst, idx, h):
        v = jnp.concatenate([rcol[0, h], rcol[1, h]], 0)
        tmp[:, 0:2 * depth] = v.T
        w = tmp[...]
        front = jnp.where(lane < depth, w, 0.0)
        back = jnp.where(lane >= depth, w, 0.0)
        dst[idx, :, cells_y:lanes] = front + pltpu.roll(back, cells_y - 2 * depth, 1)

    def place_fields(h, carry):
        place_cols(ext, field_slot(h), h)
        return carry

    lax.fori_loop(0, n_field, place_fields, 0)
    for k in range(layers + 2):
        place_cols(cp, k, n_field + k)

    ahead_x = lambda f: pltpu.roll(f, rows - 1, 0)
    ahead_y = lambda f: pltpu.roll(f, lanes - 1, 1)
    behind_x = lambda f: pltpu.roll(f, 1, 0)
    behind_y = lambda f: pltpu.roll(f, 1, 1)
    ex_, ey_, ez_, hx_, hy_, hz_ = (c * slab for c in range(6))

    for step in range(STEPS):
        def h_update(z, carry):
            s = z + 1
            e_x = ext[ex_ + s]
            e_y = ext[ey_ + s]
            e_z = ext[ez_ + s]
            ext[hx_ + s] = ext[hx_ + s] - COURANT * ((ahead_y(e_z) - e_z) - (ext[ey_ + s + 1] - e_y))
            ext[hy_ + s] = ext[hy_ + s] - COURANT * ((ext[ex_ + s + 1] - e_x) - (ahead_x(e_z) - e_z))
            ext[hz_ + s] = ext[hz_ + s] - COURANT * ((ahead_x(e_y) - e_y) - (ahead_y(e_x) - e_x))
            return carry

        def e_update(z, carry):
            s = z + 1
            h_x = ext[hx_ + s]
            h_y = ext[hy_ + s]
            h_z = ext[hz_ + s]
            c = cp[z]
            ext[ex_ + s] = ext[ex_ + s] + c * ((h_z - behind_y(h_z)) - (h_y - ext[hy_ + s - 1]))
            ext[ey_ + s] = ext[ey_ + s] + c * ((h_x - ext[hx_ + s - 1]) - (h_z - behind_x(h_z)))
            ext[ez_ + s] = ext[ez_ + s] + c * ((h_y - behind_x(h_y)) - (h_x - behind_y(h_x)))
            return carry

        lax.fori_loop(0, layers, h_update, 0)
        lax.fori_loop(0, layers, e_update, 0)
        cosine = math.cos(OMEGA * (step + 1))
        sine = math.sin(OMEGA * (step + 1))
        p_re = cp[layers]
        p_im = cp[layers + 1]
        s = ZINJ + 1
        ext[ex_ + s] = ext[ex_ + s] + COURANT * (cosine * p_re - sine * p_im)
        ext[ey_ + s] = ext[ey_ + s] + COURANT * (sine * p_re + cosine * p_im)

    for comp in range(3):
        for z in range(layers):
            eo_ref[comp, z] = ext[comp * slab + z + 1, 0:cells_x, 0:cells_y]
            ho_ref[comp, z] = ext[(3 + comp) * slab + z + 1, 0:cells_x, 0:cells_y]


def per_device(orders, offsets, material, e_field, h_field):
    layers, cells_x, cells_y = material.shape
    plane = injection_plane(orders, offsets, cells_x, cells_y)
    coefficient = cell_coefficient(material)
    depth = HALO
    rows = cells_x + 2 * depth
    lanes = 2 * cells_y
    n_parts = 6 * layers + layers + 2
    out = jax.ShapeDtypeStruct(e_field.shape, jnp.float32)
    return pl.pallas_call(
        yee_kernel,
        out_shape=(out, out),
        in_specs=[VMEM_SPEC] * 4,
        out_specs=(VMEM_SPEC, VMEM_SPEC),
        scratch_shapes=[
            pltpu.VMEM((6 * (layers + 2), rows, lanes), jnp.float32),
            pltpu.VMEM((layers + 2, rows, lanes), jnp.float32),
            pltpu.VMEM((rows, cells_y), jnp.float32),
            pltpu.VMEM((2, n_parts, depth, cells_y), jnp.float32),
            pltpu.VMEM((2, n_parts, depth, cells_y), jnp.float32),
            pltpu.VMEM((2, n_parts, depth, rows), jnp.float32),
            pltpu.VMEM((2, n_parts, depth, rows), jnp.float32),
            pltpu.SemaphoreType.DMA((4,)),
            pltpu.SemaphoreType.DMA((4,)),
        ],
        compiler_params=pltpu.CompilerParams(
            collective_id=3, has_side_effects=True, vmem_limit_bytes=64 * 1024 * 1024
        ),
    )(e_field, h_field, coefficient, plane)


def solution(mesh):
    in_specs = (
        P("src", None, "tx", "ty"),
        P("src", None),
        P(None, "tx", "ty"),
        P(None, None, "tx", "ty"),
        P(None, None, "tx", "ty"),
    )
    out_specs = (P(None, None, "tx", "ty"), P(None, None, "tx", "ty"))
    return jax.shard_map(
        per_device, mesh=mesh, in_specs=in_specs, out_specs=out_specs, check_vma=False
    )
```

```python
import math

import jax
import jax.numpy as jnp
from jax import lax
from jax.sharding import PartitionSpec as P
from jax.experimental import pallas as pl
from jax.experimental.pallas import tpu as pltpu

STEPS = 4
ZINJ = 1


COURANT = 0.5
OMEGA = 0.7
PERMITTIVITY = (1.0, 2.6, 11.9, 2.1)
PREC = lax.Precision.HIGH
SHIFT = 8
HALO = 8


def phase_tables(freqs, positions, length):
    product = jnp.mod(freqs[:, None] * positions[None, :], length)
    angle = product.astype(jnp.float32) * (2.0 * math.pi / length)
    return (jnp.cos(angle), jnp.sin(angle))


def cell_coefficient(material):
    total = jnp.zeros(material.shape, jnp.float32)
    for number in range(len(PERMITTIVITY)):
        total = total + jnp.where(material == number, COURANT / PERMITTIVITY[number], 0.0)
    return total


MESH = pl.DeviceIdType.MESH
VMEM_SPEC = pl.BlockSpec(memory_space=pltpu.MemorySpace.VMEM)


def gather_along(block, axes, collective):
    sizes = [lax.axis_size(a) for a in axes]
    n = 1
    for s in sizes:
        n *= s

    def coords(linear):
        out = {}
        for a, s in reversed(list(zip(axes, sizes))):
            out[a] = lax.rem(linear, s)
            linear = linear // s
        return out

    def kernel(x_ref, o_ref, send, recv, local):
        me = 0
        for a, s in zip(axes, sizes):
            me = me * s + lax.axis_index(a)
        barrier = pltpu.get_barrier_semaphore()
        for k in range(1, n):
            pl.semaphore_signal(barrier, 1, device_id=coords(lax.rem(me + k, n)), device_id_type=MESH)
        pl.semaphore_wait(barrier, n - 1)
        own = pltpu.make_async_copy(x_ref, o_ref.at[me], local.at[0])
        own.start()
        copies = []
        for k in range(1, n):
            copy = pltpu.make_async_remote_copy(
                src_ref=x_ref,
                dst_ref=o_ref.at[me],
                send_sem=send.at[k - 1],
                recv_sem=recv.at[k - 1],
                device_id=coords(lax.rem(me + k, n)),
                device_id_type=MESH,
            )
            copy.start()
            copies.append(copy)
        own.wait()
        for copy in copies:
            copy.wait()

    return pl.pallas_call(
        kernel,
        out_shape=jax.ShapeDtypeStruct((n,) + block.shape, block.dtype),
        in_specs=[VMEM_SPEC],
        out_specs=VMEM_SPEC,
        scratch_shapes=[
            pltpu.SemaphoreType.DMA((n - 1,)),
            pltpu.SemaphoreType.DMA((n - 1,)),
            pltpu.SemaphoreType.DMA((1,)),
        ],
        compiler_params=pltpu.CompilerParams(collective_id=collective, has_side_effects=True),
    )(block)


def gather_with_halo(block, e_field, h_field, coefficient, depth, collective):
    n = lax.axis_size("ty")
    layers, cells_x, cells_y = coefficient.shape
    rows = cells_x + 2 * depth
    n_parts = 7 * layers

    def kernel(x_ref, e_ref, h_ref, coef_ref, o_ref, rrow, rcol,
               gsend, grecv, local, srow, scol, tmp, hsend, hrecv):
        me = lax.axis_index("ty")
        n_tx = lax.axis_size("tx")
        me_x = lax.axis_index("tx")
        x_lo = {"tx": lax.rem(me_x + n_tx - 1, n_tx)}
        x_hi = {"tx": lax.rem(me_x + 1, n_tx)}
        y_lo = {"ty": lax.rem(me + n - 1, n)}
        y_hi = {"ty": lax.rem(me + 1, n)}
        barrier = pltpu.get_barrier_semaphore()
        for k in range(1, n):
            pl.semaphore_signal(barrier, 1, device_id={"ty": lax.rem(me + k, n)}, device_id_type=MESH)
        for peer in (x_lo, x_hi):
            pl.semaphore_signal(barrier, 1, device_id=peer, device_id_type=MESH)
        pl.semaphore_wait(barrier, n + 1)
        own = pltpu.make_async_copy(x_ref, o_ref.at[me], local.at[0])
        own.start()
        gathers = []
        for k in range(1, n):
            copy = pltpu.make_async_remote_copy(
                src_ref=x_ref, dst_ref=o_ref.at[me], send_sem=gsend.at[k - 1], recv_sem=grecv.at[k - 1],
                device_id={"ty": lax.rem(me + k, n)}, device_id_type=MESH,
            )
            copy.start()
            gathers.append(copy)

        def part_of(h):
            comp = h // layers
            z = h % layers
            field = jnp.where(comp < 3, e_ref[comp % 3, z], h_ref[comp % 3, z])
            return jnp.where(comp < 6, field, coef_ref[z])

        def fill_rows(h, carry):
            part = part_of(h)
            srow[0, h] = part[0:depth]
            srow[1, h] = part[cells_x - depth:cells_x]
            return carry

        lax.fori_loop(0, n_parts, fill_rows, 0)
        row_copies = [
            pltpu.make_async_remote_copy(
                src_ref=srow.at[0], dst_ref=rrow.at[0], send_sem=hsend.at[0], recv_sem=hrecv.at[0],
                device_id=x_lo, device_id_type=MESH,
            ),
            pltpu.make_async_remote_copy(
                src_ref=srow.at[1], dst_ref=rrow.at[1], send_sem=hsend.at[1], recv_sem=hrecv.at[1],
                device_id=x_hi, device_id_type=MESH,
            ),
        ]
        for copy in row_copies:
            copy.start()
        for copy in row_copies:
            copy.wait()

        def fill_cols(h, carry):
            tmp[0:cells_x] = part_of(h)
            tmp[cells_x:cells_x + depth] = rrow[0, h]
            tmp[cells_x + depth:rows] = rrow[1, h]
            t = tmp[...].T
            scol[0, h] = t[0:depth]
            scol[1, h] = t[cells_y - depth:cells_y]
            return carry

        lax.fori_loop(0, n_parts, fill_cols, 0)
        col_copies = [
            pltpu.make_async_remote_copy(
                src_ref=scol.at[0], dst_ref=rcol.at[0], send_sem=hsend.at[2], recv_sem=hrecv.at[2],
                device_id=y_lo, device_id_type=MESH,
            ),
            pltpu.make_async_remote_copy(
                src_ref=scol.at[1], dst_ref=rcol.at[1], send_sem=hsend.at[3], recv_sem=hrecv.at[3],
                device_id=y_hi, device_id_type=MESH,
            ),
        ]
        for copy in col_copies:
            copy.start()
        for copy in col_copies:
            copy.wait()
        own.wait()
        for copy in gathers:
            copy.wait()

    return pl.pallas_call(
        kernel,
        out_shape=(
            jax.ShapeDtypeStruct((n,) + block.shape, block.dtype),
            jax.ShapeDtypeStruct((2, n_parts, depth, cells_y), jnp.float32),
            jax.ShapeDtypeStruct((2, n_parts, depth, rows), jnp.float32),
        ),
        in_specs=[VMEM_SPEC] * 4,
        out_specs=(VMEM_SPEC, VMEM_SPEC, VMEM_SPEC),
        scratch_shapes=[
            pltpu.SemaphoreType.DMA((n - 1,)),
            pltpu.SemaphoreType.DMA((n - 1,)),
            pltpu.SemaphoreType.DMA((1,)),
            pltpu.VMEM((2, n_parts, depth, cells_y), jnp.float32),
            pltpu.VMEM((2, n_parts, depth, rows), jnp.float32),
            pltpu.VMEM((rows, cells_y), jnp.float32),
            pltpu.SemaphoreType.DMA((4,)),
            pltpu.SemaphoreType.DMA((4,)),
        ],
        compiler_params=pltpu.CompilerParams(
            collective_id=collective, has_side_effects=True, vmem_limit_bytes=64 * 1024 * 1024
        ),
    )(block, e_field, h_field, coefficient)


def summed_over_pair(block, axis, collective):
    def kernel(x_ref, o_ref, got, send, recv):
        other = {axis: 1 - lax.axis_index(axis)}
        barrier = pltpu.get_barrier_semaphore()
        pl.semaphore_signal(barrier, 1, device_id=other, device_id_type=MESH)
        pl.semaphore_wait(barrier, 1)
        copy = pltpu.make_async_remote_copy(
            src_ref=x_ref, dst_ref=got, send_sem=send.at[0], recv_sem=recv.at[0],
            device_id=other, device_id_type=MESH,
        )
        copy.start()
        copy.wait()
        o_ref[...] = x_ref[...] + got[...]

    return pl.pallas_call(
        kernel,
        out_shape=jax.ShapeDtypeStruct(block.shape, block.dtype),
        in_specs=[VMEM_SPEC],
        out_specs=VMEM_SPEC,
        scratch_shapes=[
            pltpu.VMEM(block.shape, block.dtype),
            pltpu.SemaphoreType.DMA((1,)),
            pltpu.SemaphoreType.DMA((1,)),
        ],
        compiler_params=pltpu.CompilerParams(collective_id=collective, has_side_effects=True),
    )(block)


def chunk_tables(step, span, count, base, positions, length):
    c1, s1 = phase_tables(jnp.arange(count, dtype=jnp.int32) * step, positions, length)
    c2, s2 = phase_tables(jnp.arange(span, dtype=jnp.int32) - base, positions, length)
    cos_t = c1[:, None, :] * c2[None, :, :] - s1[:, None, :] * s2[None, :, :]
    sin_t = s1[:, None, :] * c2[None, :, :] + c1[:, None, :] * s2[None, :, :]
    return cos_t, sin_t


def lane_dense(block):
    flat = block.reshape(-1)
    pad = (-flat.shape[0]) % 1024
    return jnp.pad(flat, (0, pad)).reshape(-1, 128)


def injection_plane(orders, offsets, e_field, h_field, coefficient):
    layers, cells_x, cells_y = coefficient.shape
    points, _, rows_kx, cols_ky = orders.shape
    n_src = lax.axis_size("src")
    n_tx = lax.axis_size("tx")
    n_ty = lax.axis_size("ty")
    full_x = cells_x * n_tx
    full_y = cells_y * n_ty
    mx = rows_kx * n_tx
    my = cols_ky * n_ty
    span_x = rows_kx + 2 * SHIFT
    span_y = cols_ky + 2 * SHIFT
    lift_x = (
        lax.broadcasted_iota(jnp.int32, (points, span_x, rows_kx), 1)
        == lax.broadcasted_iota(jnp.int32, (points, span_x, rows_kx), 2) + offsets[:, 0:1, None] + SHIFT
    ).astype(jnp.float32)
    lift_y = (
        lax.broadcasted_iota(jnp.int32, (points, span_y, cols_ky), 1)
        == lax.broadcasted_iota(jnp.int32, (points, span_y, cols_ky), 2) + offsets[:, 1:2, None] + SHIFT
    ).astype(jnp.float32)
    exact = lax.Precision.HIGHEST
    placed = jnp.einsum("puk,prkj->pruj", lift_x, orders, precision=exact)
    merged = jnp.einsum("pruj,pvj->ruv", placed, lift_y, precision=exact)
    size = merged.size
    merged = summed_over_pair(lane_dense(merged), "src", 2)
    got, frow, fcol = gather_with_halo(merged, e_field, h_field, coefficient, HALO, 0)
    got = got.reshape(n_ty, -1)[:, :size].reshape(n_ty, 2, span_x, span_y)
    g_re = got[:, 0]
    g_im = got[:, 1]
    y_pos = lax.axis_index("ty") * cells_y + jnp.arange(cells_y, dtype=jnp.int32)
    by_c, by_s = chunk_tables(cols_ky, span_y, n_ty, my // 2 + SHIFT, y_pos, full_y)
    i_re = jnp.einsum("cuv,cvy->uy", g_re, by_c, precision=PREC) - jnp.einsum(
        "cuv,cvy->uy", g_im, by_s, precision=PREC
    )
    i_im = jnp.einsum("cuv,cvy->uy", g_re, by_s, precision=PREC) + jnp.einsum(
        "cuv,cvy->uy", g_im, by_c, precision=PREC
    )
    inner = gather_along(jnp.stack([i_re, i_im]), ("tx",), 1)
    i_re = inner[:, 0]
    i_im = inner[:, 1]
    x_pos = lax.axis_index("tx") * cells_x + jnp.arange(cells_x, dtype=jnp.int32)
    bx_c, bx_s = chunk_tables(rows_kx, span_x, n_tx, mx // 2 + SHIFT, x_pos, full_x)
    p_re = jnp.einsum("cux,cuy->xy", bx_c, i_re, precision=PREC) - jnp.einsum(
        "cux,cuy->xy", bx_s, i_im, precision=PREC
    )
    p_im = jnp.einsum("cux,cuy->xy", bx_c, i_im, precision=PREC) + jnp.einsum(
        "cux,cuy->xy", bx_s, i_re, precision=PREC
    )
    return jnp.stack([p_re, p_im]), frow, fcol


def yee_kernel(e_ref, h_ref, coef_ref, plane_ref, frow, fcol, eo_ref, ho_ref,
               ext, cp, tmp, srow, rrow, scol, rcol, send, recv):
    layers, cells_x, cells_y = coef_ref.shape
    depth = srow.shape[2]
    rows = cells_x + 2 * depth
    lanes = ext.shape[2]
    slab = layers + 2
    n_field = 6 * layers
    n_tx = lax.axis_size("tx")
    n_ty = lax.axis_size("ty")
    me_x = lax.axis_index("tx")
    me_y = lax.axis_index("ty")
    x_lo = {"tx": lax.rem(me_x + n_tx - 1, n_tx)}
    x_hi = {"tx": lax.rem(me_x + 1, n_tx)}
    y_lo = {"ty": lax.rem(me_y + n_ty - 1, n_ty)}
    y_hi = {"ty": lax.rem(me_y + 1, n_ty)}

    barrier = pltpu.get_barrier_semaphore()
    for peer in (x_lo, x_hi, y_lo, y_hi):
        pl.semaphore_signal(barrier, 1, device_id=peer, device_id_type=MESH)
    pl.semaphore_wait(barrier, 4)

    for k in range(2):
        srow[0, k] = plane_ref[k, 0:depth]
        srow[1, k] = plane_ref[k, cells_x - depth:cells_x]
    row_copies = [
        pltpu.make_async_remote_copy(
            src_ref=srow.at[0], dst_ref=rrow.at[0], send_sem=send.at[0], recv_sem=recv.at[0],
            device_id=x_lo, device_id_type=MESH,
        ),
        pltpu.make_async_remote_copy(
            src_ref=srow.at[1], dst_ref=rrow.at[1], send_sem=send.at[1], recv_sem=recv.at[1],
            device_id=x_hi, device_id_type=MESH,
        ),
    ]
    for copy in row_copies:
        copy.start()

    tmp[...] = jnp.zeros_like(tmp)
    lane = lax.broadcasted_iota(jnp.int32, (rows, cells_y), 1)

    def place_cols(dst, idx, col_a, col_b):
        v = jnp.concatenate([col_a, col_b], 0)
        tmp[:, 0:2 * depth] = v.T
        w = tmp[...]
        front = jnp.where(lane < depth, w, 0.0)
        back = jnp.where(lane >= depth, w, 0.0)
        dst[idx, :, cells_y:lanes] = front + pltpu.roll(back, cells_y - 2 * depth, 1)

    def place_part(dst, idx, own, h):
        dst[idx, 0:cells_x, 0:cells_y] = own
        dst[idx, cells_x:cells_x + depth, 0:cells_y] = frow[0, h]
        dst[idx, cells_x + depth:rows, 0:cells_y] = frow[1, h]
        place_cols(dst, idx, fcol[0, h], fcol[1, h])

    def place_fields(h, carry):
        comp = h // layers
        z = h % layers
        own = jnp.where(comp < 3, e_ref[comp % 3, z], h_ref[comp % 3, z])
        place_part(ext, comp * slab + z + 1, own, h)
        return carry

    lax.fori_loop(0, n_field, place_fields, 0)
    for z in range(layers):
        place_part(cp, z, coef_ref[z], n_field + z)
    zero = jnp.zeros((rows, lanes), jnp.float32)
    for comp in range(3):
        ext[comp * slab + slab - 1] = zero
        ext[(3 + comp) * slab] = zero
    for copy in row_copies:
        copy.wait()

    for k in range(2):
        idx = layers + k
        cp[idx, 0:cells_x, 0:cells_y] = plane_ref[k]
        cp[idx, cells_x:cells_x + depth, 0:cells_y] = rrow[0, k]
        cp[idx, cells_x + depth:rows, 0:cells_y] = rrow[1, k]
        t = cp[idx, :, 0:cells_y].T
        scol[0, k] = t[0:depth]
        scol[1, k] = t[cells_y - depth:cells_y]
    col_copies = [
        pltpu.make_async_remote_copy(
            src_ref=scol.at[0], dst_ref=rcol.at[0], send_sem=send.at[2], recv_sem=recv.at[2],
            device_id=y_lo, device_id_type=MESH,
        ),
        pltpu.make_async_remote_copy(
            src_ref=scol.at[1], dst_ref=rcol.at[1], send_sem=send.at[3], recv_sem=recv.at[3],
            device_id=y_hi, device_id_type=MESH,
        ),
    ]
    for copy in col_copies:
        copy.start()
    for copy in col_copies:
        copy.wait()
    for k in range(2):
        place_cols(cp, layers + k, rcol[0, k], rcol[1, k])

    ahead_x = lambda f: pltpu.roll(f, rows - 1, 0)
    ahead_y = lambda f: pltpu.roll(f, lanes - 1, 1)
    behind_x = lambda f: pltpu.roll(f, 1, 0)
    behind_y = lambda f: pltpu.roll(f, 1, 1)
    ex_, ey_, ez_, hx_, hy_, hz_ = (c * slab for c in range(6))

    for step in range(STEPS):
        def h_update(z, carry):
            s = z + 1
            e_x = ext[ex_ + s]
            e_y = ext[ey_ + s]
            e_z = ext[ez_ + s]
            ext[hx_ + s] = ext[hx_ + s] - COURANT * ((ahead_y(e_z) - e_z) - (ext[ey_ + s + 1] - e_y))
            ext[hy_ + s] = ext[hy_ + s] - COURANT * ((ext[ex_ + s + 1] - e_x) - (ahead_x(e_z) - e_z))
            ext[hz_ + s] = ext[hz_ + s] - COURANT * ((ahead_x(e_y) - e_y) - (ahead_y(e_x) - e_x))
            return carry

        def e_update(z, carry):
            s = z + 1
            h_x = ext[hx_ + s]
            h_y = ext[hy_ + s]
            h_z = ext[hz_ + s]
            c = cp[z]
            ext[ex_ + s] = ext[ex_ + s] + c * ((h_z - behind_y(h_z)) - (h_y - ext[hy_ + s - 1]))
            ext[ey_ + s] = ext[ey_ + s] + c * ((h_x - ext[hx_ + s - 1]) - (h_z - behind_x(h_z)))
            ext[ez_ + s] = ext[ez_ + s] + c * ((h_y - behind_x(h_y)) - (h_x - behind_y(h_x)))
            return carry

        lax.fori_loop(0, layers, h_update, 0)
        lax.fori_loop(0, layers, e_update, 0)
        cosine = math.cos(OMEGA * (step + 1))
        sine = math.sin(OMEGA * (step + 1))
        p_re = cp[layers]
        p_im = cp[layers + 1]
        s = ZINJ + 1
        ext[ex_ + s] = ext[ex_ + s] + COURANT * (cosine * p_re - sine * p_im)
        ext[ey_ + s] = ext[ey_ + s] + COURANT * (sine * p_re + cosine * p_im)

    for comp in range(3):
        for z in range(layers):
            eo_ref[comp, z] = ext[comp * slab + z + 1, 0:cells_x, 0:cells_y]
            ho_ref[comp, z] = ext[(3 + comp) * slab + z + 1, 0:cells_x, 0:cells_y]


def per_device(orders, offsets, material, e_field, h_field):
    layers, cells_x, cells_y = material.shape
    coefficient = cell_coefficient(material)
    plane, frow, fcol = injection_plane(orders, offsets, e_field, h_field, coefficient)
    depth = HALO
    rows = cells_x + 2 * depth
    lanes = 2 * cells_y
    out = jax.ShapeDtypeStruct(e_field.shape, jnp.float32)
    return pl.pallas_call(
        yee_kernel,
        out_shape=(out, out),
        in_specs=[VMEM_SPEC] * 6,
        out_specs=(VMEM_SPEC, VMEM_SPEC),
        scratch_shapes=[
            pltpu.VMEM((6 * (layers + 2), rows, lanes), jnp.float32),
            pltpu.VMEM((layers + 2, rows, lanes), jnp.float32),
            pltpu.VMEM((rows, cells_y), jnp.float32),
            pltpu.VMEM((2, 2, depth, cells_y), jnp.float32),
            pltpu.VMEM((2, 2, depth, cells_y), jnp.float32),
            pltpu.VMEM((2, 2, depth, rows), jnp.float32),
            pltpu.VMEM((2, 2, depth, rows), jnp.float32),
            pltpu.SemaphoreType.DMA((4,)),
            pltpu.SemaphoreType.DMA((4,)),
        ],
        compiler_params=pltpu.CompilerParams(
            collective_id=3, has_side_effects=True, vmem_limit_bytes=64 * 1024 * 1024
        ),
    )(e_field, h_field, coefficient, plane, frow, fcol)


def solution(mesh):
    in_specs = (
        P("src", None, "tx", "ty"),
        P("src", None),
        P(None, "tx", "ty"),
        P(None, None, "tx", "ty"),
        P(None, None, "tx", "ty"),
    )
    out_specs = (P(None, None, "tx", "ty"), P(None, None, "tx", "ty"))
    return jax.shard_map(
        per_device, mesh=mesh, in_specs=in_specs, out_specs=out_specs, check_vma=False
    )
```

```python
import math

import jax
import jax.numpy as jnp
from jax import lax
from jax.sharding import PartitionSpec as P
from jax.experimental import pallas as pl
from jax.experimental.pallas import tpu as pltpu

STEPS = 4
ZINJ = 1


COURANT = 0.5
OMEGA = 0.7
PERMITTIVITY = (1.0, 2.6, 11.9, 2.1)
PREC = lax.Precision.HIGH
SHIFT = 8
HALO = 8


def phase_tables(freqs, positions, length):
    product = jnp.mod(freqs[:, None] * positions[None, :], length)
    angle = product.astype(jnp.float32) * (2.0 * math.pi / length)
    return (jnp.cos(angle), jnp.sin(angle))


def cell_coefficient(material):
    total = jnp.zeros(material.shape, jnp.float32)
    for number in range(len(PERMITTIVITY)):
        total = total + jnp.where(material == number, COURANT / PERMITTIVITY[number], 0.0)
    return total


MESH = pl.DeviceIdType.MESH
VMEM_SPEC = pl.BlockSpec(memory_space=pltpu.MemorySpace.VMEM)


def gather_along(block, axes, collective):
    sizes = [lax.axis_size(a) for a in axes]
    n = 1
    for s in sizes:
        n *= s

    def coords(linear):
        out = {}
        for a, s in reversed(list(zip(axes, sizes))):
            out[a] = lax.rem(linear, s)
            linear = linear // s
        return out

    def kernel(x_ref, o_ref, send, recv, local):
        me = 0
        for a, s in zip(axes, sizes):
            me = me * s + lax.axis_index(a)
        barrier = pltpu.get_barrier_semaphore()
        for k in range(1, n):
            pl.semaphore_signal(barrier, 1, device_id=coords(lax.rem(me + k, n)), device_id_type=MESH)
        pl.semaphore_wait(barrier, n - 1)
        own = pltpu.make_async_copy(x_ref, o_ref.at[me], local.at[0])
        own.start()
        copies = []
        for k in range(1, n):
            copy = pltpu.make_async_remote_copy(
                src_ref=x_ref,
                dst_ref=o_ref.at[me],
                send_sem=send.at[k - 1],
                recv_sem=recv.at[k - 1],
                device_id=coords(lax.rem(me + k, n)),
                device_id_type=MESH,
            )
            copy.start()
            copies.append(copy)
        own.wait()
        for copy in copies:
            copy.wait()

    return pl.pallas_call(
        kernel,
        out_shape=jax.ShapeDtypeStruct((n,) + block.shape, block.dtype),
        in_specs=[VMEM_SPEC],
        out_specs=VMEM_SPEC,
        scratch_shapes=[
            pltpu.SemaphoreType.DMA((n - 1,)),
            pltpu.SemaphoreType.DMA((n - 1,)),
            pltpu.SemaphoreType.DMA((1,)),
        ],
        compiler_params=pltpu.CompilerParams(collective_id=collective, has_side_effects=True),
    )(block)


def gather_with_halo(block, e_field, h_field, coefficient, depth, collective):
    n = lax.axis_size("ty")
    layers, cells_x, cells_y = coefficient.shape
    rows = cells_x + 2 * depth
    n_parts = 7 * layers

    def kernel(x_ref, e_ref, h_ref, coef_ref, o_ref, rrow, rcol,
               gsend, grecv, local, srow, scol, tmp, hsend, hrecv):
        me = lax.axis_index("ty")
        n_tx = lax.axis_size("tx")
        me_x = lax.axis_index("tx")
        x_lo = {"tx": lax.rem(me_x + n_tx - 1, n_tx)}
        x_hi = {"tx": lax.rem(me_x + 1, n_tx)}
        y_lo = {"ty": lax.rem(me + n - 1, n)}
        y_hi = {"ty": lax.rem(me + 1, n)}
        barrier = pltpu.get_barrier_semaphore()
        for k in range(1, n):
            pl.semaphore_signal(barrier, 1, device_id={"ty": lax.rem(me + k, n)}, device_id_type=MESH)
        for peer in (x_lo, x_hi):
            pl.semaphore_signal(barrier, 1, device_id=peer, device_id_type=MESH)
        pl.semaphore_wait(barrier, n + 1)
        own = pltpu.make_async_copy(x_ref, o_ref.at[me], local.at[0])
        own.start()
        gathers = []
        for k in range(1, n):
            copy = pltpu.make_async_remote_copy(
                src_ref=x_ref, dst_ref=o_ref.at[me], send_sem=gsend.at[k - 1], recv_sem=grecv.at[k - 1],
                device_id={"ty": lax.rem(me + k, n)}, device_id_type=MESH,
            )
            copy.start()
            gathers.append(copy)

        def part_of(h):
            comp = h // layers
            z = h % layers
            field = jnp.where(comp < 3, e_ref[comp % 3, z], h_ref[comp % 3, z])
            return jnp.where(comp < 6, field, coef_ref[z])

        def fill_rows(h, carry):
            part = part_of(h)
            srow[0, h] = part[0:depth]
            srow[1, h] = part[cells_x - depth:cells_x]
            return carry

        lax.fori_loop(0, n_parts, fill_rows, 0)
        row_copies = [
            pltpu.make_async_remote_copy(
                src_ref=srow.at[0], dst_ref=rrow.at[0], send_sem=hsend.at[0], recv_sem=hrecv.at[0],
                device_id=x_lo, device_id_type=MESH,
            ),
            pltpu.make_async_remote_copy(
                src_ref=srow.at[1], dst_ref=rrow.at[1], send_sem=hsend.at[1], recv_sem=hrecv.at[1],
                device_id=x_hi, device_id_type=MESH,
            ),
        ]
        for copy in row_copies:
            copy.start()
        for copy in row_copies:
            copy.wait()

        def fill_cols(h, carry):
            tmp[0:cells_x] = part_of(h)
            tmp[cells_x:cells_x + depth] = rrow[0, h]
            tmp[cells_x + depth:rows] = rrow[1, h]
            t = tmp[...].T
            scol[0, h] = t[0:depth]
            scol[1, h] = t[cells_y - depth:cells_y]
            return carry

        lax.fori_loop(0, n_parts, fill_cols, 0)
        col_copies = [
            pltpu.make_async_remote_copy(
                src_ref=scol.at[0], dst_ref=rcol.at[0], send_sem=hsend.at[2], recv_sem=hrecv.at[2],
                device_id=y_lo, device_id_type=MESH,
            ),
            pltpu.make_async_remote_copy(
                src_ref=scol.at[1], dst_ref=rcol.at[1], send_sem=hsend.at[3], recv_sem=hrecv.at[3],
                device_id=y_hi, device_id_type=MESH,
            ),
        ]
        for copy in col_copies:
            copy.start()
        for copy in col_copies:
            copy.wait()
        own.wait()
        for copy in gathers:
            copy.wait()

    return pl.pallas_call(
        kernel,
        out_shape=(
            jax.ShapeDtypeStruct((n,) + block.shape, block.dtype),
            jax.ShapeDtypeStruct((2, n_parts, depth, cells_y), jnp.float32),
            jax.ShapeDtypeStruct((2, n_parts, depth, rows), jnp.float32),
        ),
        in_specs=[VMEM_SPEC] * 4,
        out_specs=(VMEM_SPEC, VMEM_SPEC, VMEM_SPEC),
        scratch_shapes=[
            pltpu.SemaphoreType.DMA((n - 1,)),
            pltpu.SemaphoreType.DMA((n - 1,)),
            pltpu.SemaphoreType.DMA((1,)),
            pltpu.VMEM((2, n_parts, depth, cells_y), jnp.float32),
            pltpu.VMEM((2, n_parts, depth, rows), jnp.float32),
            pltpu.VMEM((rows, cells_y), jnp.float32),
            pltpu.SemaphoreType.DMA((4,)),
            pltpu.SemaphoreType.DMA((4,)),
        ],
        compiler_params=pltpu.CompilerParams(
            collective_id=collective, has_side_effects=True, vmem_limit_bytes=64 * 1024 * 1024
        ),
    )(block, e_field, h_field, coefficient)


def summed_over_pair(block, axis, collective):
    def kernel(x_ref, o_ref, got, send, recv):
        other = {axis: 1 - lax.axis_index(axis)}
        barrier = pltpu.get_barrier_semaphore()
        pl.semaphore_signal(barrier, 1, device_id=other, device_id_type=MESH)
        pl.semaphore_wait(barrier, 1)
        copy = pltpu.make_async_remote_copy(
            src_ref=x_ref, dst_ref=got, send_sem=send.at[0], recv_sem=recv.at[0],
            device_id=other, device_id_type=MESH,
        )
        copy.start()
        copy.wait()
        o_ref[...] = x_ref[...] + got[...]

    return pl.pallas_call(
        kernel,
        out_shape=jax.ShapeDtypeStruct(block.shape, block.dtype),
        in_specs=[VMEM_SPEC],
        out_specs=VMEM_SPEC,
        scratch_shapes=[
            pltpu.VMEM(block.shape, block.dtype),
            pltpu.SemaphoreType.DMA((1,)),
            pltpu.SemaphoreType.DMA((1,)),
        ],
        compiler_params=pltpu.CompilerParams(collective_id=collective, has_side_effects=True),
    )(block)


def chunk_tables(step, span, count, base, positions, length):
    c1, s1 = phase_tables(jnp.arange(count, dtype=jnp.int32) * step, positions, length)
    c2, s2 = phase_tables(jnp.arange(span, dtype=jnp.int32) - base, positions, length)
    cos_t = c1[:, None, :] * c2[None, :, :] - s1[:, None, :] * s2[None, :, :]
    sin_t = s1[:, None, :] * c2[None, :, :] + c1[:, None, :] * s2[None, :, :]
    return cos_t, sin_t


def ring_positions(cells, depth):
    own = jnp.arange(cells + depth, dtype=jnp.int32)
    return jnp.concatenate([own, jnp.arange(-depth, 0, dtype=jnp.int32)])


def lane_dense(block):
    flat = block.reshape(-1)
    pad = (-flat.shape[0]) % 1024
    return jnp.pad(flat, (0, pad)).reshape(-1, 128)


def injection_plane(orders, offsets, e_field, h_field, coefficient):
    layers, cells_x, cells_y = coefficient.shape
    points, _, rows_kx, cols_ky = orders.shape
    n_src = lax.axis_size("src")
    n_tx = lax.axis_size("tx")
    n_ty = lax.axis_size("ty")
    full_x = cells_x * n_tx
    full_y = cells_y * n_ty
    mx = rows_kx * n_tx
    my = cols_ky * n_ty
    span_x = rows_kx + 2 * SHIFT
    span_y = cols_ky + 2 * SHIFT
    lift_x = (
        lax.broadcasted_iota(jnp.int32, (points, span_x, rows_kx), 1)
        == lax.broadcasted_iota(jnp.int32, (points, span_x, rows_kx), 2) + offsets[:, 0:1, None] + SHIFT
    ).astype(jnp.float32)
    lift_y = (
        lax.broadcasted_iota(jnp.int32, (points, span_y, cols_ky), 1)
        == lax.broadcasted_iota(jnp.int32, (points, span_y, cols_ky), 2) + offsets[:, 1:2, None] + SHIFT
    ).astype(jnp.float32)
    exact = lax.Precision.HIGHEST
    placed = jnp.einsum("puk,prkj->pruj", lift_x, orders, precision=exact)
    merged = jnp.einsum("pruj,pvj->ruv", placed, lift_y, precision=exact)
    size = merged.size
    merged = summed_over_pair(lane_dense(merged), "src", 2)
    got, frow, fcol = gather_with_halo(merged, e_field, h_field, coefficient, HALO, 0)
    got = got.reshape(n_ty, -1)[:, :size].reshape(n_ty, 2, span_x, span_y)
    g_re = got[:, 0]
    g_im = got[:, 1]
    y_pos = lax.axis_index("ty") * cells_y + ring_positions(cells_y, HALO)
    by_c, by_s = chunk_tables(cols_ky, span_y, n_ty, my // 2 + SHIFT, y_pos, full_y)
    i_re = jnp.einsum("cuv,cvy->uy", g_re, by_c, precision=PREC) - jnp.einsum(
        "cuv,cvy->uy", g_im, by_s, precision=PREC
    )
    i_im = jnp.einsum("cuv,cvy->uy", g_re, by_s, precision=PREC) + jnp.einsum(
        "cuv,cvy->uy", g_im, by_c, precision=PREC
    )
    inner = jnp.stack([i_re, i_im])
    size = inner.size
    inner = gather_along(lane_dense(inner), ("tx",), 1)
    inner = inner.reshape(n_tx, -1)[:, :size].reshape((n_tx,) + (2, span_x, cells_y + 2 * HALO))
    i_re = inner[:, 0]
    i_im = inner[:, 1]
    x_pos = lax.axis_index("tx") * cells_x + ring_positions(cells_x, HALO)
    bx_c, bx_s = chunk_tables(rows_kx, span_x, n_tx, mx // 2 + SHIFT, x_pos, full_x)
    p_re = jnp.einsum("cux,cuy->xy", bx_c, i_re, precision=PREC) - jnp.einsum(
        "cux,cuy->xy", bx_s, i_im, precision=PREC
    )
    p_im = jnp.einsum("cux,cuy->xy", bx_c, i_im, precision=PREC) + jnp.einsum(
        "cux,cuy->xy", bx_s, i_re, precision=PREC
    )
    return jnp.stack([p_re, p_im]), frow, fcol


def yee_kernel(e_ref, h_ref, coef_ref, plane_ref, frow, fcol, eo_ref, ho_ref, ext, cp, tmp):
    layers, cells_x, cells_y = coef_ref.shape
    depth = frow.shape[2]
    rows = cells_x + 2 * depth
    lanes = ext.shape[2]
    slab = layers + 2
    n_field = 6 * layers
    tmp[...] = jnp.zeros_like(tmp)
    lane = lax.broadcasted_iota(jnp.int32, (rows, cells_y), 1)

    def place_cols(dst, idx, col_a, col_b):
        v = jnp.concatenate([col_a, col_b], 0)
        tmp[:, 0:2 * depth] = v.T
        w = tmp[...]
        front = jnp.where(lane < depth, w, 0.0)
        back = jnp.where(lane >= depth, w, 0.0)
        dst[idx, :, cells_y:lanes] = front + pltpu.roll(back, cells_y - 2 * depth, 1)

    def place_part(dst, idx, own, h):
        dst[idx, 0:cells_x, 0:cells_y] = own
        dst[idx, cells_x:cells_x + depth, 0:cells_y] = frow[0, h]
        dst[idx, cells_x + depth:rows, 0:cells_y] = frow[1, h]
        place_cols(dst, idx, fcol[0, h], fcol[1, h])

    def place_fields(h, carry):
        comp = h // layers
        z = h % layers
        own = jnp.where(comp < 3, e_ref[comp % 3, z], h_ref[comp % 3, z])
        place_part(ext, comp * slab + z + 1, own, h)
        return carry

    lax.fori_loop(0, n_field, place_fields, 0)
    for z in range(layers):
        place_part(cp, z, coef_ref[z], n_field + z)
    zero = jnp.zeros((rows, lanes), jnp.float32)
    for comp in range(3):
        ext[comp * slab + slab - 1] = zero
        ext[(3 + comp) * slab] = zero
    for k in range(2):
        idx = layers + k
        cp[idx, :, 0:cells_y] = plane_ref[k, :, 0:cells_y]
        tmp[:, 0:2 * depth] = plane_ref[k, :, cells_y:cells_y + 2 * depth]
        w = tmp[...]
        front = jnp.where(lane < depth, w, 0.0)
        back = jnp.where(lane >= depth, w, 0.0)
        cp[idx, :, cells_y:lanes] = front + pltpu.roll(back, cells_y - 2 * depth, 1)

    ahead_x = lambda f: pltpu.roll(f, rows - 1, 0)
    ahead_y = lambda f: pltpu.roll(f, lanes - 1, 1)
    behind_x = lambda f: pltpu.roll(f, 1, 0)
    behind_y = lambda f: pltpu.roll(f, 1, 1)
    ex_, ey_, ez_, hx_, hy_, hz_ = (c * slab for c in range(6))

    for step in range(STEPS):
        def h_update(z, carry):
            s = z + 1
            e_x = ext[ex_ + s]
            e_y = ext[ey_ + s]
            e_z = ext[ez_ + s]
            ext[hx_ + s] = ext[hx_ + s] - COURANT * ((ahead_y(e_z) - e_z) - (ext[ey_ + s + 1] - e_y))
            ext[hy_ + s] = ext[hy_ + s] - COURANT * ((ext[ex_ + s + 1] - e_x) - (ahead_x(e_z) - e_z))
            ext[hz_ + s] = ext[hz_ + s] - COURANT * ((ahead_x(e_y) - e_y) - (ahead_y(e_x) - e_x))
            return carry

        def e_update(z, carry):
            s = z + 1
            h_x = ext[hx_ + s]
            h_y = ext[hy_ + s]
            h_z = ext[hz_ + s]
            c = cp[z]
            ext[ex_ + s] = ext[ex_ + s] + c * ((h_z - behind_y(h_z)) - (h_y - ext[hy_ + s - 1]))
            ext[ey_ + s] = ext[ey_ + s] + c * ((h_x - ext[hx_ + s - 1]) - (h_z - behind_x(h_z)))
            ext[ez_ + s] = ext[ez_ + s] + c * ((h_y - behind_x(h_y)) - (h_x - behind_y(h_x)))
            return carry

        lax.fori_loop(0, layers, h_update, 0)
        lax.fori_loop(0, layers, e_update, 0)
        cosine = math.cos(OMEGA * (step + 1))
        sine = math.sin(OMEGA * (step + 1))
        p_re = cp[layers]
        p_im = cp[layers + 1]
        s = ZINJ + 1
        ext[ex_ + s] = ext[ex_ + s] + COURANT * (cosine * p_re - sine * p_im)
        ext[ey_ + s] = ext[ey_ + s] + COURANT * (sine * p_re + cosine * p_im)

    for comp in range(3):
        for z in range(layers):
            eo_ref[comp, z] = ext[comp * slab + z + 1, 0:cells_x, 0:cells_y]
            ho_ref[comp, z] = ext[(3 + comp) * slab + z + 1, 0:cells_x, 0:cells_y]


def per_device(orders, offsets, material, e_field, h_field):
    layers, cells_x, cells_y = material.shape
    coefficient = cell_coefficient(material)
    plane, frow, fcol = injection_plane(orders, offsets, e_field, h_field, coefficient)
    depth = HALO
    rows = cells_x + 2 * depth
    lanes = 2 * cells_y
    out = jax.ShapeDtypeStruct(e_field.shape, jnp.float32)
    return pl.pallas_call(
        yee_kernel,
        out_shape=(out, out),
        in_specs=[VMEM_SPEC] * 6,
        out_specs=(VMEM_SPEC, VMEM_SPEC),
        scratch_shapes=[
            pltpu.VMEM((6 * (layers + 2), rows, lanes), jnp.float32),
            pltpu.VMEM((layers + 2, rows, lanes), jnp.float32),
            pltpu.VMEM((rows, cells_y), jnp.float32),
        ],
        compiler_params=pltpu.CompilerParams(vmem_limit_bytes=64 * 1024 * 1024),
    )(e_field, h_field, coefficient, plane, frow, fcol)


def solution(mesh):
    in_specs = (
        P("src", None, "tx", "ty"),
        P("src", None),
        P(None, "tx", "ty"),
        P(None, None, "tx", "ty"),
        P(None, None, "tx", "ty"),
    )
    out_specs = (P(None, None, "tx", "ty"), P(None, None, "tx", "ty"))
    return jax.shard_map(
        per_device, mesh=mesh, in_specs=in_specs, out_specs=out_specs, check_vma=False
    )
```

```python
import math

import jax
import jax.numpy as jnp
from jax import lax
from jax.sharding import PartitionSpec as P
from jax.experimental import pallas as pl
from jax.experimental.pallas import tpu as pltpu

STEPS = 4
ZINJ = 1


COURANT = 0.5
OMEGA = 0.7
PERMITTIVITY = (1.0, 2.6, 11.9, 2.1)
PREC = lax.Precision.HIGH
SHIFT = 8
HALO = 8


def phase_tables(freqs, positions, length):
    product = jnp.mod(freqs[:, None] * positions[None, :], length)
    angle = product.astype(jnp.float32) * (2.0 * math.pi / length)
    return (jnp.cos(angle), jnp.sin(angle))


def cell_coefficient(material):
    total = jnp.zeros(material.shape, jnp.float32)
    for number in range(len(PERMITTIVITY)):
        total = total + jnp.where(material == number, COURANT / PERMITTIVITY[number], 0.0)
    return total


MESH = pl.DeviceIdType.MESH
VMEM_SPEC = pl.BlockSpec(memory_space=pltpu.MemorySpace.VMEM)


def gather_along(block, axes, collective):
    sizes = [lax.axis_size(a) for a in axes]
    n = 1
    for s in sizes:
        n *= s

    def coords(linear):
        out = {}
        for a, s in reversed(list(zip(axes, sizes))):
            out[a] = lax.rem(linear, s)
            linear = linear // s
        return out

    def kernel(x_ref, o_ref, send, recv, local):
        me = 0
        for a, s in zip(axes, sizes):
            me = me * s + lax.axis_index(a)
        barrier = pltpu.get_barrier_semaphore()
        for k in range(1, n):
            pl.semaphore_signal(barrier, 1, device_id=coords(lax.rem(me + k, n)), device_id_type=MESH)
        pl.semaphore_wait(barrier, n - 1)
        own = pltpu.make_async_copy(x_ref, o_ref.at[me], local.at[0])
        own.start()
        copies = []
        for k in range(1, n):
            copy = pltpu.make_async_remote_copy(
                src_ref=x_ref,
                dst_ref=o_ref.at[me],
                send_sem=send.at[k - 1],
                recv_sem=recv.at[k - 1],
                device_id=coords(lax.rem(me + k, n)),
                device_id_type=MESH,
            )
            copy.start()
            copies.append(copy)
        own.wait()
        for copy in copies:
            copy.wait()

    return pl.pallas_call(
        kernel,
        out_shape=jax.ShapeDtypeStruct((n,) + block.shape, block.dtype),
        in_specs=[VMEM_SPEC],
        out_specs=VMEM_SPEC,
        scratch_shapes=[
            pltpu.SemaphoreType.DMA((n - 1,)),
            pltpu.SemaphoreType.DMA((n - 1,)),
            pltpu.SemaphoreType.DMA((1,)),
        ],
        compiler_params=pltpu.CompilerParams(collective_id=collective, has_side_effects=True),
    )(block)


def gather_with_halo(block, e_field, h_field, coefficient, depth, collective):
    n = lax.axis_size("ty")
    layers, cells_x, cells_y = coefficient.shape
    rows = cells_x + 2 * depth
    n_parts = 7 * layers

    def kernel(x_ref, e_ref, h_ref, coef_ref, o_ref, rrow, rcol,
               gsend, grecv, local, srow, scol, tmp, hsend, hrecv):
        me = lax.axis_index("ty")
        n_tx = lax.axis_size("tx")
        me_x = lax.axis_index("tx")
        x_lo = {"tx": lax.rem(me_x + n_tx - 1, n_tx)}
        x_hi = {"tx": lax.rem(me_x + 1, n_tx)}
        y_lo = {"ty": lax.rem(me + n - 1, n)}
        y_hi = {"ty": lax.rem(me + 1, n)}
        barrier = pltpu.get_barrier_semaphore()
        for k in range(1, n):
            pl.semaphore_signal(barrier, 1, device_id={"ty": lax.rem(me + k, n)}, device_id_type=MESH)
        for peer in (x_lo, x_hi):
            pl.semaphore_signal(barrier, 1, device_id=peer, device_id_type=MESH)
        pl.semaphore_wait(barrier, n + 1)
        own = pltpu.make_async_copy(x_ref, o_ref.at[me], local.at[0])
        own.start()
        gathers = []
        for k in range(1, n):
            copy = pltpu.make_async_remote_copy(
                src_ref=x_ref, dst_ref=o_ref.at[me], send_sem=gsend.at[k - 1], recv_sem=grecv.at[k - 1],
                device_id={"ty": lax.rem(me + k, n)}, device_id_type=MESH,
            )
            copy.start()
            gathers.append(copy)

        def part_of(h):
            comp = h // layers
            z = h % layers
            field = jnp.where(comp < 3, e_ref[comp % 3, z], h_ref[comp % 3, z])
            return jnp.where(comp < 6, field, coef_ref[z])

        def fill_rows(h, carry):
            part = part_of(h)
            srow[0, h] = part[0:depth]
            srow[1, h] = part[cells_x - depth:cells_x]
            return carry

        lax.fori_loop(0, n_parts, fill_rows, 0)
        row_copies = [
            pltpu.make_async_remote_copy(
                src_ref=srow.at[0], dst_ref=rrow.at[0], send_sem=hsend.at[0], recv_sem=hrecv.at[0],
                device_id=x_lo, device_id_type=MESH,
            ),
            pltpu.make_async_remote_copy(
                src_ref=srow.at[1], dst_ref=rrow.at[1], send_sem=hsend.at[1], recv_sem=hrecv.at[1],
                device_id=x_hi, device_id_type=MESH,
            ),
        ]
        for copy in row_copies:
            copy.start()
        for copy in row_copies:
            copy.wait()

        def fill_cols(h, carry):
            tmp[0:cells_x] = part_of(h)
            tmp[cells_x:cells_x + depth] = rrow[0, h]
            tmp[cells_x + depth:rows] = rrow[1, h]
            t = lax.dot_general(
                pick, tmp[...], (((1,), (1,)), ((), ())),
                precision=lax.Precision.HIGHEST, preferred_element_type=jnp.float32,
            )
            scol[0, h] = t[0:depth]
            scol[1, h] = t[depth:2 * depth]
            return carry

        row_id = lax.broadcasted_iota(jnp.int32, (2 * depth, cells_y), 0)
        col_id = lax.broadcasted_iota(jnp.int32, (2 * depth, cells_y), 1)
        wanted = jnp.where(row_id < depth, row_id, row_id - 2 * depth + cells_y)
        pick = (col_id == wanted).astype(jnp.float32)
        lax.fori_loop(0, n_parts, fill_cols, 0)
        col_copies = [
            pltpu.make_async_remote_copy(
                src_ref=scol.at[0], dst_ref=rcol.at[0], send_sem=hsend.at[2], recv_sem=hrecv.at[2],
                device_id=y_lo, device_id_type=MESH,
            ),
            pltpu.make_async_remote_copy(
                src_ref=scol.at[1], dst_ref=rcol.at[1], send_sem=hsend.at[3], recv_sem=hrecv.at[3],
                device_id=y_hi, device_id_type=MESH,
            ),
        ]
        for copy in col_copies:
            copy.start()
        for copy in col_copies:
            copy.wait()
        own.wait()
        for copy in gathers:
            copy.wait()

    return pl.pallas_call(
        kernel,
        out_shape=(
            jax.ShapeDtypeStruct((n,) + block.shape, block.dtype),
            jax.ShapeDtypeStruct((2, n_parts, depth, cells_y), jnp.float32),
            jax.ShapeDtypeStruct((2, n_parts, depth, rows), jnp.float32),
        ),
        in_specs=[VMEM_SPEC] * 4,
        out_specs=(VMEM_SPEC, VMEM_SPEC, VMEM_SPEC),
        scratch_shapes=[
            pltpu.SemaphoreType.DMA((n - 1,)),
            pltpu.SemaphoreType.DMA((n - 1,)),
            pltpu.SemaphoreType.DMA((1,)),
            pltpu.VMEM((2, n_parts, depth, cells_y), jnp.float32),
            pltpu.VMEM((2, n_parts, depth, rows), jnp.float32),
            pltpu.VMEM((rows, cells_y), jnp.float32),
            pltpu.SemaphoreType.DMA((4,)),
            pltpu.SemaphoreType.DMA((4,)),
        ],
        compiler_params=pltpu.CompilerParams(
            collective_id=collective, has_side_effects=True, vmem_limit_bytes=64 * 1024 * 1024
        ),
    )(block, e_field, h_field, coefficient)


def summed_over_pair(block, axis, collective):
    def kernel(x_ref, o_ref, got, send, recv):
        other = {axis: 1 - lax.axis_index(axis)}
        barrier = pltpu.get_barrier_semaphore()
        pl.semaphore_signal(barrier, 1, device_id=other, device_id_type=MESH)
        pl.semaphore_wait(barrier, 1)
        copy = pltpu.make_async_remote_copy(
            src_ref=x_ref, dst_ref=got, send_sem=send.at[0], recv_sem=recv.at[0],
            device_id=other, device_id_type=MESH,
        )
        copy.start()
        copy.wait()
        o_ref[...] = x_ref[...] + got[...]

    return pl.pallas_call(
        kernel,
        out_shape=jax.ShapeDtypeStruct(block.shape, block.dtype),
        in_specs=[VMEM_SPEC],
        out_specs=VMEM_SPEC,
        scratch_shapes=[
            pltpu.VMEM(block.shape, block.dtype),
            pltpu.SemaphoreType.DMA((1,)),
            pltpu.SemaphoreType.DMA((1,)),
        ],
        compiler_params=pltpu.CompilerParams(collective_id=collective, has_side_effects=True),
    )(block)


def chunk_tables(step, span, count, base, positions, length):
    c1, s1 = phase_tables(jnp.arange(count, dtype=jnp.int32) * step, positions, length)
    c2, s2 = phase_tables(jnp.arange(span, dtype=jnp.int32) - base, positions, length)
    cos_t = c1[:, None, :] * c2[None, :, :] - s1[:, None, :] * s2[None, :, :]
    sin_t = s1[:, None, :] * c2[None, :, :] + c1[:, None, :] * s2[None, :, :]
    return cos_t, sin_t


def ring_positions(cells, depth):
    own = jnp.arange(cells + depth, dtype=jnp.int32)
    return jnp.concatenate([own, jnp.arange(-depth, 0, dtype=jnp.int32)])


def lane_dense(block):
    flat = block.reshape(-1)
    pad = (-flat.shape[0]) % 1024
    return jnp.pad(flat, (0, pad)).reshape(-1, 128)


def injection_plane(orders, offsets, e_field, h_field, coefficient):
    layers, cells_x, cells_y = coefficient.shape
    points, _, rows_kx, cols_ky = orders.shape
    n_src = lax.axis_size("src")
    n_tx = lax.axis_size("tx")
    n_ty = lax.axis_size("ty")
    full_x = cells_x * n_tx
    full_y = cells_y * n_ty
    mx = rows_kx * n_tx
    my = cols_ky * n_ty
    span_x = rows_kx + 2 * SHIFT
    span_y = cols_ky + 2 * SHIFT
    lift_x = (
        lax.broadcasted_iota(jnp.int32, (points, span_x, rows_kx), 1)
        == lax.broadcasted_iota(jnp.int32, (points, span_x, rows_kx), 2) + offsets[:, 0:1, None] + SHIFT
    ).astype(jnp.float32)
    lift_y = (
        lax.broadcasted_iota(jnp.int32, (points, span_y, cols_ky), 1)
        == lax.broadcasted_iota(jnp.int32, (points, span_y, cols_ky), 2) + offsets[:, 1:2, None] + SHIFT
    ).astype(jnp.float32)
    exact = lax.Precision.HIGHEST
    placed = jnp.einsum("puk,prkj->pruj", lift_x, orders, precision=exact)
    merged = jnp.einsum("pruj,pvj->ruv", placed, lift_y, precision=exact)
    size = merged.size
    merged = summed_over_pair(lane_dense(merged), "src", 2)
    got, frow, fcol = gather_with_halo(merged, e_field, h_field, coefficient, HALO, 0)
    got = got.reshape(n_ty, -1)[:, :size].reshape(n_ty, 2, span_x, span_y)
    g_re = got[:, 0]
    g_im = got[:, 1]
    y_pos = lax.axis_index("ty") * cells_y + ring_positions(cells_y, HALO)
    by_c, by_s = chunk_tables(cols_ky, span_y, n_ty, my // 2 + SHIFT, y_pos, full_y)
    i_re = jnp.einsum("cuv,cvy->uy", g_re, by_c, precision=PREC) - jnp.einsum(
        "cuv,cvy->uy", g_im, by_s, precision=PREC
    )
    i_im = jnp.einsum("cuv,cvy->uy", g_re, by_s, precision=PREC) + jnp.einsum(
        "cuv,cvy->uy", g_im, by_c, precision=PREC
    )
    inner = jnp.stack([i_re, i_im])
    size = inner.size
    inner = gather_along(lane_dense(inner), ("tx",), 1)
    inner = inner.reshape(n_tx, -1)[:, :size].reshape((n_tx,) + (2, span_x, cells_y + 2 * HALO))
    i_re = inner[:, 0]
    i_im = inner[:, 1]
    x_pos = lax.axis_index("tx") * cells_x + ring_positions(cells_x, HALO)
    bx_c, bx_s = chunk_tables(rows_kx, span_x, n_tx, mx // 2 + SHIFT, x_pos, full_x)
    p_re = jnp.einsum("cux,cuy->xy", bx_c, i_re, precision=PREC) - jnp.einsum(
        "cux,cuy->xy", bx_s, i_im, precision=PREC
    )
    p_im = jnp.einsum("cux,cuy->xy", bx_c, i_im, precision=PREC) + jnp.einsum(
        "cux,cuy->xy", bx_s, i_re, precision=PREC
    )
    return jnp.stack([p_re, p_im]), frow, fcol


def yee_kernel(e_ref, h_ref, coef_ref, plane_ref, frow, fcol, eo_ref, ho_ref, ext, cp, tmp):
    layers, cells_x, cells_y = coef_ref.shape
    depth = frow.shape[2]
    rows = cells_x + 2 * depth
    lanes = ext.shape[2]
    slab = layers + 2
    n_field = 6 * layers
    tmp[...] = jnp.zeros_like(tmp)
    lane = lax.broadcasted_iota(jnp.int32, (rows, cells_y), 1)

    def place_cols(dst, idx, col_a, col_b):
        v = jnp.concatenate([col_a, col_b], 0)
        tmp[:, 0:2 * depth] = v.T
        w = tmp[...]
        front = jnp.where(lane < depth, w, 0.0)
        back = jnp.where(lane >= depth, w, 0.0)
        dst[idx, :, cells_y:lanes] = front + pltpu.roll(back, cells_y - 2 * depth, 1)

    def place_part(dst, idx, own, h):
        dst[idx, 0:cells_x, 0:cells_y] = own
        dst[idx, cells_x:cells_x + depth, 0:cells_y] = frow[0, h]
        dst[idx, cells_x + depth:rows, 0:cells_y] = frow[1, h]
        place_cols(dst, idx, fcol[0, h], fcol[1, h])

    def place_fields(h, carry):
        comp = h // layers
        z = h % layers
        own = jnp.where(comp < 3, e_ref[comp % 3, z], h_ref[comp % 3, z])
        place_part(ext, comp * slab + z + 1, own, h)
        return carry

    lax.fori_loop(0, n_field, place_fields, 0)
    for z in range(layers):
        place_part(cp, z, coef_ref[z], n_field + z)
    zero = jnp.zeros((rows, lanes), jnp.float32)
    for comp in range(3):
        ext[comp * slab + slab - 1] = zero
        ext[(3 + comp) * slab] = zero
    for k in range(2):
        idx = layers + k
        cp[idx, :, 0:cells_y] = plane_ref[k, :, 0:cells_y]
        tmp[:, 0:2 * depth] = plane_ref[k, :, cells_y:cells_y + 2 * depth]
        w = tmp[...]
        front = jnp.where(lane < depth, w, 0.0)
        back = jnp.where(lane >= depth, w, 0.0)
        cp[idx, :, cells_y:lanes] = front + pltpu.roll(back, cells_y - 2 * depth, 1)

    ahead_x = lambda f: pltpu.roll(f, rows - 1, 0)
    ahead_y = lambda f: pltpu.roll(f, lanes - 1, 1)
    behind_x = lambda f: pltpu.roll(f, 1, 0)
    behind_y = lambda f: pltpu.roll(f, 1, 1)
    ex_, ey_, ez_, hx_, hy_, hz_ = (c * slab for c in range(6))

    for step in range(STEPS):
        def h_update(z, carry):
            s = z + 1
            e_x = ext[ex_ + s]
            e_y = ext[ey_ + s]
            e_z = ext[ez_ + s]
            ext[hx_ + s] = ext[hx_ + s] - COURANT * ((ahead_y(e_z) - e_z) - (ext[ey_ + s + 1] - e_y))
            ext[hy_ + s] = ext[hy_ + s] - COURANT * ((ext[ex_ + s + 1] - e_x) - (ahead_x(e_z) - e_z))
            ext[hz_ + s] = ext[hz_ + s] - COURANT * ((ahead_x(e_y) - e_y) - (ahead_y(e_x) - e_x))
            return carry

        def e_update(z, carry):
            s = z + 1
            h_x = ext[hx_ + s]
            h_y = ext[hy_ + s]
            h_z = ext[hz_ + s]
            c = cp[z]
            ext[ex_ + s] = ext[ex_ + s] + c * ((h_z - behind_y(h_z)) - (h_y - ext[hy_ + s - 1]))
            ext[ey_ + s] = ext[ey_ + s] + c * ((h_x - ext[hx_ + s - 1]) - (h_z - behind_x(h_z)))
            ext[ez_ + s] = ext[ez_ + s] + c * ((h_y - behind_x(h_y)) - (h_x - behind_y(h_x)))
            return carry

        lax.fori_loop(0, layers, h_update, 0)
        lax.fori_loop(0, layers, e_update, 0)
        cosine = math.cos(OMEGA * (step + 1))
        sine = math.sin(OMEGA * (step + 1))
        p_re = cp[layers]
        p_im = cp[layers + 1]
        s = ZINJ + 1
        ext[ex_ + s] = ext[ex_ + s] + COURANT * (cosine * p_re - sine * p_im)
        ext[ey_ + s] = ext[ey_ + s] + COURANT * (sine * p_re + cosine * p_im)

    for comp in range(3):
        for z in range(layers):
            eo_ref[comp, z] = ext[comp * slab + z + 1, 0:cells_x, 0:cells_y]
            ho_ref[comp, z] = ext[(3 + comp) * slab + z + 1, 0:cells_x, 0:cells_y]


def per_device(orders, offsets, material, e_field, h_field):
    layers, cells_x, cells_y = material.shape
    coefficient = cell_coefficient(material)
    plane, frow, fcol = injection_plane(orders, offsets, e_field, h_field, coefficient)
    depth = HALO
    rows = cells_x + 2 * depth
    lanes = 2 * cells_y
    out = jax.ShapeDtypeStruct(e_field.shape, jnp.float32)
    return pl.pallas_call(
        yee_kernel,
        out_shape=(out, out),
        in_specs=[VMEM_SPEC] * 6,
        out_specs=(VMEM_SPEC, VMEM_SPEC),
        scratch_shapes=[
            pltpu.VMEM((6 * (layers + 2), rows, lanes), jnp.float32),
            pltpu.VMEM((layers + 2, rows, lanes), jnp.float32),
            pltpu.VMEM((rows, cells_y), jnp.float32),
        ],
        compiler_params=pltpu.CompilerParams(vmem_limit_bytes=64 * 1024 * 1024),
    )(e_field, h_field, coefficient, plane, frow, fcol)


def solution(mesh):
    in_specs = (
        P("src", None, "tx", "ty"),
        P("src", None),
        P(None, "tx", "ty"),
        P(None, None, "tx", "ty"),
        P(None, None, "tx", "ty"),
    )
    out_specs = (P(None, None, "tx", "ty"), P(None, None, "tx", "ty"))
    return jax.shard_map(
        per_device, mesh=mesh, in_specs=in_specs, out_specs=out_specs, check_vma=False
    )
```

```python
import math

import jax
import jax.numpy as jnp
from jax import lax
from jax.sharding import PartitionSpec as P
from jax.experimental import pallas as pl
from jax.experimental.pallas import tpu as pltpu

STEPS = 4
ZINJ = 1


COURANT = 0.5
OMEGA = 0.7
PERMITTIVITY = (1.0, 2.6, 11.9, 2.1)
PREC = lax.Precision.HIGH
SHIFT = 8
HALO = 8


def phase_tables(freqs, positions, length):
    product = jnp.mod(freqs[:, None] * positions[None, :], length)
    angle = product.astype(jnp.float32) * (2.0 * math.pi / length)
    return (jnp.cos(angle), jnp.sin(angle))


def cell_coefficient(material):
    total = jnp.zeros(material.shape, jnp.float32)
    for number in range(len(PERMITTIVITY)):
        total = total + jnp.where(material == number, COURANT / PERMITTIVITY[number], 0.0)
    return total


MESH = pl.DeviceIdType.MESH
VMEM_SPEC = pl.BlockSpec(memory_space=pltpu.MemorySpace.VMEM)


def gather_along(block, axes, collective):
    sizes = [lax.axis_size(a) for a in axes]
    n = 1
    for s in sizes:
        n *= s

    def coords(linear):
        out = {}
        for a, s in reversed(list(zip(axes, sizes))):
            out[a] = lax.rem(linear, s)
            linear = linear // s
        return out

    def kernel(x_ref, o_ref, send, recv, local):
        me = 0
        for a, s in zip(axes, sizes):
            me = me * s + lax.axis_index(a)
        barrier = pltpu.get_barrier_semaphore()
        for k in range(1, n):
            pl.semaphore_signal(barrier, 1, device_id=coords(lax.rem(me + k, n)), device_id_type=MESH)
        pl.semaphore_wait(barrier, n - 1)
        own = pltpu.make_async_copy(x_ref, o_ref.at[me], local.at[0])
        own.start()
        copies = []
        for k in range(1, n):
            copy = pltpu.make_async_remote_copy(
                src_ref=x_ref,
                dst_ref=o_ref.at[me],
                send_sem=send.at[k - 1],
                recv_sem=recv.at[k - 1],
                device_id=coords(lax.rem(me + k, n)),
                device_id_type=MESH,
            )
            copy.start()
            copies.append(copy)
        own.wait()
        for copy in copies:
            copy.wait()

    return pl.pallas_call(
        kernel,
        out_shape=jax.ShapeDtypeStruct((n,) + block.shape, block.dtype),
        in_specs=[VMEM_SPEC],
        out_specs=VMEM_SPEC,
        scratch_shapes=[
            pltpu.SemaphoreType.DMA((n - 1,)),
            pltpu.SemaphoreType.DMA((n - 1,)),
            pltpu.SemaphoreType.DMA((1,)),
        ],
        compiler_params=pltpu.CompilerParams(collective_id=collective, has_side_effects=True),
    )(block)


def gather_with_halo(block, e_field, h_field, coefficient, depth, collective):
    n = lax.axis_size("ty")
    layers, cells_x, cells_y = coefficient.shape
    rows = cells_x + 2 * depth
    n_parts = 7 * layers

    def kernel(x_ref, e_ref, h_ref, coef_ref, o_ref, rrow, rcol,
               gsend, grecv, local, srow, scol, tmp, hsend, hrecv):
        me = lax.axis_index("ty")
        n_tx = lax.axis_size("tx")
        me_x = lax.axis_index("tx")
        x_lo = {"tx": lax.rem(me_x + n_tx - 1, n_tx)}
        x_hi = {"tx": lax.rem(me_x + 1, n_tx)}
        y_lo = {"ty": lax.rem(me + n - 1, n)}
        y_hi = {"ty": lax.rem(me + 1, n)}
        barrier = pltpu.get_barrier_semaphore()
        for k in range(1, n):
            pl.semaphore_signal(barrier, 1, device_id={"ty": lax.rem(me + k, n)}, device_id_type=MESH)
        for peer in (x_lo, x_hi):
            pl.semaphore_signal(barrier, 1, device_id=peer, device_id_type=MESH)
        pl.semaphore_wait(barrier, n + 1)

        def part_of(h):
            comp = h // layers
            z = h % layers
            field = jnp.where(comp < 3, e_ref[comp % 3, z], h_ref[comp % 3, z])
            return jnp.where(comp < 6, field, coef_ref[z])

        def fill_rows(h, carry):
            part = part_of(h)
            srow[0, h] = part[0:depth]
            srow[1, h] = part[cells_x - depth:cells_x]
            return carry

        lax.fori_loop(0, n_parts, fill_rows, 0)
        row_copies = [
            pltpu.make_async_remote_copy(
                src_ref=srow.at[0], dst_ref=rrow.at[0], send_sem=hsend.at[0], recv_sem=hrecv.at[0],
                device_id=x_lo, device_id_type=MESH,
            ),
            pltpu.make_async_remote_copy(
                src_ref=srow.at[1], dst_ref=rrow.at[1], send_sem=hsend.at[1], recv_sem=hrecv.at[1],
                device_id=x_hi, device_id_type=MESH,
            ),
        ]
        for copy in row_copies:
            copy.start()
        own = pltpu.make_async_copy(x_ref, o_ref.at[me], local.at[0])
        own.start()
        gathers = []
        for k in range(1, n):
            copy = pltpu.make_async_remote_copy(
                src_ref=x_ref, dst_ref=o_ref.at[me], send_sem=gsend.at[k - 1], recv_sem=grecv.at[k - 1],
                device_id={"ty": lax.rem(me + k, n)}, device_id_type=MESH,
            )
            copy.start()
            gathers.append(copy)
        for copy in row_copies:
            copy.wait()

        def fill_cols(h, carry):
            tmp[0:cells_x] = part_of(h)
            tmp[cells_x:cells_x + depth] = rrow[0, h]
            tmp[cells_x + depth:rows] = rrow[1, h]
            t = tmp[...].T
            scol[0, h] = t[0:depth]
            scol[1, h] = t[cells_y - depth:cells_y]
            return carry

        lax.fori_loop(0, n_parts, fill_cols, 0)
        col_copies = [
            pltpu.make_async_remote_copy(
                src_ref=scol.at[0], dst_ref=rcol.at[0], send_sem=hsend.at[2], recv_sem=hrecv.at[2],
                device_id=y_lo, device_id_type=MESH,
            ),
            pltpu.make_async_remote_copy(
                src_ref=scol.at[1], dst_ref=rcol.at[1], send_sem=hsend.at[3], recv_sem=hrecv.at[3],
                device_id=y_hi, device_id_type=MESH,
            ),
        ]
        for copy in col_copies:
            copy.start()
        for copy in col_copies:
            copy.wait()
        own.wait()
        for copy in gathers:
            copy.wait()

    return pl.pallas_call(
        kernel,
        out_shape=(
            jax.ShapeDtypeStruct((n,) + block.shape, block.dtype),
            jax.ShapeDtypeStruct((2, n_parts, depth, cells_y), jnp.float32),
            jax.ShapeDtypeStruct((2, n_parts, depth, rows), jnp.float32),
        ),
        in_specs=[VMEM_SPEC] * 4,
        out_specs=(VMEM_SPEC, VMEM_SPEC, VMEM_SPEC),
        scratch_shapes=[
            pltpu.SemaphoreType.DMA((n - 1,)),
            pltpu.SemaphoreType.DMA((n - 1,)),
            pltpu.SemaphoreType.DMA((1,)),
            pltpu.VMEM((2, n_parts, depth, cells_y), jnp.float32),
            pltpu.VMEM((2, n_parts, depth, rows), jnp.float32),
            pltpu.VMEM((rows, cells_y), jnp.float32),
            pltpu.SemaphoreType.DMA((4,)),
            pltpu.SemaphoreType.DMA((4,)),
        ],
        compiler_params=pltpu.CompilerParams(
            collective_id=collective, has_side_effects=True, vmem_limit_bytes=64 * 1024 * 1024
        ),
    )(block, e_field, h_field, coefficient)


def summed_over_pair(block, axis, collective):
    def kernel(x_ref, o_ref, got, send, recv):
        other = {axis: 1 - lax.axis_index(axis)}
        barrier = pltpu.get_barrier_semaphore()
        pl.semaphore_signal(barrier, 1, device_id=other, device_id_type=MESH)
        pl.semaphore_wait(barrier, 1)
        copy = pltpu.make_async_remote_copy(
            src_ref=x_ref, dst_ref=got, send_sem=send.at[0], recv_sem=recv.at[0],
            device_id=other, device_id_type=MESH,
        )
        copy.start()
        copy.wait()
        o_ref[...] = x_ref[...] + got[...]

    return pl.pallas_call(
        kernel,
        out_shape=jax.ShapeDtypeStruct(block.shape, block.dtype),
        in_specs=[VMEM_SPEC],
        out_specs=VMEM_SPEC,
        scratch_shapes=[
            pltpu.VMEM(block.shape, block.dtype),
            pltpu.SemaphoreType.DMA((1,)),
            pltpu.SemaphoreType.DMA((1,)),
        ],
        compiler_params=pltpu.CompilerParams(collective_id=collective, has_side_effects=True),
    )(block)


def chunk_tables(step, span, count, base, positions, length):
    c1, s1 = phase_tables(jnp.arange(count, dtype=jnp.int32) * step, positions, length)
    c2, s2 = phase_tables(jnp.arange(span, dtype=jnp.int32) - base, positions, length)
    cos_t = c1[:, None, :] * c2[None, :, :] - s1[:, None, :] * s2[None, :, :]
    sin_t = s1[:, None, :] * c2[None, :, :] + c1[:, None, :] * s2[None, :, :]
    return cos_t, sin_t


def ring_positions(cells, depth):
    own = jnp.arange(cells + depth, dtype=jnp.int32)
    return jnp.concatenate([own, jnp.arange(-depth, 0, dtype=jnp.int32)])


def lane_dense(block):
    flat = block.reshape(-1)
    pad = (-flat.shape[0]) % 1024
    return jnp.pad(flat, (0, pad)).reshape(-1, 128)


def injection_plane(orders, offsets, e_field, h_field, coefficient):
    layers, cells_x, cells_y = coefficient.shape
    points, _, rows_kx, cols_ky = orders.shape
    n_src = lax.axis_size("src")
    n_tx = lax.axis_size("tx")
    n_ty = lax.axis_size("ty")
    full_x = cells_x * n_tx
    full_y = cells_y * n_ty
    mx = rows_kx * n_tx
    my = cols_ky * n_ty
    span_x = rows_kx + 2 * SHIFT
    span_y = cols_ky + 2 * SHIFT
    lift_x = (
        lax.broadcasted_iota(jnp.int32, (points, span_x, rows_kx), 1)
        == lax.broadcasted_iota(jnp.int32, (points, span_x, rows_kx), 2) + offsets[:, 0:1, None] + SHIFT
    ).astype(jnp.float32)
    lift_y = (
        lax.broadcasted_iota(jnp.int32, (points, span_y, cols_ky), 1)
        == lax.broadcasted_iota(jnp.int32, (points, span_y, cols_ky), 2) + offsets[:, 1:2, None] + SHIFT
    ).astype(jnp.float32)
    exact = lax.Precision.HIGHEST
    placed = jnp.einsum("puk,prkj->pruj", lift_x, orders, precision=exact)
    merged = jnp.einsum("pruj,pvj->ruv", placed, lift_y, precision=exact)
    size = merged.size
    merged = summed_over_pair(lane_dense(merged), "src", 2)
    got, frow, fcol = gather_with_halo(merged, e_field, h_field, coefficient, HALO, 0)
    got = got.reshape(n_ty, -1)[:, :size].reshape(n_ty, 2, span_x, span_y)
    g_re = got[:, 0]
    g_im = got[:, 1]
    y_pos = lax.axis_index("ty") * cells_y + ring_positions(cells_y, HALO)
    by_c, by_s = chunk_tables(cols_ky, span_y, n_ty, my // 2 + SHIFT, y_pos, full_y)
    i_re = jnp.einsum("cuv,cvy->uy", g_re, by_c, precision=PREC) - jnp.einsum(
        "cuv,cvy->uy", g_im, by_s, precision=PREC
    )
    i_im = jnp.einsum("cuv,cvy->uy", g_re, by_s, precision=PREC) + jnp.einsum(
        "cuv,cvy->uy", g_im, by_c, precision=PREC
    )
    inner = jnp.stack([i_re, i_im])
    size = inner.size
    inner = gather_along(lane_dense(inner), ("tx",), 1)
    inner = inner.reshape(n_tx, -1)[:, :size].reshape((n_tx,) + (2, span_x, cells_y + 2 * HALO))
    i_re = inner[:, 0]
    i_im = inner[:, 1]
    x_pos = lax.axis_index("tx") * cells_x + ring_positions(cells_x, HALO)
    bx_c, bx_s = chunk_tables(rows_kx, span_x, n_tx, mx // 2 + SHIFT, x_pos, full_x)
    p_re = jnp.einsum("cux,cuy->xy", bx_c, i_re, precision=PREC) - jnp.einsum(
        "cux,cuy->xy", bx_s, i_im, precision=PREC
    )
    p_im = jnp.einsum("cux,cuy->xy", bx_c, i_im, precision=PREC) + jnp.einsum(
        "cux,cuy->xy", bx_s, i_re, precision=PREC
    )
    return jnp.stack([p_re, p_im]), frow, fcol


def yee_kernel(e_ref, h_ref, coef_ref, plane_ref, frow, fcol, eo_ref, ho_ref, ext, cp, tmp):
    layers, cells_x, cells_y = coef_ref.shape
    depth = frow.shape[2]
    rows = cells_x + 2 * depth
    lanes = ext.shape[2]
    slab = layers + 2
    n_field = 6 * layers
    tmp[...] = jnp.zeros_like(tmp)
    lane = lax.broadcasted_iota(jnp.int32, (rows, cells_y), 1)

    def place_cols(dst, idx, col_a, col_b):
        v = jnp.concatenate([col_a, col_b], 0)
        tmp[:, 0:2 * depth] = v.T
        w = tmp[...]
        front = jnp.where(lane < depth, w, 0.0)
        back = jnp.where(lane >= depth, w, 0.0)
        dst[idx, :, cells_y:lanes] = front + pltpu.roll(back, cells_y - 2 * depth, 1)

    def place_part(dst, idx, own, h):
        dst[idx, 0:cells_x, 0:cells_y] = own
        dst[idx, cells_x:cells_x + depth, 0:cells_y] = frow[0, h]
        dst[idx, cells_x + depth:rows, 0:cells_y] = frow[1, h]
        place_cols(dst, idx, fcol[0, h], fcol[1, h])

    def place_fields(h, carry):
        comp = h // layers
        z = h % layers
        own = jnp.where(comp < 3, e_ref[comp % 3, z], h_ref[comp % 3, z])
        place_part(ext, comp * slab + z + 1, own, h)
        return carry

    lax.fori_loop(0, n_field, place_fields, 0)
    for z in range(layers):
        place_part(cp, z, coef_ref[z], n_field + z)
    zero = jnp.zeros((rows, lanes), jnp.float32)
    for comp in range(3):
        ext[comp * slab + slab - 1] = zero
        ext[(3 + comp) * slab] = zero
    for k in range(2):
        idx = layers + k
        cp[idx, :, 0:cells_y] = plane_ref[k, :, 0:cells_y]
        tmp[:, 0:2 * depth] = plane_ref[k, :, cells_y:cells_y + 2 * depth]
        w = tmp[...]
        front = jnp.where(lane < depth, w, 0.0)
        back = jnp.where(lane >= depth, w, 0.0)
        cp[idx, :, cells_y:lanes] = front + pltpu.roll(back, cells_y - 2 * depth, 1)

    ahead_x = lambda f: pltpu.roll(f, rows - 1, 0)
    ahead_y = lambda f: pltpu.roll(f, lanes - 1, 1)
    behind_x = lambda f: pltpu.roll(f, 1, 0)
    behind_y = lambda f: pltpu.roll(f, 1, 1)
    ex_, ey_, ez_, hx_, hy_, hz_ = (c * slab for c in range(6))

    for step in range(STEPS):
        def h_update(z, carry):
            s = z + 1
            e_x = ext[ex_ + s]
            e_y = ext[ey_ + s]
            e_z = ext[ez_ + s]
            ext[hx_ + s] = ext[hx_ + s] - COURANT * ((ahead_y(e_z) - e_z) - (ext[ey_ + s + 1] - e_y))
            ext[hy_ + s] = ext[hy_ + s] - COURANT * ((ext[ex_ + s + 1] - e_x) - (ahead_x(e_z) - e_z))
            ext[hz_ + s] = ext[hz_ + s] - COURANT * ((ahead_x(e_y) - e_y) - (ahead_y(e_x) - e_x))
            return carry

        def e_update(z, carry):
            s = z + 1
            h_x = ext[hx_ + s]
            h_y = ext[hy_ + s]
            h_z = ext[hz_ + s]
            c = cp[z]
            ext[ex_ + s] = ext[ex_ + s] + c * ((h_z - behind_y(h_z)) - (h_y - ext[hy_ + s - 1]))
            ext[ey_ + s] = ext[ey_ + s] + c * ((h_x - ext[hx_ + s - 1]) - (h_z - behind_x(h_z)))
            ext[ez_ + s] = ext[ez_ + s] + c * ((h_y - behind_x(h_y)) - (h_x - behind_y(h_x)))
            return carry

        lax.fori_loop(0, layers, h_update, 0)
        lax.fori_loop(0, layers, e_update, 0)
        cosine = math.cos(OMEGA * (step + 1))
        sine = math.sin(OMEGA * (step + 1))
        p_re = cp[layers]
        p_im = cp[layers + 1]
        s = ZINJ + 1
        ext[ex_ + s] = ext[ex_ + s] + COURANT * (cosine * p_re - sine * p_im)
        ext[ey_ + s] = ext[ey_ + s] + COURANT * (sine * p_re + cosine * p_im)

    for comp in range(3):
        for z in range(layers):
            eo_ref[comp, z] = ext[comp * slab + z + 1, 0:cells_x, 0:cells_y]
            ho_ref[comp, z] = ext[(3 + comp) * slab + z + 1, 0:cells_x, 0:cells_y]


def per_device(orders, offsets, material, e_field, h_field):
    layers, cells_x, cells_y = material.shape
    coefficient = cell_coefficient(material)
    plane, frow, fcol = injection_plane(orders, offsets, e_field, h_field, coefficient)
    depth = HALO
    rows = cells_x + 2 * depth
    lanes = 2 * cells_y
    out = jax.ShapeDtypeStruct(e_field.shape, jnp.float32)
    return pl.pallas_call(
        yee_kernel,
        out_shape=(out, out),
        in_specs=[VMEM_SPEC] * 6,
        out_specs=(VMEM_SPEC, VMEM_SPEC),
        scratch_shapes=[
            pltpu.VMEM((6 * (layers + 2), rows, lanes), jnp.float32),
            pltpu.VMEM((layers + 2, rows, lanes), jnp.float32),
            pltpu.VMEM((rows, cells_y), jnp.float32),
        ],
        compiler_params=pltpu.CompilerParams(vmem_limit_bytes=64 * 1024 * 1024),
    )(e_field, h_field, coefficient, plane, frow, fcol)


def solution(mesh):
    in_specs = (
        P("src", None, "tx", "ty"),
        P("src", None),
        P(None, "tx", "ty"),
        P(None, None, "tx", "ty"),
        P(None, None, "tx", "ty"),
    )
    out_specs = (P(None, None, "tx", "ty"), P(None, None, "tx", "ty"))
    return jax.shard_map(
        per_device, mesh=mesh, in_specs=in_specs, out_specs=out_specs, check_vma=False
    )
```

```python
import math

import jax
import jax.numpy as jnp
from jax import lax
from jax.sharding import PartitionSpec as P
from jax.experimental import pallas as pl
from jax.experimental.pallas import tpu as pltpu

STEPS = 4
ZINJ = 1


COURANT = 0.5
OMEGA = 0.7
PERMITTIVITY = (1.0, 2.6, 11.9, 2.1)
PREC = lax.Precision.HIGH
SHIFT = 8
HALO = 8


def phase_tables(freqs, positions, length):
    product = jnp.mod(freqs[:, None] * positions[None, :], length)
    angle = product.astype(jnp.float32) * (2.0 * math.pi / length)
    return (jnp.cos(angle), jnp.sin(angle))


def cell_coefficient(material):
    total = jnp.zeros(material.shape, jnp.float32)
    for number in range(len(PERMITTIVITY)):
        total = total + jnp.where(material == number, COURANT / PERMITTIVITY[number], 0.0)
    return total


MESH = pl.DeviceIdType.MESH
VMEM_SPEC = pl.BlockSpec(memory_space=pltpu.MemorySpace.VMEM)


def gather_along(block, axes, collective):
    sizes = [lax.axis_size(a) for a in axes]
    n = 1
    for s in sizes:
        n *= s

    def coords(linear):
        out = {}
        for a, s in reversed(list(zip(axes, sizes))):
            out[a] = lax.rem(linear, s)
            linear = linear // s
        return out

    def kernel(x_ref, o_ref, send, recv, local):
        me = 0
        for a, s in zip(axes, sizes):
            me = me * s + lax.axis_index(a)
        barrier = pltpu.get_barrier_semaphore()
        for k in range(1, n):
            pl.semaphore_signal(barrier, 1, device_id=coords(lax.rem(me + k, n)), device_id_type=MESH)
        pl.semaphore_wait(barrier, n - 1)
        own = pltpu.make_async_copy(x_ref, o_ref.at[me], local.at[0])
        own.start()
        copies = []
        for k in range(1, n):
            copy = pltpu.make_async_remote_copy(
                src_ref=x_ref,
                dst_ref=o_ref.at[me],
                send_sem=send.at[k - 1],
                recv_sem=recv.at[k - 1],
                device_id=coords(lax.rem(me + k, n)),
                device_id_type=MESH,
            )
            copy.start()
            copies.append(copy)
        own.wait()
        for copy in copies:
            copy.wait()

    return pl.pallas_call(
        kernel,
        out_shape=jax.ShapeDtypeStruct((n,) + block.shape, block.dtype),
        in_specs=[VMEM_SPEC],
        out_specs=VMEM_SPEC,
        scratch_shapes=[
            pltpu.SemaphoreType.DMA((n - 1,)),
            pltpu.SemaphoreType.DMA((n - 1,)),
            pltpu.SemaphoreType.DMA((1,)),
        ],
        compiler_params=pltpu.CompilerParams(collective_id=collective, has_side_effects=True),
    )(block)


def gather_with_halo(block, e_field, h_field, coefficient, depth, collective):
    n = lax.axis_size("ty")
    layers, cells_x, cells_y = coefficient.shape
    rows = cells_x + 2 * depth
    n_parts = 7 * layers

    def kernel(x_ref, e_ref, h_ref, coef_ref, o_ref, rrow, rcol,
               gsend, grecv, local, srow, scol, tmp, hsend, hrecv):
        me = lax.axis_index("ty")
        n_tx = lax.axis_size("tx")
        me_x = lax.axis_index("tx")
        x_lo = {"tx": lax.rem(me_x + n_tx - 1, n_tx)}
        x_hi = {"tx": lax.rem(me_x + 1, n_tx)}
        y_lo = {"ty": lax.rem(me + n - 1, n)}
        y_hi = {"ty": lax.rem(me + 1, n)}
        barrier = pltpu.get_barrier_semaphore()
        for k in range(1, n):
            pl.semaphore_signal(barrier, 1, device_id={"ty": lax.rem(me + k, n)}, device_id_type=MESH)
        for peer in (x_lo, x_hi):
            pl.semaphore_signal(barrier, 1, device_id=peer, device_id_type=MESH)
        pl.semaphore_wait(barrier, n + 1)

        def part_of(h):
            comp = h // layers
            z = h % layers
            field = jnp.where(comp < 3, e_ref[comp % 3, z], h_ref[comp % 3, z])
            return jnp.where(comp < 6, field, coef_ref[z])

        def fill_rows(h, carry):
            part = part_of(h)
            srow[0, h] = part[0:depth]
            srow[1, h] = part[cells_x - depth:cells_x]
            return carry

        lax.fori_loop(0, n_parts, fill_rows, 0)
        row_copies = [
            pltpu.make_async_remote_copy(
                src_ref=srow.at[0], dst_ref=rrow.at[0], send_sem=hsend.at[0], recv_sem=hrecv.at[0],
                device_id=x_lo, device_id_type=MESH,
            ),
            pltpu.make_async_remote_copy(
                src_ref=srow.at[1], dst_ref=rrow.at[1], send_sem=hsend.at[1], recv_sem=hrecv.at[1],
                device_id=x_hi, device_id_type=MESH,
            ),
        ]
        for copy in row_copies:
            copy.start()
        own = pltpu.make_async_copy(x_ref, o_ref.at[me], local.at[0])
        own.start()
        gathers = []
        for k in range(1, n):
            copy = pltpu.make_async_remote_copy(
                src_ref=x_ref, dst_ref=o_ref.at[me], send_sem=gsend.at[k - 1], recv_sem=grecv.at[k - 1],
                device_id={"ty": lax.rem(me + k, n)}, device_id_type=MESH,
            )
            copy.start()
            gathers.append(copy)
        for copy in row_copies:
            copy.wait()

        def fill_cols(h, carry):
            tmp[0:cells_x] = part_of(h)
            tmp[cells_x:cells_x + depth] = rrow[0, h]
            tmp[cells_x + depth:rows] = rrow[1, h]
            t = tmp[...].T
            scol[0, h] = t[0:depth]
            scol[1, h] = t[cells_y - depth:cells_y]
            return carry

        lax.fori_loop(0, n_parts, fill_cols, 0)
        col_copies = [
            pltpu.make_async_remote_copy(
                src_ref=scol.at[0], dst_ref=rcol.at[0], send_sem=hsend.at[2], recv_sem=hrecv.at[2],
                device_id=y_lo, device_id_type=MESH,
            ),
            pltpu.make_async_remote_copy(
                src_ref=scol.at[1], dst_ref=rcol.at[1], send_sem=hsend.at[3], recv_sem=hrecv.at[3],
                device_id=y_hi, device_id_type=MESH,
            ),
        ]
        for copy in col_copies:
            copy.start()
        for copy in col_copies:
            copy.wait()
        own.wait()
        for copy in gathers:
            copy.wait()

    return pl.pallas_call(
        kernel,
        out_shape=(
            jax.ShapeDtypeStruct((n,) + block.shape, block.dtype),
            jax.ShapeDtypeStruct((2, n_parts, depth, cells_y), jnp.float32),
            jax.ShapeDtypeStruct((2, n_parts, depth, rows), jnp.float32),
        ),
        in_specs=[VMEM_SPEC] * 4,
        out_specs=(VMEM_SPEC, VMEM_SPEC, VMEM_SPEC),
        scratch_shapes=[
            pltpu.SemaphoreType.DMA((n - 1,)),
            pltpu.SemaphoreType.DMA((n - 1,)),
            pltpu.SemaphoreType.DMA((1,)),
            pltpu.VMEM((2, n_parts, depth, cells_y), jnp.float32),
            pltpu.VMEM((2, n_parts, depth, rows), jnp.float32),
            pltpu.VMEM((rows, cells_y), jnp.float32),
            pltpu.SemaphoreType.DMA((4,)),
            pltpu.SemaphoreType.DMA((4,)),
        ],
        compiler_params=pltpu.CompilerParams(
            collective_id=collective, has_side_effects=True, vmem_limit_bytes=64 * 1024 * 1024
        ),
    )(block, e_field, h_field, coefficient)


def summed_over_pair(block, axis, collective):
    def kernel(x_ref, o_ref, got, send, recv):
        other = {axis: 1 - lax.axis_index(axis)}
        barrier = pltpu.get_barrier_semaphore()
        pl.semaphore_signal(barrier, 1, device_id=other, device_id_type=MESH)
        pl.semaphore_wait(barrier, 1)
        copy = pltpu.make_async_remote_copy(
            src_ref=x_ref, dst_ref=got, send_sem=send.at[0], recv_sem=recv.at[0],
            device_id=other, device_id_type=MESH,
        )
        copy.start()
        copy.wait()
        o_ref[...] = x_ref[...] + got[...]

    return pl.pallas_call(
        kernel,
        out_shape=jax.ShapeDtypeStruct(block.shape, block.dtype),
        in_specs=[VMEM_SPEC],
        out_specs=VMEM_SPEC,
        scratch_shapes=[
            pltpu.VMEM(block.shape, block.dtype),
            pltpu.SemaphoreType.DMA((1,)),
            pltpu.SemaphoreType.DMA((1,)),
        ],
        compiler_params=pltpu.CompilerParams(collective_id=collective, has_side_effects=True),
    )(block)


def chunk_tables(step, span, count, base, positions, length):
    c1, s1 = phase_tables(jnp.arange(count, dtype=jnp.int32) * step, positions, length)
    c2, s2 = phase_tables(jnp.arange(span, dtype=jnp.int32) - base, positions, length)
    cos_t = c1[:, None, :] * c2[None, :, :] - s1[:, None, :] * s2[None, :, :]
    sin_t = s1[:, None, :] * c2[None, :, :] + c1[:, None, :] * s2[None, :, :]
    return cos_t, sin_t


def ring_positions(cells, depth):
    own = jnp.arange(cells + depth, dtype=jnp.int32)
    return jnp.concatenate([own, jnp.arange(-depth, 0, dtype=jnp.int32)])


def lane_dense(block):
    flat = block.reshape(-1)
    pad = (-flat.shape[0]) % 1024
    return jnp.pad(flat, (0, pad)).reshape(-1, 128)


def injection_plane(orders, offsets, e_field, h_field, coefficient):
    layers, cells_x, cells_y = coefficient.shape
    points, _, rows_kx, cols_ky = orders.shape
    n_src = lax.axis_size("src")
    n_tx = lax.axis_size("tx")
    n_ty = lax.axis_size("ty")
    full_x = cells_x * n_tx
    full_y = cells_y * n_ty
    mx = rows_kx * n_tx
    my = cols_ky * n_ty
    span_x = rows_kx + 2 * SHIFT
    span_y = cols_ky + 2 * SHIFT
    lift_x = (
        lax.broadcasted_iota(jnp.int32, (points, span_x, rows_kx), 1)
        == lax.broadcasted_iota(jnp.int32, (points, span_x, rows_kx), 2) + offsets[:, 0:1, None] + SHIFT
    ).astype(jnp.float32)
    lift_y = (
        lax.broadcasted_iota(jnp.int32, (points, span_y, cols_ky), 1)
        == lax.broadcasted_iota(jnp.int32, (points, span_y, cols_ky), 2) + offsets[:, 1:2, None] + SHIFT
    ).astype(jnp.float32)
    exact = lax.Precision.HIGHEST
    placed = jnp.einsum("puk,prkj->pruj", lift_x, orders, precision=exact)
    merged = jnp.einsum("pruj,pvj->ruv", placed, lift_y, precision=exact)
    size = merged.size
    merged = summed_over_pair(lane_dense(merged), "src", 2)
    got, frow, fcol = gather_with_halo(merged, e_field, h_field, coefficient, HALO, 0)
    got = got.reshape(n_ty, -1)[:, :size].reshape(n_ty, 2, span_x, span_y)
    y_pos = lax.axis_index("ty") * cells_y + ring_positions(cells_y, HALO)
    by_c, by_s = chunk_tables(cols_ky, span_y, n_ty, my // 2 + SHIFT, y_pos, full_y)
    turn_y = jnp.stack([jnp.stack([by_c, by_s], 2), jnp.stack([-by_s, by_c], 2)], 1)
    inner = jnp.einsum("cauv,cavoy->ouy", got, turn_y, precision=PREC)
    size = inner.size
    inner = gather_along(lane_dense(inner), ("tx",), 1)
    inner = inner.reshape(n_tx, -1)[:, :size].reshape((n_tx,) + (2, span_x, cells_y + 2 * HALO))
    x_pos = lax.axis_index("tx") * cells_x + ring_positions(cells_x, HALO)
    bx_c, bx_s = chunk_tables(rows_kx, span_x, n_tx, mx // 2 + SHIFT, x_pos, full_x)
    turn_x = jnp.stack([jnp.stack([bx_c, bx_s], 2), jnp.stack([-bx_s, bx_c], 2)], 1)
    plane = jnp.einsum("cauox,cauy->oxy", turn_x, inner, precision=PREC)
    return plane, frow, fcol


def yee_kernel(e_ref, h_ref, coef_ref, plane_ref, frow, fcol, eo_ref, ho_ref, ext, cp, tmp):
    layers, cells_x, cells_y = coef_ref.shape
    depth = frow.shape[2]
    rows = cells_x + 2 * depth
    lanes = ext.shape[2]
    slab = layers + 2
    n_field = 6 * layers
    tmp[...] = jnp.zeros_like(tmp)
    lane = lax.broadcasted_iota(jnp.int32, (rows, cells_y), 1)

    def place_cols(dst, idx, col_a, col_b):
        v = jnp.concatenate([col_a, col_b], 0)
        tmp[:, 0:2 * depth] = v.T
        w = tmp[...]
        front = jnp.where(lane < depth, w, 0.0)
        back = jnp.where(lane >= depth, w, 0.0)
        dst[idx, :, cells_y:lanes] = front + pltpu.roll(back, cells_y - 2 * depth, 1)

    def place_part(dst, idx, own, h):
        dst[idx, 0:cells_x, 0:cells_y] = own
        dst[idx, cells_x:cells_x + depth, 0:cells_y] = frow[0, h]
        dst[idx, cells_x + depth:rows, 0:cells_y] = frow[1, h]
        place_cols(dst, idx, fcol[0, h], fcol[1, h])

    def place_fields(h, carry):
        comp = h // layers
        z = h % layers
        own = jnp.where(comp < 3, e_ref[comp % 3, z], h_ref[comp % 3, z])
        place_part(ext, comp * slab + z + 1, own, h)
        return carry

    lax.fori_loop(0, n_field, place_fields, 0)
    for z in range(layers):
        place_part(cp, z, coef_ref[z], n_field + z)
    zero = jnp.zeros((rows, lanes), jnp.float32)
    for comp in range(3):
        ext[comp * slab + slab - 1] = zero
        ext[(3 + comp) * slab] = zero
    for k in range(2):
        idx = layers + k
        cp[idx, :, 0:cells_y] = plane_ref[k, :, 0:cells_y]
        tmp[:, 0:2 * depth] = plane_ref[k, :, cells_y:cells_y + 2 * depth]
        w = tmp[...]
        front = jnp.where(lane < depth, w, 0.0)
        back = jnp.where(lane >= depth, w, 0.0)
        cp[idx, :, cells_y:lanes] = front + pltpu.roll(back, cells_y - 2 * depth, 1)

    ahead_x = lambda f: pltpu.roll(f, rows - 1, 0)
    ahead_y = lambda f: pltpu.roll(f, lanes - 1, 1)
    behind_x = lambda f: pltpu.roll(f, 1, 0)
    behind_y = lambda f: pltpu.roll(f, 1, 1)
    ex_, ey_, ez_, hx_, hy_, hz_ = (c * slab for c in range(6))

    for step in range(STEPS):
        def h_update(z, carry):
            s = z + 1
            e_x = ext[ex_ + s]
            e_y = ext[ey_ + s]
            e_z = ext[ez_ + s]
            ext[hx_ + s] = ext[hx_ + s] - COURANT * ((ahead_y(e_z) - e_z) - (ext[ey_ + s + 1] - e_y))
            ext[hy_ + s] = ext[hy_ + s] - COURANT * ((ext[ex_ + s + 1] - e_x) - (ahead_x(e_z) - e_z))
            ext[hz_ + s] = ext[hz_ + s] - COURANT * ((ahead_x(e_y) - e_y) - (ahead_y(e_x) - e_x))
            return carry

        def e_update(z, carry):
            s = z + 1
            h_x = ext[hx_ + s]
            h_y = ext[hy_ + s]
            h_z = ext[hz_ + s]
            c = cp[z]
            ext[ex_ + s] = ext[ex_ + s] + c * ((h_z - behind_y(h_z)) - (h_y - ext[hy_ + s - 1]))
            ext[ey_ + s] = ext[ey_ + s] + c * ((h_x - ext[hx_ + s - 1]) - (h_z - behind_x(h_z)))
            ext[ez_ + s] = ext[ez_ + s] + c * ((h_y - behind_x(h_y)) - (h_x - behind_y(h_x)))
            return carry

        lax.fori_loop(0, layers, h_update, 0)
        lax.fori_loop(0, layers, e_update, 0)
        cosine = math.cos(OMEGA * (step + 1))
        sine = math.sin(OMEGA * (step + 1))
        p_re = cp[layers]
        p_im = cp[layers + 1]
        s = ZINJ + 1
        ext[ex_ + s] = ext[ex_ + s] + COURANT * (cosine * p_re - sine * p_im)
        ext[ey_ + s] = ext[ey_ + s] + COURANT * (sine * p_re + cosine * p_im)

    for comp in range(3):
        for z in range(layers):
            eo_ref[comp, z] = ext[comp * slab + z + 1, 0:cells_x, 0:cells_y]
            ho_ref[comp, z] = ext[(3 + comp) * slab + z + 1, 0:cells_x, 0:cells_y]


def per_device(orders, offsets, material, e_field, h_field):
    layers, cells_x, cells_y = material.shape
    coefficient = cell_coefficient(material)
    plane, frow, fcol = injection_plane(orders, offsets, e_field, h_field, coefficient)
    depth = HALO
    rows = cells_x + 2 * depth
    lanes = 2 * cells_y
    out = jax.ShapeDtypeStruct(e_field.shape, jnp.float32)
    return pl.pallas_call(
        yee_kernel,
        out_shape=(out, out),
        in_specs=[VMEM_SPEC] * 6,
        out_specs=(VMEM_SPEC, VMEM_SPEC),
        scratch_shapes=[
            pltpu.VMEM((6 * (layers + 2), rows, lanes), jnp.float32),
            pltpu.VMEM((layers + 2, rows, lanes), jnp.float32),
            pltpu.VMEM((rows, cells_y), jnp.float32),
        ],
        compiler_params=pltpu.CompilerParams(vmem_limit_bytes=64 * 1024 * 1024),
    )(e_field, h_field, coefficient, plane, frow, fcol)


def solution(mesh):
    in_specs = (
        P("src", None, "tx", "ty"),
        P("src", None),
        P(None, "tx", "ty"),
        P(None, None, "tx", "ty"),
        P(None, None, "tx", "ty"),
    )
    out_specs = (P(None, None, "tx", "ty"), P(None, None, "tx", "ty"))
    return jax.shard_map(
        per_device, mesh=mesh, in_specs=in_specs, out_specs=out_specs, check_vma=False
    )
```

```python
import math

import jax
import jax.numpy as jnp
from jax import lax
from jax.sharding import PartitionSpec as P
from jax.experimental import pallas as pl
from jax.experimental.pallas import tpu as pltpu

STEPS = 4
ZINJ = 1


COURANT = 0.5
OMEGA = 0.7
PERMITTIVITY = (1.0, 2.6, 11.9, 2.1)
PREC = lax.Precision.HIGH
SHIFT = 8
HALO = 8


def phase_tables(freqs, positions, length):
    product = jnp.mod(freqs[:, None] * positions[None, :], length)
    angle = product.astype(jnp.float32) * (2.0 * math.pi / length)
    return (jnp.cos(angle), jnp.sin(angle))


def cell_coefficient(material):
    total = jnp.zeros(material.shape, jnp.float32)
    for number in range(len(PERMITTIVITY)):
        total = total + jnp.where(material == number, COURANT / PERMITTIVITY[number], 0.0)
    return total


MESH = pl.DeviceIdType.MESH
VMEM_SPEC = pl.BlockSpec(memory_space=pltpu.MemorySpace.VMEM)


def gather_along(block, axes, collective):
    sizes = [lax.axis_size(a) for a in axes]
    n = 1
    for s in sizes:
        n *= s

    def coords(linear):
        out = {}
        for a, s in reversed(list(zip(axes, sizes))):
            out[a] = lax.rem(linear, s)
            linear = linear // s
        return out

    def kernel(x_ref, o_ref, send, recv, local):
        me = 0
        for a, s in zip(axes, sizes):
            me = me * s + lax.axis_index(a)
        barrier = pltpu.get_barrier_semaphore()
        for k in range(1, n):
            pl.semaphore_signal(barrier, 1, device_id=coords(lax.rem(me + k, n)), device_id_type=MESH)
        pl.semaphore_wait(barrier, n - 1)
        own = pltpu.make_async_copy(x_ref, o_ref.at[me], local.at[0])
        own.start()
        copies = []
        for k in range(1, n):
            copy = pltpu.make_async_remote_copy(
                src_ref=x_ref,
                dst_ref=o_ref.at[me],
                send_sem=send.at[k - 1],
                recv_sem=recv.at[k - 1],
                device_id=coords(lax.rem(me + k, n)),
                device_id_type=MESH,
            )
            copy.start()
            copies.append(copy)
        own.wait()
        for copy in copies:
            copy.wait()

    return pl.pallas_call(
        kernel,
        out_shape=jax.ShapeDtypeStruct((n,) + block.shape, block.dtype),
        in_specs=[VMEM_SPEC],
        out_specs=VMEM_SPEC,
        scratch_shapes=[
            pltpu.SemaphoreType.DMA((n - 1,)),
            pltpu.SemaphoreType.DMA((n - 1,)),
            pltpu.SemaphoreType.DMA((1,)),
        ],
        compiler_params=pltpu.CompilerParams(collective_id=collective, has_side_effects=True),
    )(block)


def gather_with_halo(block, e_field, h_field, coefficient, depth, collective):
    n = lax.axis_size("ty")
    layers, cells_x, cells_y = coefficient.shape
    rows = cells_x + 2 * depth
    n_parts = 7 * layers

    def kernel(x_ref, e_ref, h_ref, coef_ref, o_ref, rrow, rcol,
               gsend, grecv, local, srow, scol, tmp, hsend, hrecv):
        me = lax.axis_index("ty")
        n_tx = lax.axis_size("tx")
        me_x = lax.axis_index("tx")
        x_lo = {"tx": lax.rem(me_x + n_tx - 1, n_tx)}
        x_hi = {"tx": lax.rem(me_x + 1, n_tx)}
        y_lo = {"ty": lax.rem(me + n - 1, n)}
        y_hi = {"ty": lax.rem(me + 1, n)}
        barrier = pltpu.get_barrier_semaphore()
        for k in range(1, n):
            pl.semaphore_signal(barrier, 1, device_id={"ty": lax.rem(me + k, n)}, device_id_type=MESH)
        for peer in (x_lo, x_hi):
            pl.semaphore_signal(barrier, 1, device_id=peer, device_id_type=MESH)
        pl.semaphore_wait(barrier, n + 1)

        def part_ref(h):
            comp, z = divmod(h, layers)
            if comp < 3:
                return e_ref.at[comp, z]
            if comp < 6:
                return h_ref.at[comp - 3, z]
            return coef_ref.at[z]

        for h in range(n_parts):
            src_ref = part_ref(h)
            srow[0, h] = src_ref[0:depth]
            srow[1, h] = src_ref[cells_x - depth:cells_x]
        row_copies = [
            pltpu.make_async_remote_copy(
                src_ref=srow.at[0], dst_ref=rrow.at[0], send_sem=hsend.at[0], recv_sem=hrecv.at[0],
                device_id=x_lo, device_id_type=MESH,
            ),
            pltpu.make_async_remote_copy(
                src_ref=srow.at[1], dst_ref=rrow.at[1], send_sem=hsend.at[1], recv_sem=hrecv.at[1],
                device_id=x_hi, device_id_type=MESH,
            ),
        ]
        for copy in row_copies:
            copy.start()
        own = pltpu.make_async_copy(x_ref, o_ref.at[me], local.at[0])
        own.start()
        gathers = []
        for k in range(1, n):
            copy = pltpu.make_async_remote_copy(
                src_ref=x_ref, dst_ref=o_ref.at[me], send_sem=gsend.at[k - 1], recv_sem=grecv.at[k - 1],
                device_id={"ty": lax.rem(me + k, n)}, device_id_type=MESH,
            )
            copy.start()
            gathers.append(copy)
        for copy in row_copies:
            copy.wait()

        for h in range(n_parts):
            tmp[0:cells_x] = part_ref(h)[...]
            tmp[cells_x:cells_x + depth] = rrow[0, h]
            tmp[cells_x + depth:rows] = rrow[1, h]
            t = tmp[...].T
            scol[0, h] = t[0:depth]
            scol[1, h] = t[cells_y - depth:cells_y]
        col_copies = [
            pltpu.make_async_remote_copy(
                src_ref=scol.at[0], dst_ref=rcol.at[0], send_sem=hsend.at[2], recv_sem=hrecv.at[2],
                device_id=y_lo, device_id_type=MESH,
            ),
            pltpu.make_async_remote_copy(
                src_ref=scol.at[1], dst_ref=rcol.at[1], send_sem=hsend.at[3], recv_sem=hrecv.at[3],
                device_id=y_hi, device_id_type=MESH,
            ),
        ]
        for copy in col_copies:
            copy.start()
        for copy in col_copies:
            copy.wait()
        own.wait()
        for copy in gathers:
            copy.wait()

    return pl.pallas_call(
        kernel,
        out_shape=(
            jax.ShapeDtypeStruct((n,) + block.shape, block.dtype),
            jax.ShapeDtypeStruct((2, n_parts, depth, cells_y), jnp.float32),
            jax.ShapeDtypeStruct((2, n_parts, depth, rows), jnp.float32),
        ),
        in_specs=[VMEM_SPEC] * 4,
        out_specs=(VMEM_SPEC, VMEM_SPEC, VMEM_SPEC),
        scratch_shapes=[
            pltpu.SemaphoreType.DMA((n - 1,)),
            pltpu.SemaphoreType.DMA((n - 1,)),
            pltpu.SemaphoreType.DMA((1,)),
            pltpu.VMEM((2, n_parts, depth, cells_y), jnp.float32),
            pltpu.VMEM((2, n_parts, depth, rows), jnp.float32),
            pltpu.VMEM((rows, cells_y), jnp.float32),
            pltpu.SemaphoreType.DMA((4,)),
            pltpu.SemaphoreType.DMA((4,)),
        ],
        compiler_params=pltpu.CompilerParams(
            collective_id=collective, has_side_effects=True, vmem_limit_bytes=64 * 1024 * 1024
        ),
    )(block, e_field, h_field, coefficient)


def summed_over_pair(block, axis, collective):
    def kernel(x_ref, o_ref, got, send, recv):
        other = {axis: 1 - lax.axis_index(axis)}
        barrier = pltpu.get_barrier_semaphore()
        pl.semaphore_signal(barrier, 1, device_id=other, device_id_type=MESH)
        pl.semaphore_wait(barrier, 1)
        copy = pltpu.make_async_remote_copy(
            src_ref=x_ref, dst_ref=got, send_sem=send.at[0], recv_sem=recv.at[0],
            device_id=other, device_id_type=MESH,
        )
        copy.start()
        copy.wait()
        o_ref[...] = x_ref[...] + got[...]

    return pl.pallas_call(
        kernel,
        out_shape=jax.ShapeDtypeStruct(block.shape, block.dtype),
        in_specs=[VMEM_SPEC],
        out_specs=VMEM_SPEC,
        scratch_shapes=[
            pltpu.VMEM(block.shape, block.dtype),
            pltpu.SemaphoreType.DMA((1,)),
            pltpu.SemaphoreType.DMA((1,)),
        ],
        compiler_params=pltpu.CompilerParams(collective_id=collective, has_side_effects=True),
    )(block)


def chunk_tables(step, span, count, base, positions, length):
    c1, s1 = phase_tables(jnp.arange(count, dtype=jnp.int32) * step, positions, length)
    c2, s2 = phase_tables(jnp.arange(span, dtype=jnp.int32) - base, positions, length)
    cos_t = c1[:, None, :] * c2[None, :, :] - s1[:, None, :] * s2[None, :, :]
    sin_t = s1[:, None, :] * c2[None, :, :] + c1[:, None, :] * s2[None, :, :]
    return cos_t, sin_t


def ring_positions(cells, depth):
    own = jnp.arange(cells + depth, dtype=jnp.int32)
    return jnp.concatenate([own, jnp.arange(-depth, 0, dtype=jnp.int32)])


def lane_dense(block):
    flat = block.reshape(-1)
    pad = (-flat.shape[0]) % 1024
    return jnp.pad(flat, (0, pad)).reshape(-1, 128)


def injection_plane(orders, offsets, e_field, h_field, coefficient):
    layers, cells_x, cells_y = coefficient.shape
    points, _, rows_kx, cols_ky = orders.shape
    n_src = lax.axis_size("src")
    n_tx = lax.axis_size("tx")
    n_ty = lax.axis_size("ty")
    full_x = cells_x * n_tx
    full_y = cells_y * n_ty
    mx = rows_kx * n_tx
    my = cols_ky * n_ty
    span_x = rows_kx + 2 * SHIFT
    span_y = cols_ky + 2 * SHIFT
    lift_x = (
        lax.broadcasted_iota(jnp.int32, (points, span_x, rows_kx), 1)
        == lax.broadcasted_iota(jnp.int32, (points, span_x, rows_kx), 2) + offsets[:, 0:1, None] + SHIFT
    ).astype(jnp.float32)
    lift_y = (
        lax.broadcasted_iota(jnp.int32, (points, span_y, cols_ky), 1)
        == lax.broadcasted_iota(jnp.int32, (points, span_y, cols_ky), 2) + offsets[:, 1:2, None] + SHIFT
    ).astype(jnp.float32)
    exact = lax.Precision.HIGHEST
    placed = jnp.einsum("puk,prkj->pruj", lift_x, orders, precision=exact)
    merged = jnp.einsum("pruj,pvj->ruv", placed, lift_y, precision=exact)
    size = merged.size
    merged = summed_over_pair(lane_dense(merged), "src", 2)
    got, frow, fcol = gather_with_halo(merged, e_field, h_field, coefficient, HALO, 0)
    got = got.reshape(n_ty, -1)[:, :size].reshape(n_ty, 2, span_x, span_y)
    g_re = got[:, 0]
    g_im = got[:, 1]
    y_pos = lax.axis_index("ty") * cells_y + ring_positions(cells_y, HALO)
    by_c, by_s = chunk_tables(cols_ky, span_y, n_ty, my // 2 + SHIFT, y_pos, full_y)
    i_re = jnp.einsum("cuv,cvy->uy", g_re, by_c, precision=PREC) - jnp.einsum(
        "cuv,cvy->uy", g_im, by_s, precision=PREC
    )
    i_im = jnp.einsum("cuv,cvy->uy", g_re, by_s, precision=PREC) + jnp.einsum(
        "cuv,cvy->uy", g_im, by_c, precision=PREC
    )
    inner = jnp.stack([i_re, i_im])
    size = inner.size
    inner = gather_along(lane_dense(inner), ("tx",), 1)
    inner = inner.reshape(n_tx, -1)[:, :size].reshape((n_tx,) + (2, span_x, cells_y + 2 * HALO))
    i_re = inner[:, 0]
    i_im = inner[:, 1]
    x_pos = lax.axis_index("tx") * cells_x + ring_positions(cells_x, HALO)
    bx_c, bx_s = chunk_tables(rows_kx, span_x, n_tx, mx // 2 + SHIFT, x_pos, full_x)
    p_re = jnp.einsum("cux,cuy->xy", bx_c, i_re, precision=PREC) - jnp.einsum(
        "cux,cuy->xy", bx_s, i_im, precision=PREC
    )
    p_im = jnp.einsum("cux,cuy->xy", bx_c, i_im, precision=PREC) + jnp.einsum(
        "cux,cuy->xy", bx_s, i_re, precision=PREC
    )
    return jnp.stack([p_re, p_im]), frow, fcol


def yee_kernel(e_ref, h_ref, coef_ref, plane_ref, frow, fcol, eo_ref, ho_ref, ext, cp, tmp):
    layers, cells_x, cells_y = coef_ref.shape
    depth = frow.shape[2]
    rows = cells_x + 2 * depth
    lanes = ext.shape[2]
    slab = layers + 2
    n_field = 6 * layers
    tmp[...] = jnp.zeros_like(tmp)
    lane = lax.broadcasted_iota(jnp.int32, (rows, cells_y), 1)

    def place_cols(dst, idx, col_a, col_b):
        v = jnp.concatenate([col_a, col_b], 0)
        tmp[:, 0:2 * depth] = v.T
        w = tmp[...]
        front = jnp.where(lane < depth, w, 0.0)
        back = jnp.where(lane >= depth, w, 0.0)
        dst[idx, :, cells_y:lanes] = front + pltpu.roll(back, cells_y - 2 * depth, 1)

    def place_part(dst, idx, own, h):
        dst[idx, 0:cells_x, 0:cells_y] = own
        dst[idx, cells_x:cells_x + depth, 0:cells_y] = frow[0, h]
        dst[idx, cells_x + depth:rows, 0:cells_y] = frow[1, h]
        place_cols(dst, idx, fcol[0, h], fcol[1, h])

    def place_fields(h, carry):
        comp = h // layers
        z = h % layers
        place_part(ext, comp * slab + z + 1, e_ref[comp, z], h)
        place_part(ext, (comp + 3) * slab + z + 1, h_ref[comp, z], h + 3 * layers)
        return carry

    lax.fori_loop(0, 3 * layers, place_fields, 0)
    for z in range(layers):
        place_part(cp, z, coef_ref[z], n_field + z)
    zero = jnp.zeros((rows, lanes), jnp.float32)
    for comp in range(3):
        ext[comp * slab + slab - 1] = zero
        ext[(3 + comp) * slab] = zero
    for k in range(2):
        idx = layers + k
        cp[idx, :, 0:cells_y] = plane_ref[k, :, 0:cells_y]
        tmp[:, 0:2 * depth] = plane_ref[k, :, cells_y:cells_y + 2 * depth]
        w = tmp[...]
        front = jnp.where(lane < depth, w, 0.0)
        back = jnp.where(lane >= depth, w, 0.0)
        cp[idx, :, cells_y:lanes] = front + pltpu.roll(back, cells_y - 2 * depth, 1)

    ahead_x = lambda f: pltpu.roll(f, rows - 1, 0)
    ahead_y = lambda f: pltpu.roll(f, lanes - 1, 1)
    behind_x = lambda f: pltpu.roll(f, 1, 0)
    behind_y = lambda f: pltpu.roll(f, 1, 1)
    ex_, ey_, ez_, hx_, hy_, hz_ = (c * slab for c in range(6))

    for step in range(STEPS):
        def h_update(z, carry):
            s = z + 1
            e_x = ext[ex_ + s]
            e_y = ext[ey_ + s]
            e_z = ext[ez_ + s]
            ext[hx_ + s] = ext[hx_ + s] - COURANT * ((ahead_y(e_z) - e_z) - (ext[ey_ + s + 1] - e_y))
            ext[hy_ + s] = ext[hy_ + s] - COURANT * ((ext[ex_ + s + 1] - e_x) - (ahead_x(e_z) - e_z))
            ext[hz_ + s] = ext[hz_ + s] - COURANT * ((ahead_x(e_y) - e_y) - (ahead_y(e_x) - e_x))
            return carry

        def e_update(z, carry):
            s = z + 1
            h_x = ext[hx_ + s]
            h_y = ext[hy_ + s]
            h_z = ext[hz_ + s]
            c = cp[z]
            ext[ex_ + s] = ext[ex_ + s] + c * ((h_z - behind_y(h_z)) - (h_y - ext[hy_ + s - 1]))
            ext[ey_ + s] = ext[ey_ + s] + c * ((h_x - ext[hx_ + s - 1]) - (h_z - behind_x(h_z)))
            ext[ez_ + s] = ext[ez_ + s] + c * ((h_y - behind_x(h_y)) - (h_x - behind_y(h_x)))
            return carry

        lax.fori_loop(0, layers, h_update, 0)
        lax.fori_loop(0, layers, e_update, 0)
        cosine = math.cos(OMEGA * (step + 1))
        sine = math.sin(OMEGA * (step + 1))
        p_re = cp[layers]
        p_im = cp[layers + 1]
        s = ZINJ + 1
        ext[ex_ + s] = ext[ex_ + s] + COURANT * (cosine * p_re - sine * p_im)
        ext[ey_ + s] = ext[ey_ + s] + COURANT * (sine * p_re + cosine * p_im)

    for comp in range(3):
        for z in range(layers):
            eo_ref[comp, z] = ext[comp * slab + z + 1, 0:cells_x, 0:cells_y]
            ho_ref[comp, z] = ext[(3 + comp) * slab + z + 1, 0:cells_x, 0:cells_y]


def per_device(orders, offsets, material, e_field, h_field):
    layers, cells_x, cells_y = material.shape
    coefficient = cell_coefficient(material)
    plane, frow, fcol = injection_plane(orders, offsets, e_field, h_field, coefficient)
    depth = HALO
    rows = cells_x + 2 * depth
    lanes = 2 * cells_y
    out = jax.ShapeDtypeStruct(e_field.shape, jnp.float32)
    return pl.pallas_call(
        yee_kernel,
        out_shape=(out, out),
        in_specs=[VMEM_SPEC] * 6,
        out_specs=(VMEM_SPEC, VMEM_SPEC),
        scratch_shapes=[
            pltpu.VMEM((6 * (layers + 2), rows, lanes), jnp.float32),
            pltpu.VMEM((layers + 2, rows, lanes), jnp.float32),
            pltpu.VMEM((rows, cells_y), jnp.float32),
        ],
        compiler_params=pltpu.CompilerParams(vmem_limit_bytes=64 * 1024 * 1024),
    )(e_field, h_field, coefficient, plane, frow, fcol)


def solution(mesh):
    in_specs = (
        P("src", None, "tx", "ty"),
        P("src", None),
        P(None, "tx", "ty"),
        P(None, None, "tx", "ty"),
        P(None, None, "tx", "ty"),
    )
    out_specs = (P(None, None, "tx", "ty"), P(None, None, "tx", "ty"))
    return jax.shard_map(
        per_device, mesh=mesh, in_specs=in_specs, out_specs=out_specs, check_vma=False
    )
```

```python
import math

import jax
import jax.numpy as jnp
from jax import lax
from jax.sharding import PartitionSpec as P
from jax.experimental import pallas as pl
from jax.experimental.pallas import tpu as pltpu

STEPS = 4
ZINJ = 1


COURANT = 0.5
OMEGA = 0.7
PERMITTIVITY = (1.0, 2.6, 11.9, 2.1)
PREC = lax.Precision.HIGH
SHIFT = 8
HALO = 8


def phase_tables(freqs, positions, length):
    product = jnp.mod(freqs[:, None] * positions[None, :], length)
    angle = product.astype(jnp.float32) * (2.0 * math.pi / length)
    return (jnp.cos(angle), jnp.sin(angle))


def cell_coefficient(material):
    total = jnp.zeros(material.shape, jnp.float32)
    for number in range(len(PERMITTIVITY)):
        total = total + jnp.where(material == number, COURANT / PERMITTIVITY[number], 0.0)
    return total


MESH = pl.DeviceIdType.MESH
VMEM_SPEC = pl.BlockSpec(memory_space=pltpu.MemorySpace.VMEM)


def gather_along(block, axes, collective):
    sizes = [lax.axis_size(a) for a in axes]
    n = 1
    for s in sizes:
        n *= s

    def coords(linear):
        out = {}
        for a, s in reversed(list(zip(axes, sizes))):
            out[a] = lax.rem(linear, s)
            linear = linear // s
        return out

    def kernel(x_ref, o_ref, send, recv, local):
        me = 0
        for a, s in zip(axes, sizes):
            me = me * s + lax.axis_index(a)
        barrier = pltpu.get_barrier_semaphore()
        for k in range(1, n):
            pl.semaphore_signal(barrier, 1, device_id=coords(lax.rem(me + k, n)), device_id_type=MESH)
        pl.semaphore_wait(barrier, n - 1)
        own = pltpu.make_async_copy(x_ref, o_ref.at[me], local.at[0])
        own.start()
        copies = []
        for k in range(1, n):
            copy = pltpu.make_async_remote_copy(
                src_ref=x_ref,
                dst_ref=o_ref.at[me],
                send_sem=send.at[k - 1],
                recv_sem=recv.at[k - 1],
                device_id=coords(lax.rem(me + k, n)),
                device_id_type=MESH,
            )
            copy.start()
            copies.append(copy)
        own.wait()
        for copy in copies:
            copy.wait()

    return pl.pallas_call(
        kernel,
        out_shape=jax.ShapeDtypeStruct((n,) + block.shape, block.dtype),
        in_specs=[VMEM_SPEC],
        out_specs=VMEM_SPEC,
        scratch_shapes=[
            pltpu.SemaphoreType.DMA((n - 1,)),
            pltpu.SemaphoreType.DMA((n - 1,)),
            pltpu.SemaphoreType.DMA((1,)),
        ],
        compiler_params=pltpu.CompilerParams(collective_id=collective, has_side_effects=True),
    )(block)


def gather_with_halo(block, e_field, h_field, coefficient, depth, collective):
    n = lax.axis_size("ty")
    layers, cells_x, cells_y = coefficient.shape
    rows = cells_x + 2 * depth
    n_parts = 7 * layers

    def kernel(x_ref, e_ref, h_ref, coef_ref, o_ref, rrow, rcol,
               gsend, grecv, local, srow, scol, tmp, hsend, hrecv):
        me = lax.axis_index("ty")
        n_tx = lax.axis_size("tx")
        me_x = lax.axis_index("tx")
        x_lo = {"tx": lax.rem(me_x + n_tx - 1, n_tx)}
        x_hi = {"tx": lax.rem(me_x + 1, n_tx)}
        y_lo = {"ty": lax.rem(me + n - 1, n)}
        y_hi = {"ty": lax.rem(me + 1, n)}
        barrier = pltpu.get_barrier_semaphore()
        for k in range(1, n):
            pl.semaphore_signal(barrier, 1, device_id={"ty": lax.rem(me + k, n)}, device_id_type=MESH)
        for peer in (x_lo, x_hi):
            pl.semaphore_signal(barrier, 1, device_id=peer, device_id_type=MESH)
        pl.semaphore_wait(barrier, n + 1)

        def part_ref(h):
            comp, z = divmod(h, layers)
            if comp < 3:
                return e_ref.at[comp, z]
            if comp < 6:
                return h_ref.at[comp - 3, z]
            return coef_ref.at[z]

        for h in range(n_parts):
            src_ref = part_ref(h)
            srow[0, h] = src_ref[0:depth]
            srow[1, h] = src_ref[cells_x - depth:cells_x]
        row_copies = [
            pltpu.make_async_remote_copy(
                src_ref=srow.at[0], dst_ref=rrow.at[0], send_sem=hsend.at[0], recv_sem=hrecv.at[0],
                device_id=x_lo, device_id_type=MESH,
            ),
            pltpu.make_async_remote_copy(
                src_ref=srow.at[1], dst_ref=rrow.at[1], send_sem=hsend.at[1], recv_sem=hrecv.at[1],
                device_id=x_hi, device_id_type=MESH,
            ),
        ]
        for copy in row_copies:
            copy.start()
        own = pltpu.make_async_copy(x_ref, o_ref.at[me], local.at[0])
        own.start()
        gathers = []
        for k in range(1, n):
            copy = pltpu.make_async_remote_copy(
                src_ref=x_ref, dst_ref=o_ref.at[me], send_sem=gsend.at[k - 1], recv_sem=grecv.at[k - 1],
                device_id={"ty": lax.rem(me + k, n)}, device_id_type=MESH,
            )
            copy.start()
            gathers.append(copy)
        for h in range(n_parts):
            t = part_ref(h)[...].T
            scol[0, h, :, 0:cells_x] = t[0:depth]
            scol[1, h, :, 0:cells_x] = t[cells_y - depth:cells_y]
        for copy in row_copies:
            copy.wait()
        for h in range(n_parts):
            t = jnp.concatenate([rrow[0, h], rrow[1, h]], 0).T
            scol[0, h, :, cells_x:rows] = t[0:depth]
            scol[1, h, :, cells_x:rows] = t[cells_y - depth:cells_y]
        col_copies = [
            pltpu.make_async_remote_copy(
                src_ref=scol.at[0], dst_ref=rcol.at[0], send_sem=hsend.at[2], recv_sem=hrecv.at[2],
                device_id=y_lo, device_id_type=MESH,
            ),
            pltpu.make_async_remote_copy(
                src_ref=scol.at[1], dst_ref=rcol.at[1], send_sem=hsend.at[3], recv_sem=hrecv.at[3],
                device_id=y_hi, device_id_type=MESH,
            ),
        ]
        for copy in col_copies:
            copy.start()
        for copy in col_copies:
            copy.wait()
        own.wait()
        for copy in gathers:
            copy.wait()

    return pl.pallas_call(
        kernel,
        out_shape=(
            jax.ShapeDtypeStruct((n,) + block.shape, block.dtype),
            jax.ShapeDtypeStruct((2, n_parts, depth, cells_y), jnp.float32),
            jax.ShapeDtypeStruct((2, n_parts, depth, rows), jnp.float32),
        ),
        in_specs=[VMEM_SPEC] * 4,
        out_specs=(VMEM_SPEC, VMEM_SPEC, VMEM_SPEC),
        scratch_shapes=[
            pltpu.SemaphoreType.DMA((n - 1,)),
            pltpu.SemaphoreType.DMA((n - 1,)),
            pltpu.SemaphoreType.DMA((1,)),
            pltpu.VMEM((2, n_parts, depth, cells_y), jnp.float32),
            pltpu.VMEM((2, n_parts, depth, rows), jnp.float32),
            pltpu.VMEM((rows, cells_y), jnp.float32),
            pltpu.SemaphoreType.DMA((4,)),
            pltpu.SemaphoreType.DMA((4,)),
        ],
        compiler_params=pltpu.CompilerParams(
            collective_id=collective, has_side_effects=True, vmem_limit_bytes=64 * 1024 * 1024
        ),
    )(block, e_field, h_field, coefficient)


def summed_over_pair(block, axis, collective):
    def kernel(x_ref, o_ref, got, send, recv):
        other = {axis: 1 - lax.axis_index(axis)}
        barrier = pltpu.get_barrier_semaphore()
        pl.semaphore_signal(barrier, 1, device_id=other, device_id_type=MESH)
        pl.semaphore_wait(barrier, 1)
        copy = pltpu.make_async_remote_copy(
            src_ref=x_ref, dst_ref=got, send_sem=send.at[0], recv_sem=recv.at[0],
            device_id=other, device_id_type=MESH,
        )
        copy.start()
        copy.wait()
        o_ref[...] = x_ref[...] + got[...]

    return pl.pallas_call(
        kernel,
        out_shape=jax.ShapeDtypeStruct(block.shape, block.dtype),
        in_specs=[VMEM_SPEC],
        out_specs=VMEM_SPEC,
        scratch_shapes=[
            pltpu.VMEM(block.shape, block.dtype),
            pltpu.SemaphoreType.DMA((1,)),
            pltpu.SemaphoreType.DMA((1,)),
        ],
        compiler_params=pltpu.CompilerParams(collective_id=collective, has_side_effects=True),
    )(block)


def chunk_tables(step, span, count, base, positions, length):
    c1, s1 = phase_tables(jnp.arange(count, dtype=jnp.int32) * step, positions, length)
    c2, s2 = phase_tables(jnp.arange(span, dtype=jnp.int32) - base, positions, length)
    cos_t = c1[:, None, :] * c2[None, :, :] - s1[:, None, :] * s2[None, :, :]
    sin_t = s1[:, None, :] * c2[None, :, :] + c1[:, None, :] * s2[None, :, :]
    return cos_t, sin_t


def ring_positions(cells, depth):
    own = jnp.arange(cells + depth, dtype=jnp.int32)
    return jnp.concatenate([own, jnp.arange(-depth, 0, dtype=jnp.int32)])


def lane_dense(block):
    flat = block.reshape(-1)
    pad = (-flat.shape[0]) % 1024
    return jnp.pad(flat, (0, pad)).reshape(-1, 128)


def injection_plane(orders, offsets, e_field, h_field, coefficient):
    layers, cells_x, cells_y = coefficient.shape
    points, _, rows_kx, cols_ky = orders.shape
    n_src = lax.axis_size("src")
    n_tx = lax.axis_size("tx")
    n_ty = lax.axis_size("ty")
    full_x = cells_x * n_tx
    full_y = cells_y * n_ty
    mx = rows_kx * n_tx
    my = cols_ky * n_ty
    span_x = rows_kx + 2 * SHIFT
    span_y = cols_ky + 2 * SHIFT
    lift_x = (
        lax.broadcasted_iota(jnp.int32, (points, span_x, rows_kx), 1)
        == lax.broadcasted_iota(jnp.int32, (points, span_x, rows_kx), 2) + offsets[:, 0:1, None] + SHIFT
    ).astype(jnp.float32)
    lift_y = (
        lax.broadcasted_iota(jnp.int32, (points, span_y, cols_ky), 1)
        == lax.broadcasted_iota(jnp.int32, (points, span_y, cols_ky), 2) + offsets[:, 1:2, None] + SHIFT
    ).astype(jnp.float32)
    exact = lax.Precision.HIGHEST
    placed = jnp.einsum("puk,prkj->pruj", lift_x, orders, precision=exact)
    merged = jnp.einsum("pruj,pvj->ruv", placed, lift_y, precision=exact)
    size = merged.size
    merged = summed_over_pair(lane_dense(merged), "src", 2)
    got, frow, fcol = gather_with_halo(merged, e_field, h_field, coefficient, HALO, 0)
    got = got.reshape(n_ty, -1)[:, :size].reshape(n_ty, 2, span_x, span_y)
    g_re = got[:, 0]
    g_im = got[:, 1]
    y_pos = lax.axis_index("ty") * cells_y + ring_positions(cells_y, HALO)
    by_c, by_s = chunk_tables(cols_ky, span_y, n_ty, my // 2 + SHIFT, y_pos, full_y)
    i_re = jnp.einsum("cuv,cvy->uy", g_re, by_c, precision=PREC) - jnp.einsum(
        "cuv,cvy->uy", g_im, by_s, precision=PREC
    )
    i_im = jnp.einsum("cuv,cvy->uy", g_re, by_s, precision=PREC) + jnp.einsum(
        "cuv,cvy->uy", g_im, by_c, precision=PREC
    )
    inner = jnp.stack([i_re, i_im])
    size = inner.size
    inner = gather_along(lane_dense(inner), ("tx",), 1)
    inner = inner.reshape(n_tx, -1)[:, :size].reshape((n_tx,) + (2, span_x, cells_y + 2 * HALO))
    i_re = inner[:, 0]
    i_im = inner[:, 1]
    x_pos = lax.axis_index("tx") * cells_x + ring_positions(cells_x, HALO)
    bx_c, bx_s = chunk_tables(rows_kx, span_x, n_tx, mx // 2 + SHIFT, x_pos, full_x)
    p_re = jnp.einsum("cux,cuy->xy", bx_c, i_re, precision=PREC) - jnp.einsum(
        "cux,cuy->xy", bx_s, i_im, precision=PREC
    )
    p_im = jnp.einsum("cux,cuy->xy", bx_c, i_im, precision=PREC) + jnp.einsum(
        "cux,cuy->xy", bx_s, i_re, precision=PREC
    )
    return jnp.stack([p_re, p_im]), frow, fcol


def yee_kernel(e_ref, h_ref, coef_ref, plane_ref, frow, fcol, eo_ref, ho_ref, ext, cp, tmp):
    layers, cells_x, cells_y = coef_ref.shape
    depth = frow.shape[2]
    rows = cells_x + 2 * depth
    lanes = ext.shape[2]
    slab = layers + 2
    n_field = 6 * layers
    tmp[...] = jnp.zeros_like(tmp)
    lane = lax.broadcasted_iota(jnp.int32, (rows, cells_y), 1)

    def place_cols(dst, idx, col_a, col_b):
        v = jnp.concatenate([col_a, col_b], 0)
        tmp[:, 0:2 * depth] = v.T
        w = tmp[...]
        front = jnp.where(lane < depth, w, 0.0)
        back = jnp.where(lane >= depth, w, 0.0)
        dst[idx, :, cells_y:lanes] = front + pltpu.roll(back, cells_y - 2 * depth, 1)

    def place_part(dst, idx, own, h):
        dst[idx, 0:cells_x, 0:cells_y] = own
        dst[idx, cells_x:cells_x + depth, 0:cells_y] = frow[0, h]
        dst[idx, cells_x + depth:rows, 0:cells_y] = frow[1, h]
        place_cols(dst, idx, fcol[0, h], fcol[1, h])

    def place_fields(h, carry):
        comp = h // layers
        z = h % layers
        place_part(ext, comp * slab + z + 1, e_ref[comp, z], h)
        place_part(ext, (comp + 3) * slab + z + 1, h_ref[comp, z], h + 3 * layers)
        return carry

    lax.fori_loop(0, 3 * layers, place_fields, 0)
    for z in range(layers):
        place_part(cp, z, coef_ref[z], n_field + z)
    zero = jnp.zeros((rows, lanes), jnp.float32)
    for comp in range(3):
        ext[comp * slab + slab - 1] = zero
        ext[(3 + comp) * slab] = zero
    for k in range(2):
        idx = layers + k
        cp[idx, :, 0:cells_y] = plane_ref[k, :, 0:cells_y]
        tmp[:, 0:2 * depth] = plane_ref[k, :, cells_y:cells_y + 2 * depth]
        w = tmp[...]
        front = jnp.where(lane < depth, w, 0.0)
        back = jnp.where(lane >= depth, w, 0.0)
        cp[idx, :, cells_y:lanes] = front + pltpu.roll(back, cells_y - 2 * depth, 1)

    ahead_x = lambda f: pltpu.roll(f, rows - 1, 0)
    ahead_y = lambda f: pltpu.roll(f, lanes - 1, 1)
    behind_x = lambda f: pltpu.roll(f, 1, 0)
    behind_y = lambda f: pltpu.roll(f, 1, 1)
    ex_, ey_, ez_, hx_, hy_, hz_ = (c * slab for c in range(6))

    for step in range(STEPS):
        def h_update(z, carry):
            s = z + 1
            e_x = ext[ex_ + s]
            e_y = ext[ey_ + s]
            e_z = ext[ez_ + s]
            ext[hx_ + s] = ext[hx_ + s] - COURANT * ((ahead_y(e_z) - e_z) - (ext[ey_ + s + 1] - e_y))
            ext[hy_ + s] = ext[hy_ + s] - COURANT * ((ext[ex_ + s + 1] - e_x) - (ahead_x(e_z) - e_z))
            ext[hz_ + s] = ext[hz_ + s] - COURANT * ((ahead_x(e_y) - e_y) - (ahead_y(e_x) - e_x))
            return carry

        def e_update(z, carry):
            s = z + 1
            h_x = ext[hx_ + s]
            h_y = ext[hy_ + s]
            h_z = ext[hz_ + s]
            c = cp[z]
            ext[ex_ + s] = ext[ex_ + s] + c * ((h_z - behind_y(h_z)) - (h_y - ext[hy_ + s - 1]))
            ext[ey_ + s] = ext[ey_ + s] + c * ((h_x - ext[hx_ + s - 1]) - (h_z - behind_x(h_z)))
            ext[ez_ + s] = ext[ez_ + s] + c * ((h_y - behind_x(h_y)) - (h_x - behind_y(h_x)))
            return carry

        lax.fori_loop(0, layers, h_update, 0)
        lax.fori_loop(0, layers, e_update, 0)
        cosine = math.cos(OMEGA * (step + 1))
        sine = math.sin(OMEGA * (step + 1))
        p_re = cp[layers]
        p_im = cp[layers + 1]
        s = ZINJ + 1
        ext[ex_ + s] = ext[ex_ + s] + COURANT * (cosine * p_re - sine * p_im)
        ext[ey_ + s] = ext[ey_ + s] + COURANT * (sine * p_re + cosine * p_im)

    for comp in range(3):
        for z in range(layers):
            eo_ref[comp, z] = ext[comp * slab + z + 1, 0:cells_x, 0:cells_y]
            ho_ref[comp, z] = ext[(3 + comp) * slab + z + 1, 0:cells_x, 0:cells_y]


def per_device(orders, offsets, material, e_field, h_field):
    layers, cells_x, cells_y = material.shape
    coefficient = cell_coefficient(material)
    plane, frow, fcol = injection_plane(orders, offsets, e_field, h_field, coefficient)
    depth = HALO
    rows = cells_x + 2 * depth
    lanes = 2 * cells_y
    out = jax.ShapeDtypeStruct(e_field.shape, jnp.float32)
    return pl.pallas_call(
        yee_kernel,
        out_shape=(out, out),
        in_specs=[VMEM_SPEC] * 6,
        out_specs=(VMEM_SPEC, VMEM_SPEC),
        scratch_shapes=[
            pltpu.VMEM((6 * (layers + 2), rows, lanes), jnp.float32),
            pltpu.VMEM((layers + 2, rows, lanes), jnp.float32),
            pltpu.VMEM((rows, cells_y), jnp.float32),
        ],
        compiler_params=pltpu.CompilerParams(vmem_limit_bytes=64 * 1024 * 1024),
    )(e_field, h_field, coefficient, plane, frow, fcol)


def solution(mesh):
    in_specs = (
        P("src", None, "tx", "ty"),
        P("src", None),
        P(None, "tx", "ty"),
        P(None, None, "tx", "ty"),
        P(None, None, "tx", "ty"),
    )
    out_specs = (P(None, None, "tx", "ty"), P(None, None, "tx", "ty"))
    return jax.shard_map(
        per_device, mesh=mesh, in_specs=in_specs, out_specs=out_specs, check_vma=False
    )
```

```python
import math

import jax
import jax.numpy as jnp
from jax import lax
from jax.sharding import PartitionSpec as P
from jax.experimental import pallas as pl
from jax.experimental.pallas import tpu as pltpu

STEPS = 4
ZINJ = 1


COURANT = 0.5
OMEGA = 0.7
PERMITTIVITY = (1.0, 2.6, 11.9, 2.1)
PREC = lax.Precision.HIGH
SHIFT = 8
HALO = 8


def phase_tables(freqs, positions, length):
    product = jnp.mod(freqs[:, None] * positions[None, :], length)
    angle = product.astype(jnp.float32) * (2.0 * math.pi / length)
    return (jnp.cos(angle), jnp.sin(angle))


def cell_coefficient(material):
    total = jnp.zeros(material.shape, jnp.float32)
    for number in range(len(PERMITTIVITY)):
        total = total + jnp.where(material == number, COURANT / PERMITTIVITY[number], 0.0)
    return total


MESH = pl.DeviceIdType.MESH
VMEM_SPEC = pl.BlockSpec(memory_space=pltpu.MemorySpace.VMEM)


def gather_along(block, axes, collective):
    sizes = [lax.axis_size(a) for a in axes]
    n = 1
    for s in sizes:
        n *= s

    def coords(linear):
        out = {}
        for a, s in reversed(list(zip(axes, sizes))):
            out[a] = lax.rem(linear, s)
            linear = linear // s
        return out

    def kernel(x_ref, o_ref, send, recv, local):
        me = 0
        for a, s in zip(axes, sizes):
            me = me * s + lax.axis_index(a)
        barrier = pltpu.get_barrier_semaphore()
        for k in range(1, n):
            pl.semaphore_signal(barrier, 1, device_id=coords(lax.rem(me + k, n)), device_id_type=MESH)
        pl.semaphore_wait(barrier, n - 1)
        own = pltpu.make_async_copy(x_ref, o_ref.at[me], local.at[0])
        own.start()
        copies = []
        for k in range(1, n):
            copy = pltpu.make_async_remote_copy(
                src_ref=x_ref,
                dst_ref=o_ref.at[me],
                send_sem=send.at[k - 1],
                recv_sem=recv.at[k - 1],
                device_id=coords(lax.rem(me + k, n)),
                device_id_type=MESH,
            )
            copy.start()
            copies.append(copy)
        own.wait()
        for copy in copies:
            copy.wait()

    return pl.pallas_call(
        kernel,
        out_shape=jax.ShapeDtypeStruct((n,) + block.shape, block.dtype),
        in_specs=[VMEM_SPEC],
        out_specs=VMEM_SPEC,
        scratch_shapes=[
            pltpu.SemaphoreType.DMA((n - 1,)),
            pltpu.SemaphoreType.DMA((n - 1,)),
            pltpu.SemaphoreType.DMA((1,)),
        ],
        compiler_params=pltpu.CompilerParams(collective_id=collective, has_side_effects=True),
    )(block)


def gather_with_halo(block, e_field, h_field, coefficient, depth, collective):
    n = lax.axis_size("ty")
    layers, cells_x, cells_y = coefficient.shape
    rows = cells_x + 2 * depth
    n_parts = 7 * layers

    def kernel(x_ref, e_ref, h_ref, coef_ref, o_ref, rrow, rcol,
               gsend, grecv, local, srow, scol, tmp, hsend, hrecv):
        me = lax.axis_index("ty")
        n_tx = lax.axis_size("tx")
        me_x = lax.axis_index("tx")
        x_lo = {"tx": lax.rem(me_x + n_tx - 1, n_tx)}
        x_hi = {"tx": lax.rem(me_x + 1, n_tx)}
        y_lo = {"ty": lax.rem(me + n - 1, n)}
        y_hi = {"ty": lax.rem(me + 1, n)}
        barrier = pltpu.get_barrier_semaphore()
        for k in range(1, n):
            pl.semaphore_signal(barrier, 1, device_id={"ty": lax.rem(me + k, n)}, device_id_type=MESH)
        for peer in (x_lo, x_hi):
            pl.semaphore_signal(barrier, 1, device_id=peer, device_id_type=MESH)
        pl.semaphore_wait(barrier, n + 1)

        def part_ref(h):
            comp, z = divmod(h, layers)
            if comp < 3:
                return e_ref.at[comp, z]
            if comp < 6:
                return h_ref.at[comp - 3, z]
            return coef_ref.at[z]

        for h in range(n_parts):
            src_ref = part_ref(h)
            srow[0, h] = src_ref[0:depth]
            srow[1, h] = src_ref[cells_x - depth:cells_x]
        row_copies = [
            pltpu.make_async_remote_copy(
                src_ref=srow.at[0], dst_ref=rrow.at[0], send_sem=hsend.at[0], recv_sem=hrecv.at[0],
                device_id=x_lo, device_id_type=MESH,
            ),
            pltpu.make_async_remote_copy(
                src_ref=srow.at[1], dst_ref=rrow.at[1], send_sem=hsend.at[1], recv_sem=hrecv.at[1],
                device_id=x_hi, device_id_type=MESH,
            ),
        ]
        for copy in row_copies:
            copy.start()
        own = pltpu.make_async_copy(x_ref, o_ref.at[me], local.at[0])
        own.start()
        gathers = []
        for k in range(1, n):
            copy = pltpu.make_async_remote_copy(
                src_ref=x_ref, dst_ref=o_ref.at[me], send_sem=gsend.at[k - 1], recv_sem=grecv.at[k - 1],
                device_id={"ty": lax.rem(me + k, n)}, device_id_type=MESH,
            )
            copy.start()
            gathers.append(copy)
        for copy in row_copies:
            copy.wait()

        for h in range(n_parts):
            tmp[0:cells_x] = part_ref(h)[...]
            tmp[cells_x:cells_x + depth] = rrow[0, h]
            tmp[cells_x + depth:rows] = rrow[1, h]
            t = tmp[...].T
            scol[0, h] = t[0:depth]
            scol[1, h] = t[cells_y - depth:cells_y]
        col_copies = [
            pltpu.make_async_remote_copy(
                src_ref=scol.at[0], dst_ref=rcol.at[0], send_sem=hsend.at[2], recv_sem=hrecv.at[2],
                device_id=y_lo, device_id_type=MESH,
            ),
            pltpu.make_async_remote_copy(
                src_ref=scol.at[1], dst_ref=rcol.at[1], send_sem=hsend.at[3], recv_sem=hrecv.at[3],
                device_id=y_hi, device_id_type=MESH,
            ),
        ]
        for copy in col_copies:
            copy.start()
        for copy in col_copies:
            copy.wait()
        own.wait()
        for copy in gathers:
            copy.wait()

    return pl.pallas_call(
        kernel,
        out_shape=(
            jax.ShapeDtypeStruct((n,) + block.shape, block.dtype),
            jax.ShapeDtypeStruct((2, n_parts, depth, cells_y), jnp.float32),
            jax.ShapeDtypeStruct((2, n_parts, depth, rows), jnp.float32),
        ),
        in_specs=[VMEM_SPEC] * 4,
        out_specs=(VMEM_SPEC, VMEM_SPEC, VMEM_SPEC),
        scratch_shapes=[
            pltpu.SemaphoreType.DMA((n - 1,)),
            pltpu.SemaphoreType.DMA((n - 1,)),
            pltpu.SemaphoreType.DMA((1,)),
            pltpu.VMEM((2, n_parts, depth, cells_y), jnp.float32),
            pltpu.VMEM((2, n_parts, depth, rows), jnp.float32),
            pltpu.VMEM((rows, cells_y), jnp.float32),
            pltpu.SemaphoreType.DMA((4,)),
            pltpu.SemaphoreType.DMA((4,)),
        ],
        compiler_params=pltpu.CompilerParams(
            collective_id=collective, has_side_effects=True, vmem_limit_bytes=64 * 1024 * 1024
        ),
    )(block, e_field, h_field, coefficient)


def summed_over_pair(block, axis, collective):
    def kernel(x_ref, o_ref, got, send, recv):
        other = {axis: 1 - lax.axis_index(axis)}
        barrier = pltpu.get_barrier_semaphore()
        pl.semaphore_signal(barrier, 1, device_id=other, device_id_type=MESH)
        pl.semaphore_wait(barrier, 1)
        copy = pltpu.make_async_remote_copy(
            src_ref=x_ref, dst_ref=got, send_sem=send.at[0], recv_sem=recv.at[0],
            device_id=other, device_id_type=MESH,
        )
        copy.start()
        copy.wait()
        o_ref[...] = x_ref[...] + got[...]

    return pl.pallas_call(
        kernel,
        out_shape=jax.ShapeDtypeStruct(block.shape, block.dtype),
        in_specs=[VMEM_SPEC],
        out_specs=VMEM_SPEC,
        scratch_shapes=[
            pltpu.VMEM(block.shape, block.dtype),
            pltpu.SemaphoreType.DMA((1,)),
            pltpu.SemaphoreType.DMA((1,)),
        ],
        compiler_params=pltpu.CompilerParams(collective_id=collective, has_side_effects=True),
    )(block)


def chunk_tables(step, span, count, base, positions, length):
    c1, s1 = phase_tables(jnp.arange(count, dtype=jnp.int32) * step, positions, length)
    c2, s2 = phase_tables(jnp.arange(span, dtype=jnp.int32) - base, positions, length)
    cos_t = c1[:, None, :] * c2[None, :, :] - s1[:, None, :] * s2[None, :, :]
    sin_t = s1[:, None, :] * c2[None, :, :] + c1[:, None, :] * s2[None, :, :]
    return cos_t, sin_t


def ring_positions(cells, depth):
    own = jnp.arange(cells + depth, dtype=jnp.int32)
    return jnp.concatenate([own, jnp.arange(-depth, 0, dtype=jnp.int32)])


def lane_dense(block):
    flat = block.reshape(-1)
    pad = (-flat.shape[0]) % 1024
    return jnp.pad(flat, (0, pad)).reshape(-1, 128)


def injection_plane(orders, offsets, e_field, h_field, coefficient):
    layers, cells_x, cells_y = coefficient.shape
    points, _, rows_kx, cols_ky = orders.shape
    n_src = lax.axis_size("src")
    n_tx = lax.axis_size("tx")
    n_ty = lax.axis_size("ty")
    full_x = cells_x * n_tx
    full_y = cells_y * n_ty
    mx = rows_kx * n_tx
    my = cols_ky * n_ty
    span_x = rows_kx + 2 * SHIFT
    span_y = cols_ky + 2 * SHIFT
    lift_x = (
        lax.broadcasted_iota(jnp.int32, (points, span_x, rows_kx), 1)
        == lax.broadcasted_iota(jnp.int32, (points, span_x, rows_kx), 2) + offsets[:, 0:1, None] + SHIFT
    ).astype(jnp.float32)
    lift_y = (
        lax.broadcasted_iota(jnp.int32, (points, span_y, cols_ky), 1)
        == lax.broadcasted_iota(jnp.int32, (points, span_y, cols_ky), 2) + offsets[:, 1:2, None] + SHIFT
    ).astype(jnp.float32)
    exact = lax.Precision.HIGHEST
    placed = jnp.einsum("puk,prkj->pruj", lift_x, orders, precision=exact)
    merged = jnp.einsum("pruj,pvj->ruv", placed, lift_y, precision=exact)
    size = merged.size
    merged = summed_over_pair(lane_dense(merged), "src", 2)
    got, frow, fcol = gather_with_halo(merged, e_field, h_field, coefficient, HALO, 0)
    got = got.reshape(n_ty, -1)[:, :size].reshape(n_ty, 2, span_x, span_y)
    g_re = got[:, 0]
    g_im = got[:, 1]
    y_pos = lax.axis_index("ty") * cells_y + ring_positions(cells_y, HALO)
    by_c, by_s = chunk_tables(cols_ky, span_y, n_ty, my // 2 + SHIFT, y_pos, full_y)
    i_re = jnp.einsum("cuv,cvy->uy", g_re, by_c, precision=PREC) - jnp.einsum(
        "cuv,cvy->uy", g_im, by_s, precision=PREC
    )
    i_im = jnp.einsum("cuv,cvy->uy", g_re, by_s, precision=PREC) + jnp.einsum(
        "cuv,cvy->uy", g_im, by_c, precision=PREC
    )
    inner = jnp.stack([i_re, i_im])
    size = inner.size
    inner = gather_along(lane_dense(inner), ("tx",), 1)
    inner = inner.reshape(n_tx, -1)[:, :size].reshape((n_tx,) + (2, span_x, cells_y + 2 * HALO))
    i_re = inner[:, 0]
    i_im = inner[:, 1]
    x_pos = lax.axis_index("tx") * cells_x + ring_positions(cells_x, HALO)
    bx_c, bx_s = chunk_tables(rows_kx, span_x, n_tx, mx // 2 + SHIFT, x_pos, full_x)
    p_re = jnp.einsum("cux,cuy->xy", bx_c, i_re, precision=PREC) - jnp.einsum(
        "cux,cuy->xy", bx_s, i_im, precision=PREC
    )
    p_im = jnp.einsum("cux,cuy->xy", bx_c, i_im, precision=PREC) + jnp.einsum(
        "cux,cuy->xy", bx_s, i_re, precision=PREC
    )
    return jnp.stack([p_re, p_im]), frow, fcol


def yee_kernel(e_ref, h_ref, coef_ref, plane_ref, frow, fcol, eo_ref, ho_ref, ext, cp, tmp):
    layers, cells_x, cells_y = coef_ref.shape
    depth = frow.shape[2]
    rows = cells_x + 2 * depth
    lanes = ext.shape[2]
    slab = layers + 2
    n_field = 6 * layers
    tmp[...] = jnp.zeros_like(tmp)
    lane = lax.broadcasted_iota(jnp.int32, (rows, cells_y), 1)

    def place_cols(dst, idx, col_a, col_b):
        v = jnp.concatenate([col_a, col_b], 0)
        tmp[:, 0:2 * depth] = v.T
        w = tmp[...]
        front = jnp.where(lane < depth, w, 0.0)
        back = jnp.where(lane >= depth, w, 0.0)
        dst[idx, :, cells_y:lanes] = front + pltpu.roll(back, cells_y - 2 * depth, 1)

    def place_part(dst, idx, own, h):
        dst[idx, 0:cells_x, 0:cells_y] = own
        dst[idx, cells_x:cells_x + depth, 0:cells_y] = frow[0, h]
        dst[idx, cells_x + depth:rows, 0:cells_y] = frow[1, h]
        place_cols(dst, idx, fcol[0, h], fcol[1, h])

    def place_fields(h, carry):
        comp = h // layers
        z = h % layers
        place_part(ext, comp * slab + z + 1, e_ref[comp, z], h)
        place_part(ext, (comp + 3) * slab + z + 1, h_ref[comp, z], h + 3 * layers)
        return carry

    lax.fori_loop(0, 3 * layers, place_fields, 0)
    for z in range(layers):
        place_part(cp, z, coef_ref[z], n_field + z)
    zero = jnp.zeros((rows, lanes), jnp.float32)
    for comp in range(3):
        ext[comp * slab + slab - 1] = zero
        ext[(3 + comp) * slab] = zero
    for k in range(2):
        idx = layers + k
        cp[idx, :, 0:cells_y] = plane_ref[k, :, 0:cells_y]
        tmp[:, 0:2 * depth] = plane_ref[k, :, cells_y:cells_y + 2 * depth]
        w = tmp[...]
        front = jnp.where(lane < depth, w, 0.0)
        back = jnp.where(lane >= depth, w, 0.0)
        cp[idx, :, cells_y:lanes] = front + pltpu.roll(back, cells_y - 2 * depth, 1)

    ahead_x = lambda f: pltpu.roll(f, rows - 1, 0)
    ahead_y = lambda f: pltpu.roll(f, lanes - 1, 1)
    behind_x = lambda f: pltpu.roll(f, 1, 0)
    behind_y = lambda f: pltpu.roll(f, 1, 1)
    ex_, ey_, ez_, hx_, hy_, hz_ = (c * slab for c in range(6))

    for step in range(STEPS):
        def h_update(z, carry):
            s = z + 1
            e_x = ext[ex_ + s]
            e_y = ext[ey_ + s]
            e_z = ext[ez_ + s]
            ext[hx_ + s] = ext[hx_ + s] - COURANT * ((ahead_y(e_z) - e_z) - (ext[ey_ + s + 1] - e_y))
            ext[hy_ + s] = ext[hy_ + s] - COURANT * ((ext[ex_ + s + 1] - e_x) - (ahead_x(e_z) - e_z))
            ext[hz_ + s] = ext[hz_ + s] - COURANT * ((ahead_x(e_y) - e_y) - (ahead_y(e_x) - e_x))
            return carry

        def e_update(z, carry):
            s = z + 1
            h_x = ext[hx_ + s]
            h_y = ext[hy_ + s]
            h_z = ext[hz_ + s]
            c = cp[z]
            ext[ex_ + s] = ext[ex_ + s] + c * ((h_z - behind_y(h_z)) - (h_y - ext[hy_ + s - 1]))
            ext[ey_ + s] = ext[ey_ + s] + c * ((h_x - ext[hx_ + s - 1]) - (h_z - behind_x(h_z)))
            ext[ez_ + s] = ext[ez_ + s] + c * ((h_y - behind_x(h_y)) - (h_x - behind_y(h_x)))
            return carry

        lax.fori_loop(0, layers, h_update, 0, unroll=True)
        lax.fori_loop(0, layers, e_update, 0, unroll=True)
        cosine = math.cos(OMEGA * (step + 1))
        sine = math.sin(OMEGA * (step + 1))
        p_re = cp[layers]
        p_im = cp[layers + 1]
        s = ZINJ + 1
        ext[ex_ + s] = ext[ex_ + s] + COURANT * (cosine * p_re - sine * p_im)
        ext[ey_ + s] = ext[ey_ + s] + COURANT * (sine * p_re + cosine * p_im)

    for comp in range(3):
        for z in range(layers):
            eo_ref[comp, z] = ext[comp * slab + z + 1, 0:cells_x, 0:cells_y]
            ho_ref[comp, z] = ext[(3 + comp) * slab + z + 1, 0:cells_x, 0:cells_y]


def per_device(orders, offsets, material, e_field, h_field):
    layers, cells_x, cells_y = material.shape
    coefficient = cell_coefficient(material)
    plane, frow, fcol = injection_plane(orders, offsets, e_field, h_field, coefficient)
    depth = HALO
    rows = cells_x + 2 * depth
    lanes = 2 * cells_y
    out = jax.ShapeDtypeStruct(e_field.shape, jnp.float32)
    return pl.pallas_call(
        yee_kernel,
        out_shape=(out, out),
        in_specs=[VMEM_SPEC] * 6,
        out_specs=(VMEM_SPEC, VMEM_SPEC),
        scratch_shapes=[
            pltpu.VMEM((6 * (layers + 2), rows, lanes), jnp.float32),
            pltpu.VMEM((layers + 2, rows, lanes), jnp.float32),
            pltpu.VMEM((rows, cells_y), jnp.float32),
        ],
        compiler_params=pltpu.CompilerParams(vmem_limit_bytes=64 * 1024 * 1024),
    )(e_field, h_field, coefficient, plane, frow, fcol)


def solution(mesh):
    in_specs = (
        P("src", None, "tx", "ty"),
        P("src", None),
        P(None, "tx", "ty"),
        P(None, None, "tx", "ty"),
        P(None, None, "tx", "ty"),
    )
    out_specs = (P(None, None, "tx", "ty"), P(None, None, "tx", "ty"))
    return jax.shard_map(
        per_device, mesh=mesh, in_specs=in_specs, out_specs=out_specs, check_vma=False
    )
```

```python
import math

import jax
import jax.numpy as jnp
from jax import lax
from jax.sharding import PartitionSpec as P
from jax.experimental import pallas as pl
from jax.experimental.pallas import tpu as pltpu

STEPS = 4
ZINJ = 1


COURANT = 0.5
OMEGA = 0.7
PERMITTIVITY = (1.0, 2.6, 11.9, 2.1)
PREC = lax.Precision.HIGH
SHIFT = 8
HALO = 8


def phase_tables(freqs, positions, length):
    product = jnp.mod(freqs[:, None] * positions[None, :], length)
    angle = product.astype(jnp.float32) * (2.0 * math.pi / length)
    return (jnp.cos(angle), jnp.sin(angle))


def cell_coefficient(material):
    total = jnp.zeros(material.shape, jnp.float32)
    for number in range(len(PERMITTIVITY)):
        total = total + jnp.where(material == number, COURANT / PERMITTIVITY[number], 0.0)
    return total


MESH = pl.DeviceIdType.MESH
VMEM_SPEC = pl.BlockSpec(memory_space=pltpu.MemorySpace.VMEM)


def gather_along(block, axes, collective):
    sizes = [lax.axis_size(a) for a in axes]
    n = 1
    for s in sizes:
        n *= s

    def coords(linear):
        out = {}
        for a, s in reversed(list(zip(axes, sizes))):
            out[a] = lax.rem(linear, s)
            linear = linear // s
        return out

    def kernel(x_ref, o_ref, send, recv, local):
        me = 0
        for a, s in zip(axes, sizes):
            me = me * s + lax.axis_index(a)
        barrier = pltpu.get_barrier_semaphore()
        for k in range(1, n):
            pl.semaphore_signal(barrier, 1, device_id=coords(lax.rem(me + k, n)), device_id_type=MESH)
        pl.semaphore_wait(barrier, n - 1)
        own = pltpu.make_async_copy(x_ref, o_ref.at[me], local.at[0])
        own.start()
        copies = []
        for k in range(1, n):
            copy = pltpu.make_async_remote_copy(
                src_ref=x_ref,
                dst_ref=o_ref.at[me],
                send_sem=send.at[k - 1],
                recv_sem=recv.at[k - 1],
                device_id=coords(lax.rem(me + k, n)),
                device_id_type=MESH,
            )
            copy.start()
            copies.append(copy)
        own.wait()
        for copy in copies:
            copy.wait()

    return pl.pallas_call(
        kernel,
        out_shape=jax.ShapeDtypeStruct((n,) + block.shape, block.dtype),
        in_specs=[VMEM_SPEC],
        out_specs=VMEM_SPEC,
        scratch_shapes=[
            pltpu.SemaphoreType.DMA((n - 1,)),
            pltpu.SemaphoreType.DMA((n - 1,)),
            pltpu.SemaphoreType.DMA((1,)),
        ],
        compiler_params=pltpu.CompilerParams(collective_id=collective, has_side_effects=True),
    )(block)


def gather_with_halo(block, e_field, h_field, coefficient, depth, collective):
    n = lax.axis_size("ty")
    layers, cells_x, cells_y = coefficient.shape
    rows = cells_x + 2 * depth
    n_parts = 7 * layers

    def kernel(x_ref, e_ref, h_ref, coef_ref, o_ref, rrow, rcol,
               gsend, grecv, local, srow, scol, tmp, hsend, hrecv):
        me = lax.axis_index("ty")
        n_tx = lax.axis_size("tx")
        me_x = lax.axis_index("tx")
        x_lo = {"tx": lax.rem(me_x + n_tx - 1, n_tx)}
        x_hi = {"tx": lax.rem(me_x + 1, n_tx)}
        y_lo = {"ty": lax.rem(me + n - 1, n)}
        y_hi = {"ty": lax.rem(me + 1, n)}
        barrier = pltpu.get_barrier_semaphore()
        for k in range(1, n):
            pl.semaphore_signal(barrier, 1, device_id={"ty": lax.rem(me + k, n)}, device_id_type=MESH)
        for peer in (x_lo, x_hi):
            pl.semaphore_signal(barrier, 1, device_id=peer, device_id_type=MESH)
        pl.semaphore_wait(barrier, n + 1)

        def part_ref(h):
            comp, z = divmod(h, layers)
            if comp < 3:
                return e_ref.at[comp, z]
            if comp < 6:
                return h_ref.at[comp - 3, z]
            return coef_ref.at[z]

        for h in range(n_parts):
            src_ref = part_ref(h)
            srow[0, h] = src_ref[0:depth]
            srow[1, h] = src_ref[cells_x - depth:cells_x]
        row_copies = [
            pltpu.make_async_remote_copy(
                src_ref=srow.at[0], dst_ref=rrow.at[0], send_sem=hsend.at[0], recv_sem=hrecv.at[0],
                device_id=x_lo, device_id_type=MESH,
            ),
            pltpu.make_async_remote_copy(
                src_ref=srow.at[1], dst_ref=rrow.at[1], send_sem=hsend.at[1], recv_sem=hrecv.at[1],
                device_id=x_hi, device_id_type=MESH,
            ),
        ]
        for copy in row_copies:
            copy.start()
        own = pltpu.make_async_copy(x_ref, o_ref.at[me], local.at[0])
        own.start()
        gathers = []
        for k in range(1, n):
            copy = pltpu.make_async_remote_copy(
                src_ref=x_ref, dst_ref=o_ref.at[me], send_sem=gsend.at[k - 1], recv_sem=grecv.at[k - 1],
                device_id={"ty": lax.rem(me + k, n)}, device_id_type=MESH,
            )
            copy.start()
            gathers.append(copy)
        for copy in row_copies:
            copy.wait()

        for h in range(n_parts):
            tmp[0:cells_x] = part_ref(h)[...]
            tmp[cells_x:cells_x + depth] = rrow[0, h]
            tmp[cells_x + depth:rows] = rrow[1, h]
            t = tmp[...].T
            scol[0, h] = t[0:depth]
            scol[1, h] = t[cells_y - depth:cells_y]
        col_copies = [
            pltpu.make_async_remote_copy(
                src_ref=scol.at[0], dst_ref=rcol.at[0], send_sem=hsend.at[2], recv_sem=hrecv.at[2],
                device_id=y_lo, device_id_type=MESH,
            ),
            pltpu.make_async_remote_copy(
                src_ref=scol.at[1], dst_ref=rcol.at[1], send_sem=hsend.at[3], recv_sem=hrecv.at[3],
                device_id=y_hi, device_id_type=MESH,
            ),
        ]
        for copy in col_copies:
            copy.start()
        for copy in col_copies:
            copy.wait()
        own.wait()
        for copy in gathers:
            copy.wait()

    return pl.pallas_call(
        kernel,
        out_shape=(
            jax.ShapeDtypeStruct((n,) + block.shape, block.dtype),
            jax.ShapeDtypeStruct((2, n_parts, depth, cells_y), jnp.float32),
            jax.ShapeDtypeStruct((2, n_parts, depth, rows), jnp.float32),
        ),
        in_specs=[VMEM_SPEC] * 4,
        out_specs=(VMEM_SPEC, VMEM_SPEC, VMEM_SPEC),
        scratch_shapes=[
            pltpu.SemaphoreType.DMA((n - 1,)),
            pltpu.SemaphoreType.DMA((n - 1,)),
            pltpu.SemaphoreType.DMA((1,)),
            pltpu.VMEM((2, n_parts, depth, cells_y), jnp.float32),
            pltpu.VMEM((2, n_parts, depth, rows), jnp.float32),
            pltpu.VMEM((rows, cells_y), jnp.float32),
            pltpu.SemaphoreType.DMA((4,)),
            pltpu.SemaphoreType.DMA((4,)),
        ],
        compiler_params=pltpu.CompilerParams(
            collective_id=collective, has_side_effects=True, vmem_limit_bytes=64 * 1024 * 1024
        ),
    )(block, e_field, h_field, coefficient)


def summed_over_pair(block, axis, collective):
    def kernel(x_ref, o_ref, got, send, recv):
        other = {axis: 1 - lax.axis_index(axis)}
        barrier = pltpu.get_barrier_semaphore()
        pl.semaphore_signal(barrier, 1, device_id=other, device_id_type=MESH)
        pl.semaphore_wait(barrier, 1)
        copy = pltpu.make_async_remote_copy(
            src_ref=x_ref, dst_ref=got, send_sem=send.at[0], recv_sem=recv.at[0],
            device_id=other, device_id_type=MESH,
        )
        copy.start()
        copy.wait()
        o_ref[...] = x_ref[...] + got[...]

    return pl.pallas_call(
        kernel,
        out_shape=jax.ShapeDtypeStruct(block.shape, block.dtype),
        in_specs=[VMEM_SPEC],
        out_specs=VMEM_SPEC,
        scratch_shapes=[
            pltpu.VMEM(block.shape, block.dtype),
            pltpu.SemaphoreType.DMA((1,)),
            pltpu.SemaphoreType.DMA((1,)),
        ],
        compiler_params=pltpu.CompilerParams(collective_id=collective, has_side_effects=True),
    )(block)


def chunk_tables(step, span, count, base, positions, length):
    c1, s1 = phase_tables(jnp.arange(count, dtype=jnp.int32) * step, positions, length)
    c2, s2 = phase_tables(jnp.arange(span, dtype=jnp.int32) - base, positions, length)
    cos_t = c1[:, None, :] * c2[None, :, :] - s1[:, None, :] * s2[None, :, :]
    sin_t = s1[:, None, :] * c2[None, :, :] + c1[:, None, :] * s2[None, :, :]
    return cos_t, sin_t


def ring_positions(cells, depth):
    own = jnp.arange(cells + depth, dtype=jnp.int32)
    return jnp.concatenate([own, jnp.arange(-depth, 0, dtype=jnp.int32)])


def lane_dense(block):
    flat = block.reshape(-1)
    pad = (-flat.shape[0]) % 1024
    return jnp.pad(flat, (0, pad)).reshape(-1, 128)


def injection_plane(orders, offsets, e_field, h_field, coefficient):
    layers, cells_x, cells_y = coefficient.shape
    points, _, rows_kx, cols_ky = orders.shape
    n_src = lax.axis_size("src")
    n_tx = lax.axis_size("tx")
    n_ty = lax.axis_size("ty")
    full_x = cells_x * n_tx
    full_y = cells_y * n_ty
    mx = rows_kx * n_tx
    my = cols_ky * n_ty
    span_x = rows_kx + 2 * SHIFT
    span_y = cols_ky + 2 * SHIFT
    lift_x = (
        lax.broadcasted_iota(jnp.int32, (points, span_x, rows_kx), 1)
        == lax.broadcasted_iota(jnp.int32, (points, span_x, rows_kx), 2) + offsets[:, 0:1, None] + SHIFT
    ).astype(jnp.float32)
    lift_y = (
        lax.broadcasted_iota(jnp.int32, (points, span_y, cols_ky), 1)
        == lax.broadcasted_iota(jnp.int32, (points, span_y, cols_ky), 2) + offsets[:, 1:2, None] + SHIFT
    ).astype(jnp.float32)
    exact = lax.Precision.HIGHEST
    placed = jnp.einsum("puk,prkj->pruj", lift_x, orders, precision=exact)
    merged = jnp.einsum("pruj,pvj->ruv", placed, lift_y, precision=exact)
    size = merged.size
    merged = summed_over_pair(lane_dense(merged), "src", 2)
    got, frow, fcol = gather_with_halo(merged, e_field, h_field, coefficient, HALO, 0)
    got = got.reshape(n_ty, -1)[:, :size].reshape(n_ty, 2, span_x, span_y)
    g_re = got[:, 0]
    g_im = got[:, 1]
    y_pos = lax.axis_index("ty") * cells_y + ring_positions(cells_y, HALO)
    by_c, by_s = chunk_tables(cols_ky, span_y, n_ty, my // 2 + SHIFT, y_pos, full_y)
    i_re = jnp.einsum("cuv,cvy->uy", g_re, by_c, precision=PREC) - jnp.einsum(
        "cuv,cvy->uy", g_im, by_s, precision=PREC
    )
    i_im = jnp.einsum("cuv,cvy->uy", g_re, by_s, precision=PREC) + jnp.einsum(
        "cuv,cvy->uy", g_im, by_c, precision=PREC
    )
    inner = jnp.stack([i_re, i_im])
    size = inner.size
    inner = gather_along(lane_dense(inner), ("tx",), 1)
    inner = inner.reshape(n_tx, -1)[:, :size].reshape((n_tx,) + (2, span_x, cells_y + 2 * HALO))
    i_re = inner[:, 0]
    i_im = inner[:, 1]
    x_pos = lax.axis_index("tx") * cells_x + ring_positions(cells_x, HALO)
    bx_c, bx_s = chunk_tables(rows_kx, span_x, n_tx, mx // 2 + SHIFT, x_pos, full_x)
    p_re = jnp.einsum("cux,cuy->xy", bx_c, i_re, precision=PREC) - jnp.einsum(
        "cux,cuy->xy", bx_s, i_im, precision=PREC
    )
    p_im = jnp.einsum("cux,cuy->xy", bx_c, i_im, precision=PREC) + jnp.einsum(
        "cux,cuy->xy", bx_s, i_re, precision=PREC
    )
    return jnp.stack([p_re, p_im]), frow, fcol


def yee_kernel(e_ref, h_ref, coef_ref, plane_ref, frow, fcol, eo_ref, ho_ref, ext, cp, tmp):
    layers, cells_x, cells_y = coef_ref.shape
    depth = frow.shape[2]
    rows = cells_x + 2 * depth
    lanes = ext.shape[2]
    slab = layers + 2
    n_field = 6 * layers
    tmp[...] = jnp.zeros_like(tmp)
    lane = lax.broadcasted_iota(jnp.int32, (rows, cells_y), 1)

    def place_cols(dst, idx, col_a, col_b):
        v = jnp.concatenate([col_a, col_b], 0)
        tmp[:, 0:2 * depth] = v.T
        w = tmp[...]
        front = jnp.where(lane < depth, w, 0.0)
        back = jnp.where(lane >= depth, w, 0.0)
        dst[idx, :, cells_y:lanes] = front + pltpu.roll(back, cells_y - 2 * depth, 1)

    def place_part(dst, idx, own, h):
        dst[idx, 0:cells_x, 0:cells_y] = own
        dst[idx, cells_x:cells_x + depth, 0:cells_y] = frow[0, h]
        dst[idx, cells_x + depth:rows, 0:cells_y] = frow[1, h]
        place_cols(dst, idx, fcol[0, h], fcol[1, h])

    def place_fields(h, carry):
        comp = h // layers
        z = h % layers
        place_part(ext, comp * slab + z + 1, e_ref[comp, z], h)
        place_part(ext, (comp + 3) * slab + z + 1, h_ref[comp, z], h + 3 * layers)
        return carry

    lax.fori_loop(0, 3 * layers, place_fields, 0, unroll=True)
    for z in range(layers):
        place_part(cp, z, coef_ref[z], n_field + z)
    zero = jnp.zeros((rows, lanes), jnp.float32)
    for comp in range(3):
        ext[comp * slab + slab - 1] = zero
        ext[(3 + comp) * slab] = zero
    for k in range(2):
        idx = layers + k
        cp[idx, :, 0:cells_y] = plane_ref[k, :, 0:cells_y]
        tmp[:, 0:2 * depth] = plane_ref[k, :, cells_y:cells_y + 2 * depth]
        w = tmp[...]
        front = jnp.where(lane < depth, w, 0.0)
        back = jnp.where(lane >= depth, w, 0.0)
        cp[idx, :, cells_y:lanes] = front + pltpu.roll(back, cells_y - 2 * depth, 1)

    ahead_x = lambda f: pltpu.roll(f, rows - 1, 0)
    ahead_y = lambda f: pltpu.roll(f, lanes - 1, 1)
    behind_x = lambda f: pltpu.roll(f, 1, 0)
    behind_y = lambda f: pltpu.roll(f, 1, 1)
    ex_, ey_, ez_, hx_, hy_, hz_ = (c * slab for c in range(6))

    for step in range(STEPS):
        def h_update(z, carry):
            s = z + 1
            e_x = ext[ex_ + s]
            e_y = ext[ey_ + s]
            e_z = ext[ez_ + s]
            ext[hx_ + s] = ext[hx_ + s] - COURANT * ((ahead_y(e_z) - e_z) - (ext[ey_ + s + 1] - e_y))
            ext[hy_ + s] = ext[hy_ + s] - COURANT * ((ext[ex_ + s + 1] - e_x) - (ahead_x(e_z) - e_z))
            ext[hz_ + s] = ext[hz_ + s] - COURANT * ((ahead_x(e_y) - e_y) - (ahead_y(e_x) - e_x))
            return carry

        def e_update(z, carry):
            s = z + 1
            h_x = ext[hx_ + s]
            h_y = ext[hy_ + s]
            h_z = ext[hz_ + s]
            c = cp[z]
            ext[ex_ + s] = ext[ex_ + s] + c * ((h_z - behind_y(h_z)) - (h_y - ext[hy_ + s - 1]))
            ext[ey_ + s] = ext[ey_ + s] + c * ((h_x - ext[hx_ + s - 1]) - (h_z - behind_x(h_z)))
            ext[ez_ + s] = ext[ez_ + s] + c * ((h_y - behind_x(h_y)) - (h_x - behind_y(h_x)))
            return carry

        lax.fori_loop(0, layers, h_update, 0, unroll=True)
        lax.fori_loop(0, layers, e_update, 0, unroll=True)
        cosine = math.cos(OMEGA * (step + 1))
        sine = math.sin(OMEGA * (step + 1))
        p_re = cp[layers]
        p_im = cp[layers + 1]
        s = ZINJ + 1
        ext[ex_ + s] = ext[ex_ + s] + COURANT * (cosine * p_re - sine * p_im)
        ext[ey_ + s] = ext[ey_ + s] + COURANT * (sine * p_re + cosine * p_im)

    for comp in range(3):
        for z in range(layers):
            eo_ref[comp, z] = ext[comp * slab + z + 1, 0:cells_x, 0:cells_y]
            ho_ref[comp, z] = ext[(3 + comp) * slab + z + 1, 0:cells_x, 0:cells_y]


def per_device(orders, offsets, material, e_field, h_field):
    layers, cells_x, cells_y = material.shape
    coefficient = cell_coefficient(material)
    plane, frow, fcol = injection_plane(orders, offsets, e_field, h_field, coefficient)
    depth = HALO
    rows = cells_x + 2 * depth
    lanes = 2 * cells_y
    out = jax.ShapeDtypeStruct(e_field.shape, jnp.float32)
    return pl.pallas_call(
        yee_kernel,
        out_shape=(out, out),
        in_specs=[VMEM_SPEC] * 6,
        out_specs=(VMEM_SPEC, VMEM_SPEC),
        scratch_shapes=[
            pltpu.VMEM((6 * (layers + 2), rows, lanes), jnp.float32),
            pltpu.VMEM((layers + 2, rows, lanes), jnp.float32),
            pltpu.VMEM((rows, cells_y), jnp.float32),
        ],
        compiler_params=pltpu.CompilerParams(vmem_limit_bytes=64 * 1024 * 1024),
    )(e_field, h_field, coefficient, plane, frow, fcol)


def solution(mesh):
    in_specs = (
        P("src", None, "tx", "ty"),
        P("src", None),
        P(None, "tx", "ty"),
        P(None, None, "tx", "ty"),
        P(None, None, "tx", "ty"),
    )
    out_specs = (P(None, None, "tx", "ty"), P(None, None, "tx", "ty"))
    return jax.shard_map(
        per_device, mesh=mesh, in_specs=in_specs, out_specs=out_specs, check_vma=False
    )
```
